32 devices in a mesh: dp: 8 (over y, x, core), tensor: 4 (over z).
Axes of the slice: x: 2, y: 2, z: 4, core: 2. Of those that a mesh axis runs over, the one named last changes fastest.
Arguments:
- layer_input: bfloat16 [8, 1024, 1024], P('dp', 'tensor'), may hold values from -6 to 6
- document_lengths: int32 [8, 8], P('dp'), may hold values from 1 to 512, 1024 in all within a row
- attention_norm_gain: float32 [1024], replicated, may hold values from 0.25 to 1.75
- feedfwd_norm_gain: float32 [1024], replicated, may hold values from 0.25 to 1.75
- query_key_value_weight: bfloat16 [3, 1024, 1024], P(None, None, 'tensor'), may hold values from -0.1875 to 0.1875
- output_weight: bfloat16 [1024, 1024], P('tensor'), may hold values from -0.75 to 0.75
- up_weight: bfloat16 [1024, 4096], P(None, 'tensor'), may hold values from -0.1875 to 0.1875
- down_weight: bfloat16 [4096, 1024], P('tensor'), may hold values from -0.09375 to 0.09375
- adapter_query_key_value_first: bfloat16 [3, 1024, 128], replicated, may hold values from -0.1875 to 0.1875
- adapter_query_key_value_second: bfloat16 [3, 128, 1024], P(None, None, 'tensor'), may hold values from -0.5 to 0.5
- adapter_output_first: bfloat16 [1024, 128], P('tensor'), may hold values from -0.75 to 0.75
- adapter_output_second: bfloat16 [128, 1024], replicated, may hold values from -0.5 to 0.5
- adapter_up_first: bfloat16 [1024, 128], replicated, may hold values from -0.1875 to 0.1875
- adapter_up_second: bfloat16 [128, 4096], P(None, 'tensor'), may hold values from -0.5 to 0.5
- adapter_down_first: bfloat16 [4096, 128], P('tensor'), may hold values from -0.09375 to 0.09375
- adapter_down_second: bfloat16 [128, 1024], replicated, may hold values from -0.5 to 0.5
- cotangent: bfloat16 [8, 1024, 1024], P('dp', 'tensor'), may hold values from -6 to 6
Outputs:
- layer_output: bfloat16 [8, 1024, 1024], P('dp', 'tensor')
- grad_in: float32 [8, 1024, 1024], P('dp', 'tensor')
- grad_a_qkv: float32 [3, 1024, 128], replicated
- grad_b_qkv: float32 [3, 128, 1024], P(None, None, 'tensor')
- grad_a_out: float32 [1024, 128], P('tensor')
- grad_b_out: float32 [128, 1024], replicated
- grad_a_up: float32 [1024, 128], replicated
- grad_b_up: float32 [128, 4096], P(None, 'tensor')
- grad_a_down: float32 [4096, 128], P('tensor')
- grad_b_down: float32 [128, 1024], replicated
The draws below stay inside these ranges and needn't reach their ends.
Inputs may be any that keep to these rules, and one draw needn't show every extreme that they name: `document_lengths`: in each row the 8 lengths are positive, sum to 1024, and the largest is exactly 512; the documents lie in the row in the order given.
All inputs are finite; a program needn't handle non-finite values.
Results may differ from the reference program's by a relative error of at most 0.012.
Values may be sent and summed in bfloat16 or wider, within the bound.
No kernel may reach another device: no remote copies, remote signals or barrier semaphores. Data moves between devices by JAX's collectives and lax.ppermute only.
A program may use at most 128 MiB of HBM per device.

```python
import math
import jax
import jax.numpy as jnp
import numpy as np
from jax import lax

MODEL_DIM = 1024
HEADS = 16
HEAD_DIM = 64
ROT = 16
FEEDFWD_UNITS = 4096
ADAPTER_RANK = 128
SEQ = 1024
DOCS = 8
ROWS = 8
MOST_DOC = 512


def levels(rng, dims, shards, smallest, largest):
    def one(position, blocks):
        heights = jax.random.uniform(jax.random.fold_in(jax.random.fold_in(rng, 6), position), (blocks,), jnp.float32, smallest / len(shards), largest / len(shards))
        return jnp.repeat(jnp.exp(heights), dims[position] // blocks).reshape((-1,) + (1,) * (len(dims) - position - 1))

    factor_of = one(*shards[0])
    for cut in shards[1:]:
        factor_of = factor_of * one(*cut)
    return factor_of


def length_profile(count, total, bound, skew):
    weights = [(1 << 20) // math.isqrt(rank ** skew) + 1 for rank in range(2, count + 1)]
    spare, counts = total - bound - (count - 1), [1] * (count - 1)
    while spare > 0:
        candidates = [i for i in range(count - 1) if counts[i] < bound]
        mass, remaining = sum([weights[i] for i in candidates]), spare
        for i in candidates:
            more = min(bound - counts[i], max(1, remaining * weights[i] // mass), spare)
            counts[i] = counts[i] + more
            spare = spare - more
    return np.array([bound] + counts)


def uneven(stream_key, count, total, most, lean):
    if count == 2:
        one = jax.random.randint(stream_key, (), max(1, total - most), min(most, total - 1) + 1)
        return jnp.stack([one, total - one])
    tallies = jnp.asarray(length_profile(count, total, most, lean), jnp.int32)
    pairs = (count - 1) // 2
    donor, receiver = tallies[1:1 + 2 * pairs:2], tallies[2:2 + 2 * pairs:2]
    slack = jnp.minimum(donor - 1, most - receiver)
    moved = jax.random.randint(jax.random.fold_in(stream_key, 1), (pairs,), 0, 1 << 20) % (slack + 1)
    tallies = tallies.at[1:1 + 2 * pairs:2].set(donor - moved).at[2:2 + 2 * pairs:2].set(receiver + moved)
    return tallies[jax.random.permutation(jax.random.fold_in(stream_key, 2), count)]


def scatter_about(stream_key, extent, scale, bound, cuts=(), kind=jnp.bfloat16):
    array = scale * jax.random.normal(stream_key, extent, jnp.float32)
    if cuts:
        array = array * levels(stream_key, extent, cuts, -0.22, 0.18)
    return jnp.clip(array, -bound, bound).astype(kind)


def setup_inputs(seed: int = 0) -> dict:
    key_of = jax.random.split(jax.random.key(seed), 18)
    return {
        "layer_input": scatter_about(key_of[0], (ROWS, SEQ, MODEL_DIM), 1.0, 6.0, ((0, 8), (1, 4))),
        "document_lengths": jax.vmap(lambda own: uneven(own, DOCS, SEQ, MOST_DOC, 2))(jax.random.split(key_of[1], ROWS)).reshape((ROWS, DOCS)).astype(jnp.int32),
        "attention_norm_gain": jnp.clip(1.0 + 0.15 * jax.random.normal(key_of[2], (MODEL_DIM,), jnp.float32), 0.25, 1.75),
        "feedfwd_norm_gain": jnp.clip(1.0 + 0.15 * jax.random.normal(key_of[3], (MODEL_DIM,), jnp.float32), 0.25, 1.75),
        "query_key_value_weight": scatter_about(key_of[4], (3, MODEL_DIM, MODEL_DIM), MODEL_DIM ** -0.5, 0.1875, ((2, 4),)),
        "output_weight": scatter_about(key_of[5], (MODEL_DIM, MODEL_DIM), (MODEL_DIM // 16) ** -0.5, 0.75, ((0, 4),)),
        "up_weight": scatter_about(key_of[6], (MODEL_DIM, FEEDFWD_UNITS), MODEL_DIM ** -0.5, 0.1875, ((1, 4),)),
        "down_weight": scatter_about(key_of[7], (FEEDFWD_UNITS, MODEL_DIM), FEEDFWD_UNITS ** -0.5, 0.09375, ((0, 4),)),
        "adapter_query_key_value_first": scatter_about(key_of[8], (3, MODEL_DIM, ADAPTER_RANK), MODEL_DIM ** -0.5, 0.1875),
        "adapter_query_key_value_second": scatter_about(key_of[9], (3, ADAPTER_RANK, MODEL_DIM), ADAPTER_RANK ** -0.5, 0.5, ((2, 4),)),
        "adapter_output_first": scatter_about(key_of[10], (MODEL_DIM, ADAPTER_RANK), (MODEL_DIM // 16) ** -0.5, 0.75, ((0, 4),)),
        "adapter_output_second": scatter_about(key_of[11], (ADAPTER_RANK, MODEL_DIM), ADAPTER_RANK ** -0.5, 0.5),
        "adapter_up_first": scatter_about(key_of[12], (MODEL_DIM, ADAPTER_RANK), MODEL_DIM ** -0.5, 0.1875),
        "adapter_up_second": scatter_about(key_of[13], (ADAPTER_RANK, FEEDFWD_UNITS), ADAPTER_RANK ** -0.5, 0.5, ((1, 4),)),
        "adapter_down_first": scatter_about(key_of[14], (FEEDFWD_UNITS, ADAPTER_RANK), FEEDFWD_UNITS ** -0.5, 0.09375, ((0, 4),)),
        "adapter_down_second": scatter_about(key_of[15], (ADAPTER_RANK, MODEL_DIM), ADAPTER_RANK ** -0.5, 0.5),
        "cotangent": scatter_about(key_of[16], (ROWS, SEQ, MODEL_DIM), 1.0, 6.0, ((0, 8), (1, 4))),
    }


@jax.custom_vjp
def low(v):
    return lax.optimization_barrier(v.astype(jnp.bfloat16)).astype(jnp.float32)

@jax.custom_vjp
def reverse_rank_rows(v):
    return v

def low_keep(v):
    return (low(v), None)

def low_pass(kept, grad):
    return (grad,)

def back_keep(v):
    return (v, None)

def back_low(kept, grad):
    return (low(grad),)
low.defvjp(low_keep, low_pass)
reverse_rank_rows.defvjp(back_keep, back_low)
EPSILON = 1e-05
ADAPTER_SCALE = 0.25
MASKED = -1e+30

def both_ways(value):
    return low(reverse_rank_rows(value))

def matrix_product(left_side, right_side):
    return jnp.dot(left_side, right_side, precision=lax.Precision.HIGHEST)

def normalize(inputs):
    center = inputs - lax.optimization_barrier(jnp.mean(inputs, axis=-1, keepdims=True))
    broadcast_rows = lax.optimization_barrier(jnp.mean(center * center, axis=-1, keepdims=True))
    return center * lax.rsqrt(broadcast_rows + EPSILON)

def token_places(document_lengths, seq_len):
    doc_ends = jnp.cumsum(document_lengths, axis=-1).astype(jnp.int32)
    doc_starts = (doc_ends - document_lengths).astype(jnp.int32)
    token_pos = jnp.arange(seq_len, dtype=jnp.int32)
    doc_ids = lax.optimization_barrier(jnp.sum((token_pos[None, :, None] >= doc_ends[:, None, :]).astype(jnp.int32), axis=-1)).astype(jnp.int32)
    slot_ids = jnp.arange(document_lengths.shape[-1], dtype=jnp.int32)
    chosen = doc_ids[:, :, None] == slot_ids[None, None, :]
    doc_begin = lax.optimization_barrier(jnp.sum(jnp.where(chosen, doc_starts[:, None, :], 0), axis=-1)).astype(jnp.int32)
    return (doc_ids, (token_pos[None, :] - doc_begin).astype(jnp.int32))

def rotate(values, document_offsets, turn_sign):
    half_rot = ROT // 2
    steps_f = jnp.arange(half_rot, dtype=jnp.float32)
    inverse = jnp.exp(steps_f * (-2.0 * math.log(10000.0) / ROT))
    angles = document_offsets.astype(jnp.float32)[..., None] * inverse
    cosine = jnp.cos(angles)[..., None, :]
    sine_part = turn_sign * jnp.sin(angles)[..., None, :]
    lead_half = values[..., :half_rot]
    tail_half = values[..., half_rot:ROT]
    return jnp.concatenate([lead_half * cosine - tail_half * sine_part, tail_half * cosine + lead_half * sine_part, values[..., ROT:]], axis=-1)

def attend_row(pieces):
    queries, keys, values, doc_ids = pieces
    seq_len = queries.shape[0]
    token_pos = jnp.arange(seq_len, dtype=jnp.int32)
    raw_scores = jnp.einsum('qhd,khd->hqk', queries, keys, precision=lax.Precision.HIGHEST)
    scores = reverse_rank_rows(raw_scores) * (1.0 / math.sqrt(HEAD_DIM))
    allowed = (doc_ids[:, None] == doc_ids[None, :]) & (token_pos[None, :] <= token_pos[:, None])
    scores = jnp.where(allowed[None], scores, MASKED)
    row_peak = lax.optimization_barrier(jnp.max(scores, axis=-1, keepdims=True))
    exp_terms = jnp.exp(scores - row_peak)
    prob_terms = exp_terms / lax.optimization_barrier(jnp.sum(exp_terms, axis=-1, keepdims=True))
    return jnp.einsum('hqk,khd->qhd', low(prob_terms), values, precision=lax.Precision.HIGHEST)

def forward(hidden, adapter_factors, frozen, doc_ids, document_offsets):
    a_qkv, query_key_value_bias, a_out, output_bias, a_up, up_bias, a_down, down_bias = adapter_factors
    attention_gain, feedfwd_gain, query_key_value_weight, output_weight, up_weight, down_weight = frozen
    row_count = hidden.shape[0]
    hat_values = normalize(hidden)
    attention_input = low(hat_values * attention_gain)
    feedfwd_input = low(hat_values * feedfwd_gain)
    projected = []
    for group_entry in range(3):
        inner_rank_rows = both_ways(matrix_product(attention_input, a_qkv[group_entry]))
        before_projection = reverse_rank_rows(matrix_product(attention_input, query_key_value_weight[group_entry]) + ADAPTER_SCALE * matrix_product(inner_rank_rows, query_key_value_bias[group_entry]))
        before_projection = before_projection.reshape(row_count, SEQ, HEADS, HEAD_DIM)
        if group_entry < 2:
            projected.append(low(rotate(before_projection, document_offsets, 1.0)))
        else:
            projected.append(low(before_projection))
    mixed_out = lax.map(jax.checkpoint(attend_row), (projected[0], projected[1], projected[2], doc_ids))
    attention_output = both_ways(mixed_out.reshape(row_count, SEQ, HEADS * HEAD_DIM))
    output_rank_rows = both_ways(matrix_product(attention_output, a_out))
    attention_branch = matrix_product(attention_output, output_weight) + ADAPTER_SCALE * matrix_product(output_rank_rows, output_bias)
    up_rank_rows = both_ways(matrix_product(feedfwd_input, a_up))
    before_up = reverse_rank_rows(matrix_product(feedfwd_input, up_weight) + ADAPTER_SCALE * matrix_product(up_rank_rows, up_bias))
    gelu_output = low(jax.nn.gelu(before_up, approximate=False))
    down_rank_rows = both_ways(matrix_product(gelu_output, a_down))
    feedfwd_branch = matrix_product(gelu_output, down_weight) + ADAPTER_SCALE * matrix_product(down_rank_rows, down_bias)
    return hidden + attention_branch + feedfwd_branch

def reference(layer_input, document_lengths, attention_norm_gain, feedfwd_norm_gain, query_key_value_weight, output_weight, up_weight, down_weight, adapter_query_key_value_first, adapter_query_key_value_second, adapter_output_first, adapter_output_second, adapter_up_first, adapter_up_second, adapter_down_first, adapter_down_second, cotangent):
    frozen = tuple((group_entry.astype(jnp.float32) for group_entry in (attention_norm_gain, feedfwd_norm_gain, query_key_value_weight, output_weight, up_weight, down_weight)))
    adapter_factors = tuple((group_entry.astype(jnp.float32) for group_entry in (adapter_query_key_value_first, adapter_query_key_value_second, adapter_output_first, adapter_output_second, adapter_up_first, adapter_up_second, adapter_down_first, adapter_down_second)))
    group_rows = math.gcd(ROWS, 4)
    step_count = ROWS // group_rows
    inputs_grouped = layer_input.astype(jnp.float32).reshape(step_count, group_rows, SEQ, MODEL_DIM)
    upstream_grouped = cotangent.astype(jnp.float32).reshape(step_count, group_rows, SEQ, MODEL_DIM)
    lengths_grouped = document_lengths.reshape(step_count, group_rows, DOCS)

    def one_group(totals, pieces):
        inputs, upstream, lengths = pieces
        doc_ids, document_offsets = token_places(lengths, SEQ)

        def apply_layer(hidden, factors_now):
            return forward(hidden, factors_now, frozen, doc_ids, document_offsets)
        result, pullback = jax.vjp(apply_layer, inputs, adapter_factors)
        grad_hidden, grad_factors = pullback(upstream)
        totals = tuple((summed + gradient for summed, gradient in zip(totals, grad_factors)))
        return (totals, (result.astype(jnp.bfloat16), grad_hidden))
    zero_sums = tuple((jnp.zeros(group_entry.shape, jnp.float32) for group_entry in adapter_factors))
    totals, outputs = lax.scan(one_group, zero_sums, (inputs_grouped, upstream_grouped, lengths_grouped))
    layer_output = outputs[0].reshape(ROWS, SEQ, MODEL_DIM)
    grad_in = outputs[1].reshape(ROWS, SEQ, MODEL_DIM)
    return (layer_output, grad_in, totals[0], totals[1], totals[2], totals[3], totals[4], totals[5], totals[6], totals[7])
```

```python
import math

import jax
import jax.numpy as jnp
from jax import lax
from jax.experimental import pallas as pl
from jax.experimental.pallas import tpu as pltpu
from jax.sharding import PartitionSpec as P

HEAD_DIM = 64
ROT = 16
HALF = ROT // 2
BLOCK = 256
MOST_DOC = 512

EPSILON = 1e-05
ADAPTER_SCALE = 0.25
MASKED = -1e30
BF = jnp.bfloat16
F32 = jnp.float32


def mm(left, right, left_dim, right_dim):
    return lax.dot_general(
        left, right, (((left_dim,), (right_dim,)), ((), ())), preferred_element_type=F32
    )


def token_starts(lengths, seq_len):
    count = lengths.shape[0]
    slot = jnp.arange(count, dtype=jnp.int32)
    ends = jnp.sum(jnp.where(slot[:, None] <= slot[None, :], lengths[:, None], 0), axis=0)
    pos = jnp.arange(seq_len, dtype=jnp.int32)
    return jnp.sum(jnp.where(pos[None, :] >= ends[:, None], lengths[:, None], 0), axis=0)


def turn(value, cosine, sine):
    lead, tail = value[:HALF], value[HALF:ROT]
    return jnp.concatenate(
        [lead * cosine - tail * sine, tail * cosine + lead * sine, value[ROT:]], axis=0
    )


def allowed_pairs(start, query_block, key_block):
    key_pos = key_block * BLOCK + lax.broadcasted_iota(jnp.int32, (BLOCK, BLOCK), 0)
    keep = key_pos >= start
    if key_block == query_block:
        query_pos = query_block * BLOCK + lax.broadcasted_iota(jnp.int32, (BLOCK, BLOCK), 1)
        keep = keep & (key_pos <= query_pos)
    return keep


def key_blocks(query_block):
    return range(max(0, query_block - MOST_DOC // BLOCK), query_block + 1)


def attend_forward(start_ref, cos_ref, sin_ref, pre_ref, qkv_ref, out_ref, log_ref):
    seq_len = start_ref.shape[1]
    cosine, sine = cos_ref[...], sin_ref[...]
    queries = (turn(pre_ref[0, 0], cosine, sine) * (HEAD_DIM**-0.5)).astype(BF)
    keys = turn(pre_ref[1, 0], cosine, sine).astype(BF)
    values = pre_ref[2, 0].astype(BF)
    qkv_ref[0, 0] = queries
    qkv_ref[1, 0] = keys
    qkv_ref[2, 0] = values
    keys_t = keys.T
    for i in range(seq_len // BLOCK):
        at = slice(i * BLOCK, (i + 1) * BLOCK)
        start = start_ref[:, at]
        scores = []
        for j in key_blocks(i):
            raw = mm(keys_t[j * BLOCK : (j + 1) * BLOCK], queries[:, at], 1, 0)
            scores.append(jnp.where(allowed_pairs(start, i, j), raw, MASKED))
        peak = jnp.max(scores[0], axis=0, keepdims=True)
        for block in scores[1:]:
            peak = jnp.maximum(peak, jnp.max(block, axis=0, keepdims=True))
        total, mixed = 0.0, 0.0
        for j, block in zip(key_blocks(i), scores):
            terms = jnp.exp(block - peak)
            total = total + jnp.sum(terms, axis=0, keepdims=True)
            mixed = mixed + mm(values[:, j * BLOCK : (j + 1) * BLOCK], terms.astype(BF), 1, 0)
        out_ref[0, :, at] = (mixed / total).astype(BF)
        log_ref[0, :, at] = peak + jnp.log(total)


def attend_backward(start_ref, cos_ref, sin_ref, qkv_ref, out_ref, log_ref, grad_ref, res_ref):
    seq_len = start_ref.shape[1]
    cosine, sine = cos_ref[...], -sin_ref[...]
    queries, keys, values = qkv_ref[0, 0], qkv_ref[1, 0], qkv_ref[2, 0]
    grad = grad_ref[0]
    inner = jnp.sum(grad.astype(F32) * out_ref[0].astype(F32), axis=0, keepdims=True)
    keys_t, values_t = keys.T, values.T
    blocks = seq_len // BLOCK
    grad_keys, grad_values = [0.0] * blocks, [0.0] * blocks
    for i in range(blocks):
        at = slice(i * BLOCK, (i + 1) * BLOCK)
        start, log_total, inner_here = start_ref[:, at], log_ref[0, :, at], inner[:, at]
        query, grad_here = queries[:, at], grad[:, at]
        grad_query = 0.0
        for j in key_blocks(i):
            there = slice(j * BLOCK, (j + 1) * BLOCK)
            raw = mm(keys_t[there], query, 1, 0)
            terms = jnp.exp(jnp.where(allowed_pairs(start, i, j), raw, MASKED) - log_total)
            grad_terms = mm(values_t[there], grad_here, 1, 0)
            grad_scores = (terms * (grad_terms - inner_here)).astype(BF)
            grad_values[j] = grad_values[j] + mm(grad_here, terms.astype(BF), 1, 1)
            grad_keys[j] = grad_keys[j] + mm(query, grad_scores, 1, 1)
            grad_query = grad_query + mm(keys[:, there], grad_scores, 1, 0)
        grad_query = turn(grad_query * (HEAD_DIM**-0.5), cosine[:, at], sine[:, at])
        res_ref[0, 0, :, at] = grad_query.astype(BF)
    for j in range(blocks):
        there = slice(j * BLOCK, (j + 1) * BLOCK)
        res_ref[1, 0, :, there] = turn(grad_keys[j], cosine[:, there], sine[:, there]).astype(BF)
        res_ref[2, 0, :, there] = grad_values[j].astype(BF)


def whole(shape):
    return pl.BlockSpec(shape, lambda h: (0,) * len(shape))


def three(seq_len):
    return pl.BlockSpec((3, 1, HEAD_DIM, seq_len), lambda h: (0, h, 0, 0))


def single(rows, seq_len):
    return pl.BlockSpec((1, rows, seq_len), lambda h: (h, 0, 0))


def forward_attention(start, cosine, sine, pre):
    _, heads, _, seq_len = pre.shape
    pairs = heads * seq_len * seq_len // 2
    return pl.pallas_call(
        attend_forward,
        grid=(heads,),
        in_specs=[
            whole((1, seq_len)),
            whole((HALF, seq_len)),
            whole((HALF, seq_len)),
            three(seq_len),
        ],
        out_specs=[three(seq_len), single(HEAD_DIM, seq_len), single(1, seq_len)],
        out_shape=[
            jax.ShapeDtypeStruct(pre.shape, BF),
            jax.ShapeDtypeStruct((heads, HEAD_DIM, seq_len), BF),
            jax.ShapeDtypeStruct((heads, 1, seq_len), F32),
        ],
        cost_estimate=pl.CostEstimate(
            flops=pairs * 4 * HEAD_DIM * 4, bytes_accessed=pre.size * 7, transcendentals=pairs
        ),
    )(start, cosine, sine, pre)


def backward_attention(start, cosine, sine, qkv, out, log_total, grad):
    _, heads, _, seq_len = qkv.shape
    pairs = heads * seq_len * seq_len // 2
    return pl.pallas_call(
        attend_backward,
        grid=(heads,),
        in_specs=[
            whole((1, seq_len)),
            whole((HALF, seq_len)),
            whole((HALF, seq_len)),
            three(seq_len),
            single(HEAD_DIM, seq_len),
            single(1, seq_len),
            single(HEAD_DIM, seq_len),
        ],
        out_specs=three(seq_len),
        out_shape=jax.ShapeDtypeStruct(qkv.shape, BF),
        cost_estimate=pl.CostEstimate(
            flops=pairs * 10 * HEAD_DIM * 4, bytes_accessed=qkv.size * 6, transcendentals=pairs
        ),
    )(start, cosine, sine, qkv, out, log_total, grad)


def ring_gather(shard, place):
    n = lax.axis_size("tensor")
    me = lax.axis_index("tensor")
    up = [(i, (i + 1) % n) for i in range(n)]
    down = [(i, (i - 1) % n) for i in range(n)]
    half = shard.shape[0] // 2
    first, second = shard[:half], shard[half:]
    place(me, 0, first)
    place(me, 1, second)
    for step in range(1, n):
        first = lax.ppermute(first, "tensor", up)
        second = lax.ppermute(second, "tensor", down)
        place((me - step) % n, 0, first)
        place((me + step) % n, 1, second)


def gather_rows(shard):
    n = lax.axis_size("tensor")
    half = shard.shape[0] // 2
    total = [jnp.zeros((n * shard.shape[0],) + shard.shape[1:], shard.dtype)]

    def place(owner, which, rows):
        total[0] = lax.dynamic_update_slice_in_dim(
            total[0], rows, owner * 2 * half + which * half, axis=0
        )

    ring_gather(shard, place)
    return total[0]


def ring_scatter(piece):
    n = lax.axis_size("tensor")
    me = lax.axis_index("tensor")
    up = [(i, (i + 1) % n) for i in range(n)]
    running = piece((me - 1) % n).astype(BF)
    for step in range(2, n + 1):
        arrived = lax.ppermute(running, "tensor", up)
        total = arrived.astype(F32) + piece((me - step) % n)
        running = total.astype(BF)
    return total


def group_sum(shared, split):
    members = lax.axis_size("dp")
    n = lax.axis_size("tensor")
    me = lax.axis_index("dp")
    width = shared.shape[-1]
    n_shared = shared.shape[0] // members
    current = jnp.concatenate(
        [shared.reshape(members, -1, width), split.reshape(members, -1, width)], axis=1
    )
    bit, steps = members // 2, []
    place = 0
    while (1 << place) < members:
        half = current.shape[0] // 2
        pairs = [(k, k ^ (1 << place)) for k in range(members)]
        mine = (me >> place) & 1
        kept = lax.dynamic_slice_in_dim(current, mine * half, half, 0)
        sent = lax.dynamic_slice_in_dim(current, (1 - mine) * half, half, 0)
        current = kept + lax.ppermute(sent.astype(BF), "dp", pairs).astype(F32)
        steps.append((pairs, mine))
        place += 1
    all_part, own_part = current[:, :n_shared].astype(BF), current[:, n_shared:].astype(BF)
    jump = 1
    while jump < n:
        arrived = lax.ppermute(all_part, "tensor", [(k, k ^ jump) for k in range(n)])
        all_part = (all_part.astype(F32) + arrived.astype(F32)).astype(BF)
        jump *= 2
    current = jnp.concatenate([all_part, own_part], axis=1)
    for pairs, mine in steps[::-1]:
        arrived = lax.ppermute(current, "dp", pairs)
        low = jnp.where(mine == 0, current, arrived)
        high = jnp.where(mine == 0, arrived, current)
        current = jnp.concatenate([low, high], axis=0)
    current = current.astype(F32)
    return current[:, :n_shared].reshape(-1, width), current[:, n_shared:].reshape(-1, width)


def normalize(inputs):
    values = inputs.astype(F32)
    center = values - jnp.mean(values, axis=-1, keepdims=True)
    inv_scale = lax.rsqrt(jnp.mean(center * center, axis=-1, keepdims=True) + EPSILON)
    return center * inv_scale, inv_scale


def on_device(
    layer_input,
    document_lengths,
    attention_norm_gain,
    feedfwd_norm_gain,
    query_key_value_weight,
    output_weight,
    up_weight,
    down_weight,
    adapter_query_key_value_first,
    adapter_query_key_value_second,
    adapter_output_first,
    adapter_output_second,
    adapter_up_first,
    adapter_up_second,
    adapter_down_first,
    adapter_down_second,
    cotangent,
):
    own_x, own_g = layer_input[0], cotangent[0]
    shard_len, width = own_x.shape
    seq_len = shard_len * lax.axis_size("tensor")
    rank = adapter_up_first.shape[1]
    head_cols = query_key_value_weight.shape[2]
    heads = head_cols // HEAD_DIM

    start = token_starts(document_lengths[0], seq_len)
    offset = (jnp.arange(seq_len, dtype=jnp.int32) - start).astype(F32)
    inverse = jnp.exp(jnp.arange(HALF, dtype=F32) * (-2.0 * math.log(10000.0) / ROT))
    angles = inverse[:, None] * offset[None, :]
    cosine, sine, start = jnp.cos(angles), jnp.sin(angles), start[None]

    gain_a, gain_m = attention_norm_gain[:, None], feedfwd_norm_gain[:, None]
    in_weight = jnp.concatenate(
        [
            (
                (
                    query_key_value_weight[i].astype(F32)
                    + ADAPTER_SCALE
                    * mm(
                        adapter_query_key_value_first[i], adapter_query_key_value_second[i], 1, 0
                    )
                )
                * gain_a
            ).astype(BF)
            for i in range(3)
        ],
        axis=1,
    )
    up_in = (
        (up_weight.astype(F32) + ADAPTER_SCALE * mm(adapter_up_first, adapter_up_second, 1, 0))
        * gain_m
    ).astype(BF)
    low_in = jnp.concatenate(
        [(adapter_query_key_value_first[i].astype(F32) * gain_a).astype(BF) for i in range(3)]
        + [(adapter_up_first.astype(F32) * gain_m).astype(BF)],
        axis=1,
    )
    out_full = (
        output_weight.astype(F32)
        + ADAPTER_SCALE * mm(adapter_output_first, adapter_output_second, 1, 0)
    ).astype(BF)
    down_full = (
        down_weight.astype(F32)
        + ADAPTER_SCALE * mm(adapter_down_first, adapter_down_second, 1, 0)
    ).astype(BF)
    second = jnp.concatenate([adapter_output_second, adapter_down_second], axis=0)

    rows = gather_rows(own_x)
    hat = normalize(rows)[0].astype(BF)
    pre = mm(in_weight, hat, 0, 1).reshape(3, heads, HEAD_DIM, seq_len)
    low = mm(hat, low_in, 1, 0).astype(BF)
    pre_up = mm(hat, up_in, 1, 0)
    qkv, mixed, log_total = forward_attention(start, cosine, sine, pre)
    mixed_rows = mixed.reshape(head_cols, seq_len)
    cdf = 0.5 * (1.0 + lax.erf(pre_up * (2.0**-0.5)))
    act = (pre_up * cdf).astype(BF)
    slope = cdf + pre_up * (jnp.exp(-0.5 * pre_up * pre_up) * (1.0 / math.sqrt(2.0 * math.pi)))
    slope = slope.astype(BF)

    def out_piece(c):
        at = c * shard_len
        return mm(
            lax.dynamic_slice_in_dim(mixed_rows, at, shard_len, 1), out_full, 0, 0
        ) + mm(lax.dynamic_slice_in_dim(act, at, shard_len, 0), down_full, 1, 0)

    layer_output = (own_x.astype(F32) + ring_scatter(out_piece)).astype(BF)

    own_g_late, rows = lax.optimization_barrier((own_g, rows))
    grad = gather_rows(own_g_late)
    grad_mixed = mm(out_full, grad, 1, 1).astype(BF)
    grad_act = mm(grad, down_full, 1, 1)
    grad_up = (grad_act * slope.astype(F32)).astype(BF)
    grad_low_out = (ADAPTER_SCALE * mm(grad, second, 1, 1)).astype(BF)
    low_out = jnp.concatenate(
        [
            mm(mixed_rows, adapter_output_first, 0, 0).astype(BF),
            mm(act, adapter_down_first, 1, 0).astype(BF),
        ],
        axis=1,
    )
    b_out_t = ADAPTER_SCALE * mm(grad, low_out, 0, 0)
    a_out = mm(mixed_rows, grad_low_out[:, :rank], 1, 0)
    a_down = mm(act, grad_low_out[:, rank:], 0, 0)
    low_up_grad = (ADAPTER_SCALE * mm(grad_up, adapter_up_second, 1, 1)).astype(BF)
    a_up = mm(hat, low_up_grad, 0, 0) * gain_m
    b_up_t = ADAPTER_SCALE * mm(grad_up, low[:, 3 * rank :], 0, 0)
    early_shared, early_split = group_sum(
        jnp.concatenate([a_up, b_out_t[:, :rank], b_out_t[:, rank:]], axis=0),
        jnp.concatenate([b_up_t, a_out, a_down], axis=0),
    )

    grad_pre = backward_attention(
        start,
        cosine,
        sine,
        qkv,
        mixed,
        log_total,
        grad_mixed.reshape(heads, HEAD_DIM, seq_len),
    ).reshape(3 * head_cols, seq_len)

    def in_piece(c):
        at = c * shard_len
        return mm(
            lax.dynamic_slice_in_dim(grad_pre, at, shard_len, 1), in_weight, 0, 1
        ) + mm(lax.dynamic_slice_in_dim(grad_up, at, shard_len, 0), up_in, 1, 1)

    grad_hat = ring_scatter(in_piece)
    parts = [grad_pre[i * head_cols : (i + 1) * head_cols] for i in range(3)]
    low_grad = jnp.concatenate(
        [
            (ADAPTER_SCALE * mm(parts[i], adapter_query_key_value_second[i], 0, 1)).astype(BF)
            for i in range(3)
        ],
        axis=1,
    )
    a_qkv = mm(hat, low_grad, 0, 0) * gain_a
    b_qkv_t = jnp.concatenate(
        [
            ADAPTER_SCALE * mm(parts[i], low[:, i * rank : (i + 1) * rank], 1, 0)
            for i in range(3)
        ],
        axis=0,
    )
    late_shared, late_split = group_sum(
        jnp.concatenate([a_qkv[:, i * rank : (i + 1) * rank] for i in range(3)], axis=0),
        b_qkv_t,
    )

    own_hat, own_scale = normalize(own_x)
    mean_grad = jnp.mean(grad_hat, axis=-1, keepdims=True)
    mean_cross = jnp.mean(grad_hat * own_hat, axis=-1, keepdims=True)
    grad_in = own_g.astype(F32) + own_scale * (grad_hat - mean_grad - own_hat * mean_cross)

    hidden = up_weight.shape[1]
    return (
        layer_output[None],
        grad_in[None],
        late_shared.reshape(3, width, rank),
        jnp.swapaxes(late_split.reshape(3, head_cols, rank), 1, 2),
        early_split[hidden : hidden + head_cols],
        early_shared[width : 2 * width].T,
        early_shared[:width],
        early_split[:hidden].T,
        early_split[hidden + head_cols :],
        early_shared[2 * width :].T,
    )


def solution(mesh):
    in_specs = (
        P("dp", "tensor", None),
        P("dp", None),
        P(),
        P(),
        P(None, None, "tensor"),
        P("tensor", None),
        P(None, "tensor"),
        P("tensor", None),
        P(),
        P(None, None, "tensor"),
        P("tensor", None),
        P(),
        P(),
        P(None, "tensor"),
        P("tensor", None),
        P(),
        P("dp", "tensor", None),
    )
    out_specs = (
        P("dp", "tensor", None),
        P("dp", "tensor", None),
        P(),
        P(None, None, "tensor"),
        P("tensor", None),
        P(),
        P(),
        P(None, "tensor"),
        P("tensor", None),
        P(),
    )
    return jax.shard_map(
        on_device, mesh=mesh, in_specs=in_specs, out_specs=out_specs, check_vma=False
    )
```

```python
import math

import jax
import jax.numpy as jnp
from jax import lax
from jax.experimental import pallas as pl
from jax.experimental.pallas import tpu as pltpu
from jax.sharding import PartitionSpec as P

HEAD_DIM = 64
ROT = 16
HALF = ROT // 2
BLOCK = 256
MOST_DOC = 512

EPSILON = 1e-05
ADAPTER_SCALE = 0.25
MASKED = -1e30
VMEM_GRANT = 12 << 20
BF = jnp.bfloat16
F32 = jnp.float32


def mm(left, right, left_dim, right_dim):
    return lax.dot_general(
        left, right, (((left_dim,), (right_dim,)), ((), ())), preferred_element_type=F32
    )


def call(kernel, operands, outputs, scratch=(), flops=0, exps=0, scalars=0):
    spaces = [pltpu.SMEM] * scalars + [pltpu.VMEM] * (len(operands) - scalars)
    moved = sum(math.prod(s) * jnp.dtype(d).itemsize for s, d in outputs)
    return pl.pallas_call(
        kernel,
        in_specs=[pl.BlockSpec(memory_space=space) for space in spaces],
        out_specs=[pl.BlockSpec(memory_space=pltpu.VMEM) for _ in outputs],
        out_shape=[jax.ShapeDtypeStruct(s, d) for s, d in outputs],
        scratch_shapes=list(scratch),
        compiler_params=pltpu.CompilerParams(vmem_limit_bytes=VMEM_GRANT),
        cost_estimate=pl.CostEstimate(
            flops=flops, bytes_accessed=2 * moved, transcendentals=exps
        ),
    )(*operands)


def places_kernel(places_ref, lengths_ref, start_ref, cos_ref, sin_ref, *shards):
    count, seq_len = lengths_ref.shape[1], start_ref.shape[1]
    pos = lax.broadcasted_iota(jnp.int32, (HALF, seq_len), 1)
    start, end = jnp.zeros((HALF, seq_len), jnp.int32), jnp.int32(0)
    for j in range(count):
        end = end + lengths_ref[0, j]
        start = jnp.where(pos >= end, end, start)
    start_ref[...] = start[:1]
    row = lax.broadcasted_iota(jnp.int32, (HALF, seq_len), 0).astype(F32)
    inverse = jnp.exp(row * (-2.0 * math.log(10000.0) / ROT))
    angles = (pos - start).astype(F32) * inverse
    cos_ref[...] = jnp.cos(angles)
    sin_ref[...] = jnp.sin(angles)
    n = len(shards) // 2
    for k in range(n):
        at = lanes(places_ref[k], seq_len // n)
        shards[k][...] = cos_ref[:, at]
        shards[n + k][...] = sin_ref[:, at]


def turn(value, cosine, sine):
    lead, tail = value[:HALF], value[HALF:ROT]
    return jnp.concatenate(
        [lead * cosine - tail * sine, tail * cosine + lead * sine, value[ROT:]], axis=0
    )


def lanes(place, count):
    return pl.ds(pl.multiple_of(place * count, 128), count)


def merge_kernel(
    qkv_ref,
    qkv_first_ref,
    qkv_second_ref,
    up_ref,
    up_first_ref,
    up_second_ref,
    out_ref,
    out_first_ref,
    out_second_ref,
    down_ref,
    down_first_ref,
    down_second_ref,
    gain_a_ref,
    gain_m_ref,
    in_full_ref,
    up_full_ref,
    out_full_ref,
    down_full_ref,
):
    cols = qkv_ref.shape[2]

    def joined(weight, first, second):
        return weight.astype(F32) + ADAPTER_SCALE * mm(first, second, 1, 0)

    def column(row):
        return jnp.broadcast_to(row, (128, row.shape[1])).T

    def times(value, tall):
        return jnp.concatenate(
            [value[:, k : k + 128] * tall for k in range(0, value.shape[1], 128)], axis=1
        )

    gain_a, gain_m = column(gain_a_ref[...]), column(gain_m_ref[...])

    for i in range(3):
        in_full_ref[:, i * cols : (i + 1) * cols] = times(
            joined(qkv_ref[i], qkv_first_ref[i], qkv_second_ref[i]), gain_a
        ).astype(BF)
    up_full_ref[...] = times(
        joined(up_ref[...], up_first_ref[...], up_second_ref[...]), gain_m
    ).astype(BF)
    out_full_ref[...] = joined(out_ref[...], out_first_ref[...], out_second_ref[...]).astype(BF)
    down_full_ref[...] = joined(down_ref[...], down_first_ref[...], down_second_ref[...]).astype(
        BF
    )


def merge_weights(qkv, up, out, down, qkv_ab, up_ab, out_ab, down_ab, gain_a, gain_m):
    steps = 4
    width, cols = qkv.shape[1], qkv.shape[2]
    hidden, rank = up.shape[1], up_ab[0].shape[1]
    rows, out_rows, down_rows = width // steps, cols // steps, hidden // steps

    def fixed(shape):
        return pl.BlockSpec(shape, lambda s: (0,) * len(shape))

    def moving(shape):
        return pl.BlockSpec(shape, lambda s: (s,) + (0,) * (len(shape) - 1))

    def middle(shape):
        return pl.BlockSpec(shape, lambda s: (0, s, 0))

    return pl.pallas_call(
        merge_kernel,
        grid=(steps,),
        in_specs=[
            middle((3, rows, cols)),
            middle((3, rows, rank)),
            fixed((3, rank, cols)),
            moving((rows, hidden)),
            moving((rows, rank)),
            fixed((rank, hidden)),
            moving((out_rows, width)),
            moving((out_rows, rank)),
            fixed((rank, width)),
            moving((down_rows, width)),
            moving((down_rows, rank)),
            fixed((rank, width)),
            pl.BlockSpec((1, rows), lambda s: (0, s)),
            pl.BlockSpec((1, rows), lambda s: (0, s)),
        ],
        out_specs=[
            moving((rows, 3 * cols)),
            moving((rows, hidden)),
            moving((out_rows, width)),
            moving((down_rows, width)),
        ],
        out_shape=[
            jax.ShapeDtypeStruct((width, 3 * cols), BF),
            jax.ShapeDtypeStruct((width, hidden), BF),
            jax.ShapeDtypeStruct((cols, width), BF),
            jax.ShapeDtypeStruct((hidden, width), BF),
        ],
        compiler_params=pltpu.CompilerParams(vmem_limit_bytes=VMEM_GRANT),
        cost_estimate=pl.CostEstimate(
            flops=2 * rank * width * (4 * cols + 2 * hidden),
            bytes_accessed=4 * width * (4 * cols + 2 * hidden),
            transcendentals=0,
        ),
    )(
        qkv,
        qkv_ab[0],
        qkv_ab[1],
        up,
        up_ab[0],
        up_ab[1],
        out,
        out_ab[0],
        out_ab[1],
        down,
        down_ab[0],
        down_ab[1],
        gain_a,
        gain_m,
    )


def project_kernel(
    x_ref,
    gain_a_ref,
    gain_m_ref,
    cos_ref,
    sin_ref,
    qkv_weight_ref,
    qkv_first_ref,
    qkv_second_ref,
    up_first_ref,
    up_ref,
    up_second_ref,
    qkv_ref,
    low_ref,
    hat_ref,
    act_ref,
    slope_ref,
):
    rank = up_first_ref.shape[1]
    cols = qkv_weight_ref.shape[2]
    values = x_ref[...].astype(F32)
    center = values - jnp.mean(values, axis=-1, keepdims=True)
    hat = center * lax.rsqrt(jnp.mean(center * center, axis=-1, keepdims=True) + EPSILON)
    hat_ref[...] = hat.astype(BF)
    attn_in = (hat * gain_a_ref[...]).astype(BF)
    feed_in = (hat * gain_m_ref[...]).astype(BF)
    cosine, sine = cos_ref[...], sin_ref[...]
    for i in range(3):
        low = mm(attn_in, qkv_first_ref[i], 1, 0).astype(BF)
        low_ref[:, i * rank : (i + 1) * rank] = low
        pre = mm(attn_in, qkv_weight_ref[i], 1, 0) + ADAPTER_SCALE * mm(
            low, qkv_second_ref[i], 1, 0
        )
        pre = pre.T
        for head in range(cols // HEAD_DIM):
            rows = pre[head * HEAD_DIM : (head + 1) * HEAD_DIM]
            if i < 2:
                rows = turn(rows, cosine, sine)
            if i == 0:
                rows = rows * (HEAD_DIM**-0.5)
            qkv_ref[i, head] = rows.astype(BF)
    low = mm(feed_in, up_first_ref[...], 1, 0).astype(BF)
    low_ref[:, 3 * rank :] = low
    for begin in range(0, up_ref.shape[1], BLOCK):
        part = slice(begin, begin + BLOCK)
        pre = mm(feed_in, up_ref[:, part], 1, 0) + ADAPTER_SCALE * mm(
            low, up_second_ref[:, part], 1, 0
        )
        cdf = 0.5 * (1.0 + lax.erf(pre * (2.0**-0.5)))
        act_ref[:, part] = (pre * cdf).astype(BF)
        slope_ref[:, part] = (
            cdf + pre * (jnp.exp(-0.5 * pre * pre) * (1.0 / math.sqrt(2.0 * math.pi)))
        ).astype(BF)


def project(rows, gains, turns, weights):
    count, width = rows.shape
    cols, hidden, rank = weights[0].shape[2], weights[4].shape[1], weights[3].shape[1]
    return call(
        project_kernel,
        [rows, *gains, *turns, *weights],
        [
            ((3, cols // HEAD_DIM, HEAD_DIM, count), BF),
            ((count, 4 * rank), BF),
            ((count, width), BF),
            ((count, hidden), BF),
            ((count, hidden), BF),
        ],
        flops=2 * count * width * (3 * cols + hidden + 4 * rank),
        exps=2 * count * hidden,
    )


def allowed_pairs(start, query_block, key_block):
    key_pos = key_block * BLOCK + lax.broadcasted_iota(jnp.int32, (BLOCK, BLOCK), 0)
    keep = key_pos >= start
    if key_block == query_block:
        query_pos = query_block * BLOCK + lax.broadcasted_iota(jnp.int32, (BLOCK, BLOCK), 1)
        keep = keep & (key_pos <= query_pos)
    return keep


def key_blocks(query_block):
    return range(max(0, query_block - MOST_DOC // BLOCK), query_block + 1)


def attend_forward(n, places_ref, start_ref, *rest):
    chunks, outs, log_ref = rest[:n], rest[n : 2 * n], rest[2 * n]
    qkv, mixed_all = rest[2 * n + 1 :]
    seq_len = start_ref.shape[1]
    count = seq_len // n
    heads = qkv.shape[1]
    for c in range(n):
        qkv[:, :, :, lanes(places_ref[c], count)] = chunks[c][...]

    def one_head(head, carry):
        queries, keys, values = qkv[0, head], qkv[1, head], qkv[2, head]
        keys_t = keys.T
        for i in range(seq_len // BLOCK):
            at = slice(i * BLOCK, (i + 1) * BLOCK)
            start = start_ref[:, at]
            scores = []
            for j in key_blocks(i):
                raw = mm(keys_t[j * BLOCK : (j + 1) * BLOCK], queries[:, at], 1, 0)
                scores.append(jnp.where(allowed_pairs(start, i, j), raw, MASKED))
            peak = jnp.max(scores[0], axis=0, keepdims=True)
            for block in scores[1:]:
                peak = jnp.maximum(peak, jnp.max(block, axis=0, keepdims=True))
            total, mixed = 0.0, 0.0
            for j, block in zip(key_blocks(i), scores):
                terms = jnp.exp(block - peak)
                total = total + jnp.sum(terms, axis=0, keepdims=True)
                mixed = mixed + mm(
                    values[:, j * BLOCK : (j + 1) * BLOCK], terms.astype(BF), 1, 0
                )
            mixed_all[head, :, at] = (mixed / total).astype(BF)
            log_ref[head, :, at] = peak + jnp.log(total)
        return carry

    lax.fori_loop(0, heads, one_head, 0)
    for c in range(n):
        outs[c][...] = mixed_all[:, :, lanes(places_ref[c], count)]


def attend_backward(n, places_ref, start_ref, cos_ref, sin_ref, log_ref, *rest):
    chunks, outs, grads, results = (rest[k * n : (k + 1) * n] for k in range(4))
    qkv, mixed_all, grad_all, result = rest[4 * n :]
    seq_len = start_ref.shape[1]
    count = seq_len // n
    heads = qkv.shape[1]
    for c in range(n):
        at = lanes(places_ref[c], count)
        qkv[:, :, :, at] = chunks[c][...]
        mixed_all[:, :, at] = outs[c][...]
        grad_all[:, :, at] = grads[c][...]
    cosine, sine = cos_ref[...], -sin_ref[...]
    blocks = seq_len // BLOCK

    def one_head(head, carry):
        queries, keys, values = qkv[0, head], qkv[1, head], qkv[2, head]
        grad = grad_all[head]
        inner = jnp.sum(
            grad.astype(F32) * mixed_all[head].astype(F32), axis=0, keepdims=True
        )
        keys_t, values_t = keys.T, values.T
        grad_keys, grad_values = [0.0] * blocks, [0.0] * blocks
        for i in range(blocks):
            at = slice(i * BLOCK, (i + 1) * BLOCK)
            start, log_total, inner_here = start_ref[:, at], log_ref[head, :, at], inner[:, at]
            query, grad_here = queries[:, at], grad[:, at]
            grad_query = 0.0
            for j in key_blocks(i):
                there = slice(j * BLOCK, (j + 1) * BLOCK)
                raw = mm(keys_t[there], query, 1, 0)
                terms = jnp.exp(jnp.where(allowed_pairs(start, i, j), raw, MASKED) - log_total)
                grad_terms = mm(values_t[there], grad_here, 1, 0)
                grad_scores = (terms * (grad_terms - inner_here)).astype(BF)
                grad_values[j] = grad_values[j] + mm(grad_here, terms.astype(BF), 1, 1)
                grad_keys[j] = grad_keys[j] + mm(query, grad_scores, 1, 1)
                grad_query = grad_query + mm(keys[:, there], grad_scores, 1, 0)
            grad_query = turn(grad_query * (HEAD_DIM**-0.5), cosine[:, at], sine[:, at])
            result[0, head, :, at] = grad_query.astype(BF)
        for j in range(blocks):
            there = slice(j * BLOCK, (j + 1) * BLOCK)
            result[1, head, :, there] = turn(
                grad_keys[j], cosine[:, there], sine[:, there]
            ).astype(BF)
            result[2, head, :, there] = grad_values[j].astype(BF)
        return carry

    lax.fori_loop(0, heads, one_head, 0)
    for c in range(n):
        results[c][...] = result[:, :, :, lanes(places_ref[c], count)]


def forward_attention(places, start, chunks):
    n = len(chunks)
    _, heads, _, count = chunks[0].shape
    seq_len = n * count
    pairs = heads * seq_len * seq_len // 2
    *outs, log_total = call(
        lambda *refs: attend_forward(n, *refs),
        [places, start, *chunks],
        [((heads, HEAD_DIM, count), BF)] * n + [((heads, 1, seq_len), F32)],
        [
            pltpu.VMEM((3, heads, HEAD_DIM, seq_len), BF),
            pltpu.VMEM((heads, HEAD_DIM, seq_len), BF),
        ],
        flops=pairs * 4 * HEAD_DIM * 4,
        exps=pairs,
        scalars=1,
    )
    return outs, log_total


def backward_attention(places, start, cosine, sine, log_total, chunks, outs, grads):
    n = len(chunks)
    _, heads, _, count = chunks[0].shape
    seq_len = n * count
    pairs = heads * seq_len * seq_len // 2
    return call(
        lambda *refs: attend_backward(n, *refs),
        [places, start, cosine, sine, log_total, *chunks, *outs, *grads],
        [((3, heads, HEAD_DIM, count), BF)] * n,
        [
            pltpu.VMEM((3, heads, HEAD_DIM, seq_len), BF),
            pltpu.VMEM((heads, HEAD_DIM, seq_len), BF),
            pltpu.VMEM((heads, HEAD_DIM, seq_len), BF),
            pltpu.VMEM((3, heads, HEAD_DIM, seq_len), BF),
        ],
        flops=pairs * 10 * HEAD_DIM * 4,
        exps=pairs,
        scalars=1,
    )


def out_kernel(
    mixed_ref, act_ref, out_full_ref, down_full_ref, out_first_ref, down_first_ref, *rest
):
    piece_ref, low_ref = rest[-2:]
    rank = out_first_ref.shape[1]
    cols, count = out_full_ref.shape[0], act_ref.shape[0]
    mixed = mixed_ref[...].reshape(cols, count)
    act = act_ref[...]
    total = mm(mixed, out_full_ref[...], 0, 0) + mm(act, down_full_ref[...], 1, 0)
    if len(rest) > 2:
        total = total + rest[0][...].astype(F32)
    piece_ref[...] = total.astype(piece_ref.dtype)
    low_ref[:, :rank] = mm(mixed, out_first_ref[...], 0, 0).astype(BF)
    low_ref[:, rank:] = mm(act, down_first_ref[...], 1, 0).astype(BF)


def out_piece(mixed, act, out_full, down_full, out_first, down_first, dtype, arrived=None):
    count, hidden = act.shape
    width, rank = out_full.shape[1], out_first.shape[1]
    operands = [mixed, act, out_full, down_full, out_first, down_first]
    return call(
        out_kernel,
        operands + ([] if arrived is None else [arrived]),
        [((count, width), dtype), ((count, 2 * rank), BF)],
        flops=2 * count * (out_full.shape[0] + hidden) * width,
    )


def pull_kernel(
    g_ref,
    slope_ref,
    out_full_ref,
    down_ref,
    out_second_ref,
    down_second_ref,
    mixed_ref,
    low_ref,
    up_ref,
):
    grad = g_ref[...]
    mixed = mm(out_full_ref[...], grad, 1, 1)
    for head in range(mixed.shape[0] // HEAD_DIM):
        mixed_ref[head] = mixed[head * HEAD_DIM : (head + 1) * HEAD_DIM].astype(BF)
    rank = out_second_ref.shape[0]
    low_ref[:, :rank] = (ADAPTER_SCALE * mm(grad, out_second_ref[...], 1, 1)).astype(BF)
    low_ref[:, rank:] = (ADAPTER_SCALE * mm(grad, down_second_ref[...], 1, 1)).astype(BF)
    for begin in range(0, up_ref.shape[1], BLOCK):
        part = slice(begin, begin + BLOCK)
        up_ref[:, part] = (
            mm(grad, down_ref[part], 1, 1) * slope_ref[:, part].astype(F32)
        ).astype(BF)


def pull_back(grad, slope, out_full, down_full, out_second, down_second):
    count, width = grad.shape
    hidden, cols, twice = slope.shape[1], out_full.shape[0], 2 * out_second.shape[0]
    return call(
        pull_kernel,
        [grad, slope, out_full, down_full, out_second, down_second],
        [
            ((cols // HEAD_DIM, HEAD_DIM, count), BF),
            ((count, twice), BF),
            ((count, hidden), BF),
        ],
        flops=2 * count * width * (cols + hidden + twice),
    )


def slot_code(slot, bits):
    return sum(((slot >> b) & 1) << (bits - 1 - b) for b in range(bits))


def part_sizes(members):
    sizes = []
    while members > 1:
        members //= 2
        sizes.append(members)
    return sizes + [1]


def spread(me, members, fields, parts):
    bits = members.bit_length() - 1
    for size, part in zip(part_sizes(members), parts):
        for k in range(size):
            slot = k + (size if part is not parts[-1] else 0)
            owner = me ^ slot_code(slot, bits)
            low = 0
            for field in fields:
                rows = field.shape[0] // members
                at = pl.ds(pl.multiple_of(owner * rows, rows), rows)
                part[k, low : low + rows] = field[at]
                low += rows


def gather_spread(me, members, fields, parts):
    bits = members.bit_length() - 1
    for size, part in zip(part_sizes(members), parts):
        for k in range(size):
            slot = k + (size if part is not parts[-1] else 0)
            owner = me ^ slot_code(slot, bits)
            low = 0
            for field in fields:
                rows = field.shape[0] // members
                at = pl.ds(pl.multiple_of(owner * rows, rows), rows)
                field[at] = part[k, low : low + rows]
                low += rows


def early_kernel(chunks, packs, me_ref, up_second_ref, gain_ref, *rest):
    fields = 8
    more = rest[fields * chunks :]
    before, more = (more[:3], more[3:]) if packs != 1 else (None, more)
    if packs > 1:
        parts, more = more[: packs - 1], more[packs - 1 :]
        out_ref, shared_ref, split_ref = more
    else:
        shared_ref, split_ref, out_ref = more
    rank = up_second_ref.shape[0]
    shared_up, shared_out, up_b, down_a, out_a = 0.0, 0.0, 0.0, 0.0, 0.0
    for c in range(chunks):
        grad, grad_up, hat, act, low, low_out, grad_low, mixed = (
            ref[...] for ref in rest[c * fields : (c + 1) * fields]
        )
        mixed = mixed.reshape(-1, mixed.shape[-1])
        low_up_grad = (ADAPTER_SCALE * mm(grad_up, up_second_ref[...], 1, 1)).astype(BF)
        shared_up = shared_up + mm(low_up_grad, hat, 0, 0)
        shared_out = shared_out + mm(low_out, grad, 0, 0)
        up_b = up_b + mm(low[:, 3 * rank :], grad_up, 0, 0)
        down_a = down_a + mm(grad_low[:, rank:], act, 0, 0)
        out_a = out_a + mm(grad_low[:, :rank], mixed, 0, 1)
    shared_up = shared_up * gain_ref[...]
    shared_out = ADAPTER_SCALE * shared_out
    up_b = ADAPTER_SCALE * up_b
    if before is not None:
        shared_up = shared_up + before[0][:rank]
        shared_out = shared_out + before[0][rank:]
        up_b = up_b + before[1][:rank]
        down_a = down_a + before[1][rank:]
        out_a = out_a + before[2][...]
    shared_ref[:rank] = shared_up.astype(shared_ref.dtype)
    shared_ref[rank:] = shared_out.astype(shared_ref.dtype)
    split_ref[:rank] = up_b.astype(split_ref.dtype)
    split_ref[rank:] = down_a.astype(split_ref.dtype)
    out_ref[...] = out_a.astype(out_ref.dtype)
    if packs > 1:
        members = 1 << (packs - 2)
        spread(me_ref[0], members, (shared_ref, split_ref), parts)


def part_shapes(members, rows, width):
    return [((size, rows, width), BF) for size in part_sizes(members)]


def early_sums(me, items, up_second, gain, before=None, members=0):
    width, hidden, rank = items[0][0].shape[1], items[0][1].shape[1], up_second.shape[0]
    cols = items[0][7].shape[0] * HEAD_DIM
    sums = [((3 * rank, width), F32), ((2 * rank, hidden), F32), ((rank, cols), F32)]
    operands = [me, up_second, gain] + [array for item in items for array in item]
    scratch = []
    if before is None:
        packs, outputs = 1, sums
    elif not members:
        packs, outputs = 0, sums
    else:
        packs = members.bit_length() + 1
        outputs = part_shapes(members, 5 * rank // members, width) + [((rank, cols), BF)]
        scratch = [pltpu.VMEM((3 * rank, width), BF), pltpu.VMEM((2 * rank, hidden), BF)]
    return call(
        lambda *refs: early_kernel(len(items), packs, *refs),
        operands + ([] if before is None else list(before)),
        outputs,
        scratch,
        flops=2 * len(items) * items[0][0].shape[0] * rank * 6 * width,
        scalars=1,
    )


def in_kernel(grad_pre_ref, grad_up_ref, in_full_ref, up_full_ref, *rest):
    piece_ref = rest[-1]
    grad_pre = grad_pre_ref[...].reshape(in_full_ref.shape[1], grad_up_ref.shape[0])
    total = mm(grad_pre, in_full_ref[...], 0, 1) + mm(grad_up_ref[...], up_full_ref[...], 1, 1)
    if len(rest) > 1:
        total = total + rest[0][...].astype(F32)
    piece_ref[...] = total.astype(piece_ref.dtype)


def in_piece(grad_pre, grad_up, in_full, up_full, dtype, arrived=None):
    count, hidden = grad_up.shape
    width = up_full.shape[0]
    operands = [grad_pre, grad_up, in_full, up_full]
    (piece,) = call(
        in_kernel,
        operands + ([] if arrived is None else [arrived]),
        [((count, width), dtype)],
        flops=2 * count * (in_full.shape[1] + hidden) * width,
    )
    return piece


def late_kernel(chunks, packs, me_ref, second_ref, gain_ref, *rest):
    fields = 3
    more = rest[fields * chunks :]
    rank, cols = second_ref.shape[1], second_ref.shape[2]
    shared, split = [0.0] * 3, [0.0] * 3
    for c in range(chunks):
        grad_pre, low, hat = (ref[...] for ref in rest[c * fields : (c + 1) * fields])
        for i in range(3):
            part = grad_pre[i].reshape(cols, -1)
            low_grad = (ADAPTER_SCALE * mm(part, second_ref[i], 0, 1)).astype(BF)
            shared[i] = shared[i] + mm(low_grad, hat, 0, 0)
            split[i] = split[i] + mm(low[:, i * rank : (i + 1) * rank], part, 0, 1)
    out_ref, more = more[0], more[1:]
    shared_ref, split_ref = more[-2:]
    for i in range(3):
        shared_ref[i * rank : (i + 1) * rank] = (shared[i] * gain_ref[...]).astype(BF)
        split_ref[:, i * cols : (i + 1) * cols] = (ADAPTER_SCALE * split[i]).astype(BF)
    split_ref[:, 3 * cols :] = out_ref[...].astype(BF)
    if packs:
        spread(me_ref[0], 1 << (packs - 1), (shared_ref, split_ref), more[:packs])


def late_sums(me, items, second, gain, out_a, members=0):
    width, rank, cols = items[0][2].shape[1], second.shape[1], second.shape[2]
    sums = [((3 * rank, width), BF), ((rank, 4 * cols), BF)]
    packs = members.bit_length() if members else 0
    return call(
        lambda *refs: late_kernel(len(items), packs, *refs),
        [me, second, gain] + [array for item in items for array in item] + [out_a],
        part_shapes(members, 4 * rank // members, width) if packs else sums,
        [pltpu.VMEM(*spec) for spec in sums] if packs else [],
        flops=2 * len(items) * items[0][1].shape[0] * rank * 3 * (width + 2 * cols),
        scalars=1,
    )


def early_unpack_kernel(packs, me_ref, *rest):
    parts = rest[:packs]
    up_a_ref, out_b_ref, down_b_ref, up_b_ref, down_a_ref, shared_ref, split_ref = rest[packs:]
    rank = out_b_ref.shape[0]
    gather_spread(me_ref[0], 1 << (packs - 1), (shared_ref, split_ref), parts)
    up_a_ref[...] = shared_ref[:rank].astype(F32).T
    out_b_ref[...] = shared_ref[rank : 2 * rank].astype(F32)
    down_b_ref[...] = shared_ref[2 * rank :].astype(F32)
    up_b_ref[...] = split_ref[:rank].astype(F32)
    down_a_ref[...] = split_ref[rank:].astype(F32).T


def late_unpack_kernel(packs, me_ref, *rest):
    parts = rest[:packs]
    a_ref, b_ref, out_a_ref, shared_ref, split_ref = rest[packs:]
    rank, cols = b_ref.shape[1], b_ref.shape[2]
    gather_spread(me_ref[0], 1 << (packs - 1), (shared_ref, split_ref), parts)
    for i in range(3):
        a_ref[i] = shared_ref[i * rank : (i + 1) * rank].astype(F32).T
        b_ref[i] = split_ref[:, i * cols : (i + 1) * cols].astype(F32)
    out_a_ref[...] = split_ref[:, 3 * cols :].astype(F32).T


def output_kernel(x_ref, own_ref, *rest):
    total = x_ref[...].astype(F32) + own_ref[...]
    for ref in rest[:-1]:
        total = total + ref[...].astype(F32)
    rest[-1][...] = total.astype(BF)


def input_grad_kernel(x_ref, g_ref, own_ref, *rest):
    total = own_ref[...]
    for ref in rest[:-1]:
        total = total + ref[...].astype(F32)
    hat, scale = normalize(x_ref[...])
    mean_grad = jnp.mean(total, axis=-1, keepdims=True)
    mean_cross = jnp.mean(total * hat, axis=-1, keepdims=True)
    rest[-1][...] = g_ref[...].astype(F32) + scale * (total - mean_grad - hat * mean_cross)


def swap_pairs(n):
    return [(i, i ^ 1) for i in range(n)]


def mirror_pairs(n):
    return [(i, n - 1 - i) for i in range(n)]


def together(*values):
    return lax.optimization_barrier(values)


def ring_scatter(piece, pieces):
    up = [(i, (i + 1) % pieces) for i in range(pieces)]
    running = piece(1, None)
    for k in range(2, pieces + 1):
        running = piece(k % pieces, lax.ppermute(running, "tensor", up))
    return running


def group_sum(parts, n_shared):
    members, n = lax.axis_size("dp"), lax.axis_size("tensor")
    parts = list(parts)
    bits = len(parts) - 1
    pairs = [[(k, k ^ (1 << b)) for k in range(members)] for b in range(bits)]
    for b in range(bits):
        arrived = lax.ppermute(parts[b], "dp", pairs[b]).astype(F32)
        for later in range(b + 1, bits + 1):
            size = parts[later].shape[0]
            low = size if later < bits else 0
            parts[later] = (
                parts[later].astype(F32) + arrived[low : low + size]
            ).astype(BF)
    shared, split = parts[-1][:, :n_shared], parts[-1][:, n_shared:]
    jump = 1
    while jump < n:
        arrived = lax.ppermute(shared, "tensor", [(k, k ^ jump) for k in range(n)])
        shared = (shared.astype(F32) + arrived.astype(F32)).astype(BF)
        jump *= 2
    have = jnp.concatenate([shared, split], axis=1)
    results = [have]
    for b in range(bits - 1, -1, -1):
        arrived = lax.ppermute(have, "dp", pairs[b])
        results.append(arrived)
        if b:
            have = jnp.concatenate([have, arrived], axis=0)
    return results[::-1]


def slow_parts(me, shared, split, members):
    bits = members.bit_length() - 1
    width = shared.shape[1]
    both = jnp.concatenate(
        [
            shared.astype(BF).reshape(members, -1, width),
            split.astype(BF).reshape(members, -1, width),
        ],
        axis=1,
    )
    order = jnp.asarray([slot_code(slot, bits) for slot in range(members)], jnp.int32) ^ me
    both = both[order]
    parts, top = [], members
    for size in part_sizes(members)[:-1]:
        parts.append(both[size:top])
        top = size
    return parts + [both[:1]]


def slow_whole(me, parts, n_shared, members):
    bits = members.bit_length() - 1
    both = jnp.concatenate(parts[::-1], axis=0)
    order = jnp.asarray([slot_code(slot, bits) for slot in range(members)], jnp.int32)
    both = both[order[jnp.arange(members, dtype=jnp.int32) ^ me]].astype(F32)
    width = both.shape[-1]
    return both[:, :n_shared].reshape(-1, width), both[:, n_shared:].reshape(-1, width)


def normalize(inputs):
    values = inputs.astype(F32)
    center = values - jnp.mean(values, axis=-1, keepdims=True)
    inv_scale = lax.rsqrt(jnp.mean(center * center, axis=-1, keepdims=True) + EPSILON)
    return center * inv_scale, inv_scale


def on_device(
    layer_input,
    document_lengths,
    attention_norm_gain,
    feedfwd_norm_gain,
    query_key_value_weight,
    output_weight,
    up_weight,
    down_weight,
    adapter_query_key_value_first,
    adapter_query_key_value_second,
    adapter_output_first,
    adapter_output_second,
    adapter_up_first,
    adapter_up_second,
    adapter_down_first,
    adapter_down_second,
    cotangent,
):
    own_x, own_g = layer_input[0], cotangent[0]
    shard_len, width = own_x.shape
    n = lax.axis_size("tensor")
    me = lax.axis_index("tensor")
    seq_len = shard_len * n
    rank = adapter_up_first.shape[1]
    cols = query_key_value_weight.shape[2]
    hidden = up_weight.shape[1]
    swap, mirror = swap_pairs(n), mirror_pairs(n)
    short = n == 4

    def send(value, pairs):
        return lax.ppermute(value, "tensor", pairs)

    members = lax.axis_size("dp")
    bits = members.bit_length() - 1
    tidy = short and hidden == width and 4 * cols == width and rank % (16 * members) == 0
    if short:
        owners = [me, me ^ 1, n - 1 - me, (n - 1 - me) ^ 1]
    else:
        owners = [lax.rem(me - k + n, n) for k in range(n)]
    places = jnp.stack(owners).astype(jnp.int32)
    me_dp = lax.axis_index("dp").astype(jnp.int32).reshape(1)
    places, me_dp, own_x = together(places, me_dp, own_x)
    turns = call(
        places_kernel,
        [places, document_lengths],
        [((1, seq_len), jnp.int32), ((HALF, seq_len), F32), ((HALF, seq_len), F32)]
        + [((HALF, shard_len), F32)] * (2 * n),
        scalars=2,
    )
    start, cosine, sine, turns = turns[0], turns[1], turns[2], turns[3:]
    gain_a, gain_m = attention_norm_gain[None], feedfwd_norm_gain[None]
    weights = (
        query_key_value_weight,
        adapter_query_key_value_first,
        adapter_query_key_value_second,
        adapter_up_first,
        up_weight,
        adapter_up_second,
    )

    def projected(k, rows):
        return project(rows, (gain_a, gain_m), (turns[k], turns[n + k]), weights)

    def merged():
        return merge_weights(
            query_key_value_weight,
            up_weight,
            output_weight,
            down_weight,
            (adapter_query_key_value_first, adapter_query_key_value_second),
            (adapter_up_first, adapter_up_second),
            (adapter_output_first, adapter_output_second),
            (adapter_down_first, adapter_down_second),
            gain_a,
            gain_m,
        )

    own_g_late = own_g
    if short:
        x_near, x_facing = send(own_x, swap), send(own_x, mirror)
        full = merged()
        first = projected(0, own_x)
        x_near, x_facing, first, full = together(x_near, x_facing, first, full)
        x_far = send(x_facing, swap)
        state = [first, projected(1, x_near), projected(2, x_facing)]
        x_far, state, own_g_late = together(x_far, state, own_g)
        g_near, g_facing = send(own_g_late, swap), send(own_g_late, mirror)
        state = state + [projected(3, x_far)]
    else:
        full = merged()
        up_ring = [(i, (i + 1) % n) for i in range(n)]
        state, moving = [projected(0, own_x)], own_x
        for k in range(1, n):
            moving = send(moving, up_ring)
            state.append(projected(k, moving))
    in_full, up_full, out_full, down_full = full
    qkv, low, hat, act, slope = (list(field) for field in zip(*state))
    mixed, log_total = forward_attention(places, start, qkv)
    low_out = [None] * n

    def out_part(k, dtype, arrived=None):
        piece, low_out[k] = out_piece(
            mixed[k],
            act[k],
            out_full,
            down_full,
            adapter_output_first,
            adapter_down_first,
            dtype,
            arrived,
        )
        return piece

    def pulled(k, grad):
        return pull_back(
            grad,
            slope[k],
            out_full,
            down_full,
            adapter_output_second,
            adapter_down_second,
        )

    def early_item(k, grad, back):
        return (grad, back[2], hat[k], act[k], low[k], low_out[k], back[1], mixed[k])

    if short:
        backs = [pulled(0, own_g)]
        y_far = out_part(3, BF)
        g_near, g_facing, backs, y_far = together(g_near, g_facing, backs, y_far)
        g_far = send(g_facing, swap)
        y_swap = send(y_far, swap)
        backs = backs + [pulled(1, g_near), pulled(2, g_facing)]
        y_near, y_own = out_part(1, BF), out_part(0, F32)
        y_facing = out_part(2, F32)
        all_g = [own_g, g_near, g_facing]
        before = early_sums(
            me_dp, [early_item(k, all_g[k], backs[k]) for k in range(3)], adapter_up_second, gain_m
        )
        g_far, y_swap, y_near, y_own, y_facing, backs, before = together(
            g_far, y_swap, y_near, y_own, y_facing, backs, before
        )
        backs = backs + [pulled(3, g_far)]
        early = early_sums(
            me_dp,
            [early_item(3, g_far, backs[3])],
            adapter_up_second,
            gain_m,
            before,
            members if tidy else 0,
        )
        y_facing = (y_facing + y_swap.astype(F32)).astype(BF)
        y_a, y_b = send(y_near, swap), send(y_facing, mirror)
    else:
        y_own = ring_scatter(lambda k, arrived: out_part(k, BF if k else F32, arrived), n)
        backs, moving, all_g = [pulled(0, own_g)], own_g, [own_g]
        for k in range(1, n):
            moving = send(moving, up_ring)
            all_g.append(moving)
            backs.append(pulled(k, moving))
        early = early_sums(
            me_dp, [early_item(k, all_g[k], backs[k]) for k in range(n)], adapter_up_second, gain_m
        )

    *early, out_a = early
    if not tidy:
        early = slow_parts(me_dp[0], early[0], early[1].reshape(-1, width), members)
    early = group_sum(early, 3 * rank // members)
    grad_pre = backward_attention(
        places, start, cosine, sine, log_total, qkv, mixed, [back[0] for back in backs]
    )

    def in_part(k, dtype, arrived=None):
        return in_piece(grad_pre[k], backs[k][2], in_full, up_full, dtype, arrived)

    if short:
        y_parts = [y_own, y_a, y_b]
        dx_swap = send(in_part(3, BF), swap)
        dx_a = send(in_part(1, BF), swap)
        dx_b = send(in_part(2, BF, dx_swap), mirror)
        dx_parts = [in_part(0, F32), dx_a, dx_b]
    else:
        y_parts = [y_own]
        dx_parts = [
            ring_scatter(lambda k, arrived: in_part(k, BF if k else F32, arrived), n)
        ]
    (layer_output,) = call(output_kernel, [own_x, *y_parts], [((shard_len, width), BF)])
    late = late_sums(
        me_dp,
        [(grad_pre[k], low[k], hat[k]) for k in range(n)],
        adapter_query_key_value_second,
        gain_a,
        out_a,
        members if tidy else 0,
    )
    if not tidy:
        late = slow_parts(me_dp[0], late[0], late[1].reshape(-1, width), members)
    late = group_sum(late, 3 * rank // members)
    (grad_in,) = call(
        input_grad_kernel, [own_x, own_g, *dx_parts], [((shard_len, width), F32)]
    )

    if tidy:
        up_a, out_b, down_b, up_b, down_a = call(
            lambda *refs: early_unpack_kernel(bits + 1, *refs),
            [me_dp, *early],
            [
                ((width, rank), F32),
                ((rank, width), F32),
                ((rank, width), F32),
                ((rank, hidden), F32),
                ((hidden, rank), F32),
            ],
            [pltpu.VMEM((3 * rank, width), BF), pltpu.VMEM((2 * rank, width), BF)],
            scalars=1,
        )
        a_qkv, b_qkv, out_a = call(
            lambda *refs: late_unpack_kernel(bits + 1, *refs),
            [me_dp, *late],
            [((3, width, rank), F32), ((3, rank, cols), F32), ((cols, rank), F32)],
            [pltpu.VMEM((3 * rank, width), BF), pltpu.VMEM((rank, width), BF)],
            scalars=1,
        )
    else:
        early_a, early_b = slow_whole(me_dp[0], early, 3 * rank // members, members)
        up_a, out_b, down_b = early_a[:rank].T, early_a[rank : 2 * rank], early_a[2 * rank :]
        early_b = early_b.reshape(2 * rank, hidden)
        up_b, down_a = early_b[:rank], early_b[rank:].T
        late_a, late_b = slow_whole(me_dp[0], late, 3 * rank // members, members)
        late_b = late_b.reshape(rank, 4 * cols)
        a_qkv = jnp.swapaxes(late_a.reshape(3, rank, width), 1, 2)
        b_qkv = jnp.stack([late_b[:, i * cols : (i + 1) * cols] for i in range(3)])
        out_a = late_b[:, 3 * cols :].T
    return (
        layer_output[None],
        grad_in[None],
        a_qkv,
        b_qkv,
        out_a,
        out_b,
        up_a,
        up_b,
        down_a,
        down_b,
    )


def solution(mesh):
    in_specs = (
        P("dp", "tensor", None),
        P("dp", None),
        P(),
        P(),
        P(None, None, "tensor"),
        P("tensor", None),
        P(None, "tensor"),
        P("tensor", None),
        P(),
        P(None, None, "tensor"),
        P("tensor", None),
        P(),
        P(),
        P(None, "tensor"),
        P("tensor", None),
        P(),
        P("dp", "tensor", None),
    )
    out_specs = (
        P("dp", "tensor", None),
        P("dp", "tensor", None),
        P(),
        P(None, None, "tensor"),
        P("tensor", None),
        P(),
        P(),
        P(None, "tensor"),
        P("tensor", None),
        P(),
    )
    return jax.shard_map(
        on_device, mesh=mesh, in_specs=in_specs, out_specs=out_specs, check_vma=False
    )
```

```python
import math

import jax
import jax.numpy as jnp
from jax import lax
from jax.experimental import pallas as pl
from jax.experimental.pallas import tpu as pltpu
from jax.sharding import PartitionSpec as P

HEAD_DIM = 64
ROT = 16
HALF = ROT // 2
BLOCK = 256
MOST_DOC = 512

EPSILON = 1e-05
ADAPTER_SCALE = 0.25
MASKED = -1e30
VMEM_GRANT = 12 << 20
BF = jnp.bfloat16
F32 = jnp.float32


def mm(left, right, left_dim, right_dim):
    return lax.dot_general(
        left, right, (((left_dim,), (right_dim,)), ((), ())), preferred_element_type=F32
    )


def call(kernel, operands, outputs, scratch=(), flops=0, exps=0, scalars=0):
    spaces = [pltpu.SMEM] * scalars + [pltpu.VMEM] * (len(operands) - scalars)
    moved = sum(math.prod(s) * jnp.dtype(d).itemsize for s, d in outputs)
    return pl.pallas_call(
        kernel,
        in_specs=[pl.BlockSpec(memory_space=space) for space in spaces],
        out_specs=[pl.BlockSpec(memory_space=pltpu.VMEM) for _ in outputs],
        out_shape=[jax.ShapeDtypeStruct(s, d) for s, d in outputs],
        scratch_shapes=list(scratch),
        compiler_params=pltpu.CompilerParams(vmem_limit_bytes=VMEM_GRANT),
        cost_estimate=pl.CostEstimate(
            flops=flops, bytes_accessed=2 * moved, transcendentals=exps
        ),
    )(*operands)


def places_kernel(places_ref, lengths_ref, start_ref, cos_ref, sin_ref, *shards):
    count, seq_len = lengths_ref.shape[1], start_ref.shape[1]
    pos = lax.broadcasted_iota(jnp.int32, (HALF, seq_len), 1)
    start, end = jnp.zeros((HALF, seq_len), jnp.int32), jnp.int32(0)
    for j in range(count):
        end = end + lengths_ref[0, j]
        start = jnp.where(pos >= end, end, start)
    start_ref[...] = start[:1]
    row = lax.broadcasted_iota(jnp.int32, (HALF, seq_len), 0).astype(F32)
    inverse = jnp.exp(row * (-2.0 * math.log(10000.0) / ROT))
    angles = (pos - start).astype(F32) * inverse
    cos_ref[...] = jnp.cos(angles)
    sin_ref[...] = jnp.sin(angles)
    n = len(shards) // 2
    for k in range(n):
        at = lanes(places_ref[k], seq_len // n)
        shards[k][...] = cos_ref[:, at]
        shards[n + k][...] = sin_ref[:, at]


def turn(value, cosine, sine):
    lead, tail = value[:HALF], value[HALF:ROT]
    return jnp.concatenate(
        [lead * cosine - tail * sine, tail * cosine + lead * sine, value[ROT:]], axis=0
    )


def lanes(place, count):
    return pl.ds(pl.multiple_of(place * count, 128), count)


def merge_kernel(
    qkv_ref,
    qkv_first_ref,
    qkv_second_ref,
    up_ref,
    up_first_ref,
    up_second_ref,
    out_ref,
    out_first_ref,
    out_second_ref,
    down_ref,
    down_first_ref,
    down_second_ref,
    gain_a_ref,
    gain_m_ref,
    in_full_ref,
    up_full_ref,
    out_full_ref,
    down_full_ref,
):
    cols = qkv_ref.shape[2]

    def joined(weight, first, second):
        return weight.astype(F32) + ADAPTER_SCALE * mm(first, second, 1, 0)

    def column(row):
        return jnp.broadcast_to(row, (128, row.shape[1])).T

    def times(value, tall):
        return jnp.concatenate(
            [value[:, k : k + 128] * tall for k in range(0, value.shape[1], 128)], axis=1
        )

    gain_a, gain_m = column(gain_a_ref[...]), column(gain_m_ref[...])

    for i in range(3):
        in_full_ref[:, i * cols : (i + 1) * cols] = times(
            joined(qkv_ref[i], qkv_first_ref[i], qkv_second_ref[i]), gain_a
        ).astype(BF)
    up_full_ref[...] = times(
        joined(up_ref[...], up_first_ref[...], up_second_ref[...]), gain_m
    ).astype(BF)
    out_full_ref[...] = joined(out_ref[...], out_first_ref[...], out_second_ref[...]).astype(BF)
    down_full_ref[...] = joined(down_ref[...], down_first_ref[...], down_second_ref[...]).astype(
        BF
    )


def merge_weights(qkv, up, out, down, qkv_ab, up_ab, out_ab, down_ab, gain_a, gain_m):
    steps = 4
    width, cols = qkv.shape[1], qkv.shape[2]
    hidden, rank = up.shape[1], up_ab[0].shape[1]
    rows, out_rows, down_rows = width // steps, cols // steps, hidden // steps

    def fixed(shape):
        return pl.BlockSpec(shape, lambda s: (0,) * len(shape))

    def moving(shape):
        return pl.BlockSpec(shape, lambda s: (s,) + (0,) * (len(shape) - 1))

    def middle(shape):
        return pl.BlockSpec(shape, lambda s: (0, s, 0))

    return pl.pallas_call(
        merge_kernel,
        grid=(steps,),
        in_specs=[
            middle((3, rows, cols)),
            middle((3, rows, rank)),
            fixed((3, rank, cols)),
            moving((rows, hidden)),
            moving((rows, rank)),
            fixed((rank, hidden)),
            moving((out_rows, width)),
            moving((out_rows, rank)),
            fixed((rank, width)),
            moving((down_rows, width)),
            moving((down_rows, rank)),
            fixed((rank, width)),
            pl.BlockSpec((1, rows), lambda s: (0, s)),
            pl.BlockSpec((1, rows), lambda s: (0, s)),
        ],
        out_specs=[
            moving((rows, 3 * cols)),
            moving((rows, hidden)),
            moving((out_rows, width)),
            moving((down_rows, width)),
        ],
        out_shape=[
            jax.ShapeDtypeStruct((width, 3 * cols), BF),
            jax.ShapeDtypeStruct((width, hidden), BF),
            jax.ShapeDtypeStruct((cols, width), BF),
            jax.ShapeDtypeStruct((hidden, width), BF),
        ],
        compiler_params=pltpu.CompilerParams(vmem_limit_bytes=VMEM_GRANT),
        cost_estimate=pl.CostEstimate(
            flops=2 * rank * width * (4 * cols + 2 * hidden),
            bytes_accessed=4 * width * (4 * cols + 2 * hidden),
            transcendentals=0,
        ),
    )(
        qkv,
        qkv_ab[0],
        qkv_ab[1],
        up,
        up_ab[0],
        up_ab[1],
        out,
        out_ab[0],
        out_ab[1],
        down,
        down_ab[0],
        down_ab[1],
        gain_a,
        gain_m,
    )


def project_kernel(
    x_ref,
    gain_a_ref,
    gain_m_ref,
    cos_ref,
    sin_ref,
    qkv_weight_ref,
    qkv_first_ref,
    qkv_second_ref,
    up_first_ref,
    up_ref,
    up_second_ref,
    qkv_ref,
    low_ref,
    hat_ref,
    act_ref,
    slope_ref,
    mlp_ref,
):
    rank = up_first_ref.shape[1]
    cols = qkv_weight_ref.shape[2]
    values = x_ref[...].astype(F32)
    center = values - jnp.mean(values, axis=-1, keepdims=True)
    hat = center * lax.rsqrt(jnp.mean(center * center, axis=-1, keepdims=True) + EPSILON)
    hat_ref[...] = hat.astype(BF)
    attn_in = (hat * gain_a_ref[...]).astype(BF)
    feed_in = (hat * gain_m_ref[...]).astype(BF)
    cosine, sine = cos_ref[...], sin_ref[...]

    def one_third(i, carry):
        low = mm(attn_in, qkv_first_ref[i], 1, 0).astype(BF)
        low_ref[:, lanes(i, rank)] = low
        pre = mm(attn_in, qkv_weight_ref[i], 1, 0) + ADAPTER_SCALE * mm(
            low, qkv_second_ref[i], 1, 0
        )
        pre = pre.T
        turned = (i < 2).astype(F32)
        scale = jnp.where(i == 0, HEAD_DIM**-0.5, 1.0)
        cos_here = 1.0 + turned * (cosine - 1.0)
        sin_here = turned * sine
        for head in range(cols // HEAD_DIM):
            rows = turn(pre[head * HEAD_DIM : (head + 1) * HEAD_DIM], cos_here, sin_here)
            qkv_ref[i, head] = (rows * scale).astype(BF)
        return carry

    lax.fori_loop(0, 3, one_third, 0)
    low = mm(feed_in, up_first_ref[...], 1, 0).astype(BF)
    low_ref[:, 3 * rank :] = low
    mlp_ref[...] = feed_in

    def one_block(k, carry):
        part = lanes(k, BLOCK)
        pre = mm(mlp_ref[...], up_ref[:, part], 1, 0) + ADAPTER_SCALE * mm(
            low, up_second_ref[:, part], 1, 0
        )
        cdf = 0.5 * (1.0 + lax.erf(pre * (2.0**-0.5)))
        act_ref[:, part] = (pre * cdf).astype(BF)
        slope_ref[:, part] = (
            cdf + pre * (jnp.exp(-0.5 * pre * pre) * (1.0 / math.sqrt(2.0 * math.pi)))
        ).astype(BF)
        return carry

    lax.fori_loop(0, up_ref.shape[1] // BLOCK, one_block, 0)


def project(rows, gains, turns, weights):
    count, width = rows.shape
    cols, hidden, rank = weights[0].shape[2], weights[4].shape[1], weights[3].shape[1]
    return call(
        project_kernel,
        [rows, *gains, *turns, *weights],
        [
            ((3, cols // HEAD_DIM, HEAD_DIM, count), BF),
            ((count, 4 * rank), BF),
            ((count, width), BF),
            ((count, hidden), BF),
            ((count, hidden), BF),
        ],
        [pltpu.VMEM((count, width), BF)],
        flops=2 * count * width * (3 * cols + hidden + 4 * rank),
        exps=2 * count * hidden,
    )


def allowed_pairs(start, query_block, key_block):
    key_pos = key_block * BLOCK + lax.broadcasted_iota(jnp.int32, (BLOCK, BLOCK), 0)
    keep = key_pos >= start
    if key_block == query_block:
        query_pos = query_block * BLOCK + lax.broadcasted_iota(jnp.int32, (BLOCK, BLOCK), 1)
        keep = keep & (key_pos <= query_pos)
    return keep


def key_blocks(query_block):
    return range(max(0, query_block - MOST_DOC // BLOCK), query_block + 1)


def attend_forward(n, places_ref, start_ref, *rest):
    chunks, outs, log_ref = rest[:n], rest[n : 2 * n], rest[2 * n]
    qkv, mixed_all = rest[2 * n + 1 :]
    seq_len = start_ref.shape[1]
    count = seq_len // n
    heads = qkv.shape[1]
    for c in range(n):
        qkv[:, :, :, lanes(places_ref[c], count)] = chunks[c][...]

    def one_head(head, carry):
        queries, keys, values = qkv[0, head], qkv[1, head], qkv[2, head]
        keys_t = keys.T
        for i in range(seq_len // BLOCK):
            at = slice(i * BLOCK, (i + 1) * BLOCK)
            start = start_ref[:, at]
            scores = []
            for j in key_blocks(i):
                raw = mm(keys_t[j * BLOCK : (j + 1) * BLOCK], queries[:, at], 1, 0)
                scores.append(jnp.where(allowed_pairs(start, i, j), raw, MASKED))
            peak = jnp.max(scores[0], axis=0, keepdims=True)
            for block in scores[1:]:
                peak = jnp.maximum(peak, jnp.max(block, axis=0, keepdims=True))
            total, mixed = 0.0, 0.0
            for j, block in zip(key_blocks(i), scores):
                terms = jnp.exp(block - peak)
                total = total + jnp.sum(terms, axis=0, keepdims=True)
                mixed = mixed + mm(
                    values[:, j * BLOCK : (j + 1) * BLOCK], terms.astype(BF), 1, 0
                )
            mixed_all[head, :, at] = (mixed / total).astype(BF)
            log_ref[head, :, at] = peak + jnp.log(total)
        return carry

    lax.fori_loop(0, heads, one_head, 0)
    for c in range(n):
        outs[c][...] = mixed_all[:, :, lanes(places_ref[c], count)]


def attend_backward(n, places_ref, start_ref, cos_ref, sin_ref, log_ref, *rest):
    chunks, outs, grads, results = (rest[k * n : (k + 1) * n] for k in range(4))
    qkv, mixed_all, grad_all, result = rest[4 * n :]
    seq_len = start_ref.shape[1]
    count = seq_len // n
    heads = qkv.shape[1]
    for c in range(n):
        at = lanes(places_ref[c], count)
        qkv[:, :, :, at] = chunks[c][...]
        mixed_all[:, :, at] = outs[c][...]
        grad_all[:, :, at] = grads[c][...]
    cosine, sine = cos_ref[...], -sin_ref[...]
    blocks = seq_len // BLOCK

    def one_head(head, carry):
        queries, keys, values = qkv[0, head], qkv[1, head], qkv[2, head]
        grad = grad_all[head]
        inner = jnp.sum(
            grad.astype(F32) * mixed_all[head].astype(F32), axis=0, keepdims=True
        )
        keys_t, values_t = keys.T, values.T
        grad_keys, grad_values = [0.0] * blocks, [0.0] * blocks
        for i in range(blocks):
            at = slice(i * BLOCK, (i + 1) * BLOCK)
            start, log_total, inner_here = start_ref[:, at], log_ref[head, :, at], inner[:, at]
            query, grad_here = queries[:, at], grad[:, at]
            grad_query = 0.0
            for j in key_blocks(i):
                there = slice(j * BLOCK, (j + 1) * BLOCK)
                raw = mm(keys_t[there], query, 1, 0)
                terms = jnp.exp(jnp.where(allowed_pairs(start, i, j), raw, MASKED) - log_total)
                grad_terms = mm(values_t[there], grad_here, 1, 0)
                grad_scores = (terms * (grad_terms - inner_here)).astype(BF)
                grad_values[j] = grad_values[j] + mm(grad_here, terms.astype(BF), 1, 1)
                grad_keys[j] = grad_keys[j] + mm(query, grad_scores, 1, 1)
                grad_query = grad_query + mm(keys[:, there], grad_scores, 1, 0)
            grad_query = turn(grad_query * (HEAD_DIM**-0.5), cosine[:, at], sine[:, at])
            result[0, head, :, at] = grad_query.astype(BF)
        for j in range(blocks):
            there = slice(j * BLOCK, (j + 1) * BLOCK)
            result[1, head, :, there] = turn(
                grad_keys[j], cosine[:, there], sine[:, there]
            ).astype(BF)
            result[2, head, :, there] = grad_values[j].astype(BF)
        return carry

    lax.fori_loop(0, heads, one_head, 0)
    for c in range(n):
        results[c][...] = result[:, :, :, lanes(places_ref[c], count)]


def forward_attention(places, start, chunks):
    n = len(chunks)
    _, heads, _, count = chunks[0].shape
    seq_len = n * count
    pairs = heads * seq_len * seq_len // 2
    *outs, log_total = call(
        lambda *refs: attend_forward(n, *refs),
        [places, start, *chunks],
        [((heads, HEAD_DIM, count), BF)] * n + [((heads, 1, seq_len), F32)],
        [
            pltpu.VMEM((3, heads, HEAD_DIM, seq_len), BF),
            pltpu.VMEM((heads, HEAD_DIM, seq_len), BF),
        ],
        flops=pairs * 4 * HEAD_DIM * 4,
        exps=pairs,
        scalars=1,
    )
    return outs, log_total


def backward_attention(places, start, cosine, sine, log_total, chunks, outs, grads):
    n = len(chunks)
    _, heads, _, count = chunks[0].shape
    seq_len = n * count
    pairs = heads * seq_len * seq_len // 2
    return call(
        lambda *refs: attend_backward(n, *refs),
        [places, start, cosine, sine, log_total, *chunks, *outs, *grads],
        [((3, heads, HEAD_DIM, count), BF)] * n,
        [
            pltpu.VMEM((3, heads, HEAD_DIM, seq_len), BF),
            pltpu.VMEM((heads, HEAD_DIM, seq_len), BF),
            pltpu.VMEM((heads, HEAD_DIM, seq_len), BF),
            pltpu.VMEM((3, heads, HEAD_DIM, seq_len), BF),
        ],
        flops=pairs * 10 * HEAD_DIM * 4,
        exps=pairs,
        scalars=1,
    )


def out_kernel(
    mixed_ref, act_ref, out_full_ref, down_full_ref, out_first_ref, down_first_ref, *rest
):
    arrived_ref = rest[0] if len(rest) % 2 else None
    piece_ref, low_ref = rest[len(rest) % 2 :][:2]
    rank = out_first_ref.shape[1]
    cols, count = out_full_ref.shape[0], act_ref.shape[0]
    mixed = mixed_ref[...].reshape(cols, count)
    act = act_ref[...]
    total = mm(mixed, out_full_ref[...], 0, 0) + mm(act, down_full_ref[...], 1, 0)
    if arrived_ref is not None:
        total = total + arrived_ref[...].astype(F32)
    piece_ref[...] = total.astype(piece_ref.dtype)
    if len(rest) > 3:
        rest[-2][...] = total.astype(BF)
        rest[-1][...] = jnp.zeros(rest[-1].shape, BF)
    low_ref[:, :rank] = mm(mixed, out_first_ref[...], 0, 0).astype(BF)
    low_ref[:, rank:] = mm(act, down_first_ref[...], 1, 0).astype(BF)


def out_piece(
    mixed, act, out_full, down_full, out_first, down_first, dtype, arrived=None, both=False
):
    count, hidden = act.shape
    width, rank = out_full.shape[1], out_first.shape[1]
    operands = [mixed, act, out_full, down_full, out_first, down_first]
    return call(
        out_kernel,
        operands + ([] if arrived is None else [arrived]),
        [((count, width), dtype), ((count, 2 * rank), BF)]
        + ([((count, width), BF), ((8, 128), BF)] if both else []),
        flops=2 * count * (out_full.shape[0] + hidden) * width,
    )


def pull_kernel(
    g_ref,
    slope_ref,
    out_full_ref,
    down_ref,
    out_second_ref,
    down_second_ref,
    mixed_ref,
    low_ref,
    up_ref,
):
    grad = g_ref[...]
    mixed = mm(out_full_ref[...], grad, 1, 1)
    for head in range(mixed.shape[0] // HEAD_DIM):
        mixed_ref[head] = mixed[head * HEAD_DIM : (head + 1) * HEAD_DIM].astype(BF)
    rank = out_second_ref.shape[0]
    low_ref[:, :rank] = (ADAPTER_SCALE * mm(grad, out_second_ref[...], 1, 1)).astype(BF)
    low_ref[:, rank:] = (ADAPTER_SCALE * mm(grad, down_second_ref[...], 1, 1)).astype(BF)
    for begin in range(0, up_ref.shape[1], BLOCK):
        part = slice(begin, begin + BLOCK)
        up_ref[:, part] = (
            mm(grad, down_ref[part], 1, 1) * slope_ref[:, part].astype(F32)
        ).astype(BF)


def pull_back(grad, slope, out_full, down_full, out_second, down_second):
    count, width = grad.shape
    hidden, cols, twice = slope.shape[1], out_full.shape[0], 2 * out_second.shape[0]
    return call(
        pull_kernel,
        [grad, slope, out_full, down_full, out_second, down_second],
        [
            ((cols // HEAD_DIM, HEAD_DIM, count), BF),
            ((count, twice), BF),
            ((count, hidden), BF),
        ],
        flops=2 * count * width * (cols + hidden + twice),
    )


def slot_code(slot, bits):
    return sum(((slot >> b) & 1) << (bits - 1 - b) for b in range(bits))


def part_sizes(members):
    sizes = []
    while members > 1:
        members //= 2
        sizes.append(members)
    return sizes + [1]


def spread(me, members, fields, parts):
    bits = members.bit_length() - 1
    for size, part in zip(part_sizes(members), parts):
        for k in range(size):
            slot = k + (size if part is not parts[-1] else 0)
            owner = me ^ slot_code(slot, bits)
            low = 0
            for field in fields:
                rows = field.shape[0] // members
                at = pl.ds(pl.multiple_of(owner * rows, rows), rows)
                part[k, low : low + rows] = field[at]
                low += rows


def gather_spread(me, members, fields, parts):
    bits = members.bit_length() - 1
    for size, part in zip(part_sizes(members), parts):
        for k in range(size):
            slot = k + (size if part is not parts[-1] else 0)
            owner = me ^ slot_code(slot, bits)
            low = 0
            for field in fields:
                rows = field.shape[0] // members
                at = pl.ds(pl.multiple_of(owner * rows, rows), rows)
                field[at] = part[k, low : low + rows]
                low += rows


def early_kernel(chunks, packs, me_ref, up_second_ref, gain_ref, *rest):
    fields = 8
    more = rest[fields * chunks :]
    before, more = (more[:3], more[3:]) if packs != 1 else (None, more)
    if packs > 1:
        parts, more = more[: packs - 1], more[packs - 1 :]
        out_ref, shared_ref, split_ref = more
    else:
        shared_ref, split_ref, out_ref = more
    rank = up_second_ref.shape[0]
    shared_up, shared_out, up_b, down_a, out_a = 0.0, 0.0, 0.0, 0.0, 0.0
    for c in range(chunks):
        grad, grad_up, hat, act, low, low_out, grad_low, mixed = (
            ref[...] for ref in rest[c * fields : (c + 1) * fields]
        )
        mixed = mixed.reshape(-1, mixed.shape[-1])
        low_up_grad = (ADAPTER_SCALE * mm(grad_up, up_second_ref[...], 1, 1)).astype(BF)
        shared_up = shared_up + mm(low_up_grad, hat, 0, 0)
        shared_out = shared_out + mm(low_out, grad, 0, 0)
        up_b = up_b + mm(low[:, 3 * rank :], grad_up, 0, 0)
        down_a = down_a + mm(grad_low[:, rank:], act, 0, 0)
        out_a = out_a + mm(grad_low[:, :rank], mixed, 0, 1)
    shared_up = shared_up * gain_ref[...]
    shared_out = ADAPTER_SCALE * shared_out
    up_b = ADAPTER_SCALE * up_b
    if before is not None:
        shared_up = shared_up + before[0][:rank]
        shared_out = shared_out + before[0][rank:]
        up_b = up_b + before[1][:rank]
        down_a = down_a + before[1][rank:]
        out_a = out_a + before[2][...]
    shared_ref[:rank] = shared_up.astype(shared_ref.dtype)
    shared_ref[rank:] = shared_out.astype(shared_ref.dtype)
    split_ref[:rank] = up_b.astype(split_ref.dtype)
    split_ref[rank:] = down_a.astype(split_ref.dtype)
    out_ref[...] = out_a.astype(out_ref.dtype)
    if packs > 1:
        members = 1 << (packs - 2)
        spread(me_ref[0], members, (shared_ref, split_ref), parts)


def part_shapes(members, rows, width):
    return [((size, rows, width), BF) for size in part_sizes(members)]


def early_sums(me, items, up_second, gain, before=None, members=0):
    width, hidden, rank = items[0][0].shape[1], items[0][1].shape[1], up_second.shape[0]
    cols = items[0][7].shape[0] * HEAD_DIM
    sums = [((3 * rank, width), F32), ((2 * rank, hidden), F32), ((rank, cols), F32)]
    operands = [me, up_second, gain] + [array for item in items for array in item]
    scratch = []
    if before is None:
        packs, outputs = 1, sums
    elif not members:
        packs, outputs = 0, sums
    else:
        packs = members.bit_length() + 1
        outputs = part_shapes(members, 5 * rank // members, width) + [((rank, cols), BF)]
        scratch = [pltpu.VMEM((3 * rank, width), BF), pltpu.VMEM((2 * rank, hidden), BF)]
    return call(
        lambda *refs: early_kernel(len(items), packs, *refs),
        operands + ([] if before is None else list(before)),
        outputs,
        scratch,
        flops=2 * len(items) * items[0][0].shape[0] * rank * 6 * width,
        scalars=1,
    )


def in_kernel(grad_pre_ref, grad_up_ref, in_full_ref, up_full_ref, *rest):
    piece_ref = rest[-1]
    grad_pre = grad_pre_ref[...].reshape(in_full_ref.shape[1], grad_up_ref.shape[0])
    total = mm(grad_pre, in_full_ref[...], 0, 1) + mm(grad_up_ref[...], up_full_ref[...], 1, 1)
    if len(rest) > 1:
        total = total + rest[0][...].astype(F32)
    piece_ref[...] = total.astype(piece_ref.dtype)


def in_piece(grad_pre, grad_up, in_full, up_full, dtype, arrived=None):
    count, hidden = grad_up.shape
    width = up_full.shape[0]
    operands = [grad_pre, grad_up, in_full, up_full]
    (piece,) = call(
        in_kernel,
        operands + ([] if arrived is None else [arrived]),
        [((count, width), dtype)],
        flops=2 * count * (in_full.shape[1] + hidden) * width,
    )
    return piece


def late_kernel(chunks, packs, me_ref, second_ref, gain_ref, *rest):
    fields = 3
    more = rest[fields * chunks :]
    rank, cols = second_ref.shape[1], second_ref.shape[2]
    out_ref, more = more[0], more[1:]
    shared_ref, split_ref = more[-2:]

    def one_third(i, carry):
        shared, split = 0.0, 0.0
        for c in range(chunks):
            grad_pre, low, hat = rest[c * fields : (c + 1) * fields]
            part = grad_pre[i].reshape(cols, -1)
            low_grad = (ADAPTER_SCALE * mm(part, second_ref[i], 0, 1)).astype(BF)
            shared = shared + mm(low_grad, hat[...], 0, 0)
            split = split + mm(low[:, lanes(i, rank)], part, 0, 1)
        shared_ref[pl.ds(pl.multiple_of(i * rank, rank), rank)] = (
            shared * gain_ref[...]
        ).astype(BF)
        split_ref[:, lanes(i, cols)] = (ADAPTER_SCALE * split).astype(BF)
        return carry

    lax.fori_loop(0, 3, one_third, 0, unroll=True)
    split_ref[:, 3 * cols :] = out_ref[...].astype(BF)
    if packs:
        spread(me_ref[0], 1 << (packs - 1), (shared_ref, split_ref), more[:packs])


def late_sums(me, items, second, gain, out_a, members=0):
    width, rank, cols = items[0][2].shape[1], second.shape[1], second.shape[2]
    sums = [((3 * rank, width), BF), ((rank, 4 * cols), BF)]
    packs = members.bit_length() if members else 0
    return call(
        lambda *refs: late_kernel(len(items), packs, *refs),
        [me, second, gain] + [array for item in items for array in item] + [out_a],
        part_shapes(members, 4 * rank // members, width) if packs else sums,
        [pltpu.VMEM(*spec) for spec in sums] if packs else [],
        flops=2 * len(items) * items[0][1].shape[0] * rank * 3 * (width + 2 * cols),
        scalars=1,
    )


def early_unpack_kernel(packs, me_ref, *rest):
    parts = rest[:packs]
    up_a_ref, out_b_ref, down_b_ref, up_b_ref, down_a_ref, shared_ref, split_ref = rest[packs:]
    rank = out_b_ref.shape[0]
    gather_spread(me_ref[0], 1 << (packs - 1), (shared_ref, split_ref), parts)
    up_a_ref[...] = shared_ref[:rank].astype(F32).T
    out_b_ref[...] = shared_ref[rank : 2 * rank].astype(F32)
    down_b_ref[...] = shared_ref[2 * rank :].astype(F32)
    up_b_ref[...] = split_ref[:rank].astype(F32)
    down_a_ref[...] = split_ref[rank:].astype(F32).T


def late_unpack_kernel(packs, me_ref, *rest):
    parts = rest[:packs]
    a_ref, b_ref, out_a_ref, shared_ref, split_ref = rest[packs:]
    rank, cols = b_ref.shape[1], b_ref.shape[2]
    gather_spread(me_ref[0], 1 << (packs - 1), (shared_ref, split_ref), parts)
    for i in range(3):
        a_ref[i] = shared_ref[i * rank : (i + 1) * rank].astype(F32).T
        b_ref[i] = split_ref[:, i * cols : (i + 1) * cols].astype(F32)
    out_a_ref[...] = split_ref[:, 3 * cols :].astype(F32).T


def output_kernel(x_ref, own_ref, *rest):
    total = x_ref[...].astype(F32) + own_ref[...]
    for ref in rest[:-1]:
        total = total + ref[...].astype(F32)
    rest[-1][...] = total.astype(BF)


def input_grad_kernel(x_ref, g_ref, own_ref, *rest):
    total = own_ref[...]
    for ref in rest[:-1]:
        total = total + ref[...].astype(F32)
    hat, scale = normalize(x_ref[...])
    mean_grad = jnp.mean(total, axis=-1, keepdims=True)
    mean_cross = jnp.mean(total * hat, axis=-1, keepdims=True)
    rest[-1][...] = g_ref[...].astype(F32) + scale * (total - mean_grad - hat * mean_cross)


def add_kernel(left_ref, right_ref, sum_ref):
    sum_ref[...] = (left_ref[...].astype(F32) + right_ref[...].astype(F32)).astype(BF)


def added(left, right):
    return call(add_kernel, [left, right], [(left.shape, BF)])[0]


def fold_kernel(arrived_ref, *rest):
    parts, results = rest[: len(rest) // 2], rest[len(rest) // 2 :]
    for part, result in zip(parts, results):
        size = part.shape[0]
        low = size if part is not parts[-1] else 0
        result[...] = (
            part[...].astype(F32) + arrived_ref[low : low + size].astype(F32)
        ).astype(BF)


def close_kernel(shared_ref, arrived_ref, split_ref, both_ref):
    rows = shared_ref.shape[1]
    both_ref[:, :rows] = (
        shared_ref[...].astype(F32) + arrived_ref[...].astype(F32)
    ).astype(BF)
    both_ref[:, rows:] = split_ref[...]


def join_kernel(first_ref, second_ref, both_ref):
    size = first_ref.shape[0]
    both_ref[:size] = first_ref[...]
    both_ref[size:] = second_ref[...]


def swap_pairs(n):
    return [(i, i ^ 1) for i in range(n)]


def mirror_pairs(n):
    return [(i, n - 1 - i) for i in range(n)]


def together(*values):
    return lax.optimization_barrier(values)


def after(value, *earlier):
    return lax.optimization_barrier((value, earlier))[0]


def ring_scatter(piece, pieces):
    up = [(i, (i + 1) % pieces) for i in range(pieces)]
    running = piece(1, None)
    for k in range(2, pieces + 1):
        running = piece(k % pieces, lax.ppermute(running, "tensor", up))
    return running


class GroupSum:
    def __init__(self, parts, n_shared):
        self.parts, self.n_shared = list(parts), n_shared
        self.members, self.n = lax.axis_size("dp"), lax.axis_size("tensor")
        self.bits = len(self.parts) - 1
        self.steps = [("down", b) for b in range(self.bits)]
        jump = 1
        while jump < self.n:
            self.steps.append(("across", jump))
            jump *= 2
        self.steps += [("back", b) for b in reversed(range(self.bits))]
        self.moving, self.at, self.results = None, 0, []

    def start(self):
        kind, which = self.steps[self.at]
        if kind == "across":
            pairs = [(k, k ^ which) for k in range(self.n)]
            self.moving = lax.ppermute(self.shared, "tensor", pairs)
        else:
            pairs = [(k, k ^ (1 << which)) for k in range(self.members)]
            sent = self.parts[which] if kind == "down" else self.have
            self.moving = lax.ppermute(sent, "dp", pairs)

    def finish(self, *earlier):
        kind, which = self.steps[self.at]
        arrived = after(self.moving, *earlier) if earlier else self.moving
        if kind == "down":
            later = self.parts[which + 1 :]
            self.parts[which + 1 :] = call(
                fold_kernel, [arrived, *later], [(part.shape, BF) for part in later]
            )
            if which == self.bits - 1:
                own = self.parts[-1]
                self.shared, self.split = own[:, : self.n_shared], own[:, self.n_shared :]
            value = self.parts[-1]
        elif kind == "across":
            if self.steps[self.at + 1][0] == "back":
                (self.have,) = call(
                    close_kernel,
                    [self.shared, arrived, self.split],
                    [(self.parts[-1].shape, BF)],
                )
                self.results, value = [self.have], self.have
            else:
                self.shared = value = added(self.shared, arrived)
        else:
            self.results.append(arrived)
            value = arrived
            if which:
                rows = self.have.shape
                (self.have,) = call(
                    join_kernel, [self.have, arrived], [((2 * rows[0], *rows[1:]), BF)]
                )
                value = self.have
        self.at += 1
        return value

    def rest(self):
        while self.at < len(self.steps):
            self.start()
            self.finish()
        return self.results[::-1]


def slow_parts(me, shared, split, members):
    bits = members.bit_length() - 1
    width = shared.shape[1]
    both = jnp.concatenate(
        [
            shared.astype(BF).reshape(members, -1, width),
            split.astype(BF).reshape(members, -1, width),
        ],
        axis=1,
    )
    order = jnp.asarray([slot_code(slot, bits) for slot in range(members)], jnp.int32) ^ me
    both = both[order]
    parts, top = [], members
    for size in part_sizes(members)[:-1]:
        parts.append(both[size:top])
        top = size
    return parts + [both[:1]]


def slow_whole(me, parts, n_shared, members):
    bits = members.bit_length() - 1
    both = jnp.concatenate(parts[::-1], axis=0)
    order = jnp.asarray([slot_code(slot, bits) for slot in range(members)], jnp.int32)
    both = both[order[jnp.arange(members, dtype=jnp.int32) ^ me]].astype(F32)
    width = both.shape[-1]
    return both[:, :n_shared].reshape(-1, width), both[:, n_shared:].reshape(-1, width)


def normalize(inputs):
    values = inputs.astype(F32)
    center = values - jnp.mean(values, axis=-1, keepdims=True)
    inv_scale = lax.rsqrt(jnp.mean(center * center, axis=-1, keepdims=True) + EPSILON)
    return center * inv_scale, inv_scale


def whole_step(
    layer_input,
    document_lengths,
    attention_norm_gain,
    feedfwd_norm_gain,
    query_key_value_weight,
    output_weight,
    up_weight,
    down_weight,
    adapter_query_key_value_first,
    adapter_query_key_value_second,
    adapter_output_first,
    adapter_output_second,
    adapter_up_first,
    adapter_up_second,
    adapter_down_first,
    adapter_down_second,
    cotangent,
):
    own_x, own_g = layer_input[0], cotangent[0]
    shard_len, width = own_x.shape
    n = lax.axis_size("tensor")
    me = lax.axis_index("tensor")
    seq_len = shard_len * n
    rank = adapter_up_first.shape[1]
    cols = query_key_value_weight.shape[2]
    hidden = up_weight.shape[1]
    swap, mirror = swap_pairs(n), mirror_pairs(n)
    short = n == 4

    def send(value, pairs):
        return lax.ppermute(value, "tensor", pairs)

    members = lax.axis_size("dp")
    bits = members.bit_length() - 1
    tidy = short and hidden == width and 4 * cols == width and rank % (16 * members) == 0
    if short:
        owners = [me, me ^ 1, n - 1 - me, (n - 1 - me) ^ 1]
    else:
        owners = [lax.rem(me - k + n, n) for k in range(n)]
    places = jnp.stack(owners).astype(jnp.int32)
    me_dp = lax.axis_index("dp").astype(jnp.int32).reshape(1)
    places, me_dp, own_x = together(places, me_dp, own_x)
    turns = call(
        places_kernel,
        [places, document_lengths],
        [((1, seq_len), jnp.int32), ((HALF, seq_len), F32), ((HALF, seq_len), F32)]
        + [((HALF, shard_len), F32)] * (2 * n),
        scalars=2,
    )
    start, cosine, sine, turns = turns[0], turns[1], turns[2], turns[3:]
    gain_a, gain_m = attention_norm_gain[None], feedfwd_norm_gain[None]
    weights = (
        query_key_value_weight,
        adapter_query_key_value_first,
        adapter_query_key_value_second,
        adapter_up_first,
        up_weight,
        adapter_up_second,
    )

    def projected(k, rows):
        return project(rows, (gain_a, gain_m), (turns[k], turns[n + k]), weights)

    def merged():
        return merge_weights(
            query_key_value_weight,
            up_weight,
            output_weight,
            down_weight,
            (adapter_query_key_value_first, adapter_query_key_value_second),
            (adapter_up_first, adapter_up_second),
            (adapter_output_first, adapter_output_second),
            (adapter_down_first, adapter_down_second),
            gain_a,
            gain_m,
        )

    outward, inward, middle = [(0, 1), (3, 2)], [(1, 0), (2, 3)], [(1, 2), (2, 1)]
    if short:
        x_near, x_facing = send(own_x, swap), send(own_x, mirror)
        full = merged()
        first = projected(0, own_x)
        x_near, x_facing, first, full, own_g = together(x_near, x_facing, first, full, own_g)
        x_far = send(x_facing, swap)
        g_near, g_mid = send(own_g, swap), send(own_g, middle)
        state = [first, projected(1, x_near), projected(2, x_facing)]
        x_far, state = together(x_far, state)
        state = state + [projected(3, x_far)]
    else:
        full = merged()
        up_ring = [(i, (i + 1) % n) for i in range(n)]
        state, moving = [projected(0, own_x)], own_x
        for k in range(1, n):
            moving = send(moving, up_ring)
            state.append(projected(k, moving))
    in_full, up_full, out_full, down_full = full
    qkv, low, hat, act, slope = (list(field) for field in zip(*state))
    mixed, log_total = forward_attention(places, start, qkv)
    low_out = [None] * n

    def out_part(k, dtype, arrived=None, both=False):
        piece, low_out[k], *more = out_piece(
            mixed[k],
            act[k],
            out_full,
            down_full,
            adapter_output_first,
            adapter_down_first,
            dtype,
            arrived,
            both,
        )
        return (piece, more[0]) if both else piece

    def pulled(k, grad):
        return pull_back(
            grad,
            slope[k],
            out_full,
            down_full,
            adapter_output_second,
            adapter_down_second,
        )

    def early_item(k, grad, back):
        return (grad, back[2], hat[k], act[k], low[k], low_out[k], back[1], mixed[k])

    if short:
        y_facing, y_facing_low = out_part(2, F32, both=True)
        y_far, y_far_low = out_part(3, F32, both=True)
        y_1, y_2 = send(y_facing_low, outward), send(y_far_low, outward)
        g_near, g_mid = after((g_near, g_mid), y_facing, y_far)
        g_mid_far, g_end_far = send(g_near, middle), send(g_mid, inward)
        y_near, y_own = out_part(1, F32), out_part(0, F32)
        backs = [pulled(0, own_g), pulled(1, g_near)]
        g_mid_far, g_end_far = after((g_mid_far, g_end_far), backs, y_near, y_own)
        g_end = send(g_mid_far, inward)
        g_far = added(g_mid_far, g_end_far)
        y_3 = send(added(y_far, after(y_1, g_far)), middle)
        backs = backs + [None, pulled(3, g_far)]
        all_g = [own_g, g_near, None, g_far]
        before = early_sums(
            me_dp,
            [early_item(k, all_g[k], backs[k]) for k in (0, 1, 3)],
            adapter_up_second,
            gain_m,
        )
        y_5 = send(added(y_facing, after(y_2, before)), middle)
        g_end = after(g_end, before)
        g_facing = added(g_mid, g_end)
        backs[2] = pulled(2, g_facing)
        early = early_sums(
            me_dp,
            [early_item(2, g_facing, backs[2])],
            adapter_up_second,
            gain_m,
            before,
            members if tidy else 0,
        )
        y_near = added(y_near, after(y_3, early))
        y_4 = send(y_near, swap)
    else:
        y_own = ring_scatter(lambda k, arrived: out_part(k, BF if k else F32, arrived), n)
        backs, moving, all_g = [pulled(0, own_g)], own_g, [own_g]
        for k in range(1, n):
            moving = send(moving, up_ring)
            all_g.append(moving)
            backs.append(pulled(k, moving))
        early = early_sums(
            me_dp, [early_item(k, all_g[k], backs[k]) for k in range(n)], adapter_up_second, gain_m
        )

    *early, out_a = early
    if not tidy:
        early = slow_parts(me_dp[0], early[0], early[1].reshape(-1, width), members)
    early = GroupSum(early, 3 * rank // members)
    early.start()
    grads_mixed = [back[0] for back in backs]
    if short:
        last = early.finish()
        early.start()
        grads_mixed = after(grads_mixed, y_near, last)
    grad_pre = backward_attention(places, start, cosine, sine, log_total, qkv, mixed, grads_mixed)

    def in_part(k, dtype, arrived=None, last=None):
        pre = grad_pre[k] if last is None else after(grad_pre[k], last)
        return in_piece(pre, backs[k][2], in_full, up_full, dtype, arrived)

    def early_whole(parts):
        if not tidy:
            early_a, early_b = slow_whole(me_dp[0], parts, 3 * rank // members, members)
            early_b = early_b.reshape(2 * rank, hidden)
            return (
                early_a[:rank].T,
                early_a[rank : 2 * rank],
                early_a[2 * rank :],
                early_b[:rank],
                early_b[rank:].T,
            )
        return call(
            lambda *refs: early_unpack_kernel(bits + 1, *refs),
            [me_dp, *parts],
            [
                ((width, rank), F32),
                ((rank, width), F32),
                ((rank, width), F32),
                ((rank, hidden), F32),
                ((hidden, rank), F32),
            ],
            [pltpu.VMEM((3 * rank, width), BF), pltpu.VMEM((2 * rank, width), BF)],
            scalars=1,
        )

    def late_parts():
        late = late_sums(
            me_dp,
            [(grad_pre[k], low[k], hat[k]) for k in range(n)],
            adapter_query_key_value_second,
            gain_a,
            out_a,
            members if tidy else 0,
        )
        if not tidy:
            late = slow_parts(me_dp[0], late[0], late[1].reshape(-1, width), members)
        return GroupSum(late, 3 * rank // members)

    if short:
        last = early.finish(grad_pre)
        early.start()
        late = late_parts()
        late.start()
        dx_far = in_part(3, BF)
        last = late.finish(dx_far)
        late.start()
        last = early.finish(last)
        early.start()
        dx_swap = send(dx_far, swap)
        dx_near, dx_own = in_part(1, BF, last=last), in_part(0, F32, last=last)
        last = early.finish(dx_near, dx_own)
        early.start()
        last = late.finish(last)
        late.start()
        dx_facing = in_part(2, BF, after(dx_swap, last))
        last = late.finish(dx_facing)
        late.start()
        last = early.finish(last)
        early.start()
        last = late.finish(last)
        late.start()
        dx_a = send(dx_near, swap)
        dx_b = send(dx_facing, mirror)
        last = early.finish(last)
        early.start()
        (layer_output,) = call(
            output_kernel,
            [own_x, y_own, *after((y_4, y_5), last)],
            [((shard_len, width), BF)],
        )
        last = late.finish(last, layer_output)
        late.start()
        last = early.finish(last)
        early.start()
        last = late.finish(last)
        late.start()
        early.finish(last)
        early_done = early_whole(early.rest())
        last = late.finish(early_done)
        late.start()
        dx_parts = [dx_own, *after((dx_a, dx_b), last)]
    else:
        (layer_output,) = call(output_kernel, [own_x, y_own], [((shard_len, width), BF)])
        dx_parts = [
            ring_scatter(lambda k, arrived: in_part(k, BF if k else F32, arrived), n)
        ]
        early.finish()
        late = late_parts()
        early_done = early_whole(early.rest())
    (grad_in,) = call(
        input_grad_kernel, [own_x, own_g, *dx_parts], [((shard_len, width), F32)]
    )

    up_a, out_b, down_b, up_b, down_a = early_done
    late = late.rest()
    if tidy:
        a_qkv, b_qkv, out_a = call(
            lambda *refs: late_unpack_kernel(bits + 1, *refs),
            [me_dp, *late],
            [((3, width, rank), F32), ((3, rank, cols), F32), ((cols, rank), F32)],
            [pltpu.VMEM((3 * rank, width), BF), pltpu.VMEM((rank, width), BF)],
            scalars=1,
        )
    else:
        late_a, late_b = slow_whole(me_dp[0], late, 3 * rank // members, members)
        late_b = late_b.reshape(rank, 4 * cols)
        a_qkv = jnp.swapaxes(late_a.reshape(3, rank, width), 1, 2)
        b_qkv = jnp.stack([late_b[:, i * cols : (i + 1) * cols] for i in range(3)])
        out_a = late_b[:, 3 * cols :].T
    return (
        layer_output[None],
        grad_in[None],
        a_qkv,
        b_qkv,
        out_a,
        out_b,
        up_a,
        up_b,
        down_a,
        down_b,
    )


def solution(mesh):
    in_specs = (
        P("dp", "tensor", None),
        P("dp", None),
        P(),
        P(),
        P(None, None, "tensor"),
        P("tensor", None),
        P(None, "tensor"),
        P("tensor", None),
        P(),
        P(None, None, "tensor"),
        P("tensor", None),
        P(),
        P(),
        P(None, "tensor"),
        P("tensor", None),
        P(),
        P("dp", "tensor", None),
    )
    out_specs = (
        P("dp", "tensor", None),
        P("dp", "tensor", None),
        P(),
        P(None, None, "tensor"),
        P("tensor", None),
        P(),
        P(),
        P(None, "tensor"),
        P("tensor", None),
        P(),
    )
    return jax.shard_map(
        whole_step, mesh=mesh, in_specs=in_specs, out_specs=out_specs, check_vma=False
    )
```

```python
import math

import jax
import jax.numpy as jnp
from jax import lax
from jax.experimental import pallas as pl
from jax.experimental.pallas import tpu as pltpu
from jax.sharding import PartitionSpec as P

HEAD_DIM = 64
ROT = 16
HALF = ROT // 2
BLOCK = 256
MOST_DOC = 512

EPSILON = 1e-05
ADAPTER_SCALE = 0.25
MASKED = -1e30
VMEM_GRANT = 12 << 20
BF = jnp.bfloat16
F32 = jnp.float32


def mm(left, right, left_dim, right_dim):
    return lax.dot_general(
        left, right, (((left_dim,), (right_dim,)), ((), ())), preferred_element_type=F32
    )


def call(kernel, operands, outputs, scratch=(), flops=0, exps=0, scalars=0):
    spaces = [pltpu.SMEM] * scalars + [pltpu.VMEM] * (len(operands) - scalars)
    moved = sum(math.prod(s) * jnp.dtype(d).itemsize for s, d in outputs)
    return pl.pallas_call(
        kernel,
        in_specs=[pl.BlockSpec(memory_space=space) for space in spaces],
        out_specs=[pl.BlockSpec(memory_space=pltpu.VMEM) for _ in outputs],
        out_shape=[jax.ShapeDtypeStruct(s, d) for s, d in outputs],
        scratch_shapes=list(scratch),
        compiler_params=pltpu.CompilerParams(vmem_limit_bytes=VMEM_GRANT),
        cost_estimate=pl.CostEstimate(
            flops=flops, bytes_accessed=2 * moved, transcendentals=exps
        ),
    )(*operands)


def places_kernel(places_ref, lengths_ref, start_ref, cos_ref, sin_ref, *shards):
    count, seq_len = lengths_ref.shape[1], start_ref.shape[1]
    pos = lax.broadcasted_iota(jnp.int32, (HALF, seq_len), 1)
    start, end = jnp.zeros((HALF, seq_len), jnp.int32), jnp.int32(0)
    for j in range(count):
        end = end + lengths_ref[0, j]
        start = jnp.where(pos >= end, end, start)
    start_ref[...] = start[:1]
    row = lax.broadcasted_iota(jnp.int32, (HALF, seq_len), 0).astype(F32)
    inverse = jnp.exp(row * (-2.0 * math.log(10000.0) / ROT))
    angles = (pos - start).astype(F32) * inverse
    cos_ref[...] = jnp.cos(angles)
    sin_ref[...] = jnp.sin(angles)
    n = len(shards) // 2
    for k in range(n):
        at = lanes(places_ref[k], seq_len // n)
        shards[k][...] = cos_ref[:, at]
        shards[n + k][...] = sin_ref[:, at]


def turn(value, cosine, sine):
    lead, tail = value[:HALF], value[HALF:ROT]
    return jnp.concatenate(
        [lead * cosine - tail * sine, tail * cosine + lead * sine, value[ROT:]], axis=0
    )


def lanes(place, count):
    return pl.ds(pl.multiple_of(place * count, 128), count)


def merge_kernel(
    qkv_ref,
    qkv_first_ref,
    qkv_second_ref,
    up_ref,
    up_first_ref,
    up_second_ref,
    out_ref,
    out_first_ref,
    out_second_ref,
    down_ref,
    down_first_ref,
    down_second_ref,
    gain_a_ref,
    gain_m_ref,
    in_full_ref,
    up_full_ref,
    out_full_ref,
    down_full_ref,
):
    cols = qkv_ref.shape[2]

    def joined(weight, first, second):
        return weight.astype(F32) + ADAPTER_SCALE * mm(first, second, 1, 0)

    def column(row):
        return jnp.broadcast_to(row, (128, row.shape[1])).T

    def times(value, tall):
        return jnp.concatenate(
            [value[:, k : k + 128] * tall for k in range(0, value.shape[1], 128)], axis=1
        )

    gain_a, gain_m = column(gain_a_ref[...]), column(gain_m_ref[...])

    for i in range(3):
        in_full_ref[:, i * cols : (i + 1) * cols] = times(
            joined(qkv_ref[i], qkv_first_ref[i], qkv_second_ref[i]), gain_a
        ).astype(BF)
    up_full_ref[...] = times(
        joined(up_ref[...], up_first_ref[...], up_second_ref[...]), gain_m
    ).astype(BF)
    out_full_ref[...] = joined(out_ref[...], out_first_ref[...], out_second_ref[...]).astype(BF)
    down_full_ref[...] = joined(down_ref[...], down_first_ref[...], down_second_ref[...]).astype(
        BF
    )


def merge_weights(qkv, up, out, down, qkv_ab, up_ab, out_ab, down_ab, gain_a, gain_m):
    steps = 4
    width, cols = qkv.shape[1], qkv.shape[2]
    hidden, rank = up.shape[1], up_ab[0].shape[1]
    rows, out_rows, down_rows = width // steps, cols // steps, hidden // steps

    def fixed(shape):
        return pl.BlockSpec(shape, lambda s: (0,) * len(shape))

    def moving(shape):
        return pl.BlockSpec(shape, lambda s: (s,) + (0,) * (len(shape) - 1))

    def middle(shape):
        return pl.BlockSpec(shape, lambda s: (0, s, 0))

    return pl.pallas_call(
        merge_kernel,
        grid=(steps,),
        in_specs=[
            middle((3, rows, cols)),
            middle((3, rows, rank)),
            fixed((3, rank, cols)),
            moving((rows, hidden)),
            moving((rows, rank)),
            fixed((rank, hidden)),
            moving((out_rows, width)),
            moving((out_rows, rank)),
            fixed((rank, width)),
            moving((down_rows, width)),
            moving((down_rows, rank)),
            fixed((rank, width)),
            pl.BlockSpec((1, rows), lambda s: (0, s)),
            pl.BlockSpec((1, rows), lambda s: (0, s)),
        ],
        out_specs=[
            moving((rows, 3 * cols)),
            moving((rows, hidden)),
            moving((out_rows, width)),
            moving((down_rows, width)),
        ],
        out_shape=[
            jax.ShapeDtypeStruct((width, 3 * cols), BF),
            jax.ShapeDtypeStruct((width, hidden), BF),
            jax.ShapeDtypeStruct((cols, width), BF),
            jax.ShapeDtypeStruct((hidden, width), BF),
        ],
        compiler_params=pltpu.CompilerParams(vmem_limit_bytes=VMEM_GRANT),
        cost_estimate=pl.CostEstimate(
            flops=2 * rank * width * (4 * cols + 2 * hidden),
            bytes_accessed=4 * width * (4 * cols + 2 * hidden),
            transcendentals=0,
        ),
    )(
        qkv,
        qkv_ab[0],
        qkv_ab[1],
        up,
        up_ab[0],
        up_ab[1],
        out,
        out_ab[0],
        out_ab[1],
        down,
        down_ab[0],
        down_ab[1],
        gain_a,
        gain_m,
    )


def project_kernel(
    x_ref,
    gain_a_ref,
    gain_m_ref,
    cos_ref,
    sin_ref,
    qkv_weight_ref,
    qkv_first_ref,
    qkv_second_ref,
    up_first_ref,
    up_ref,
    up_second_ref,
    qkv_ref,
    low_ref,
    hat_ref,
    act_ref,
    slope_ref,
    mlp_ref,
):
    rank = up_first_ref.shape[1]
    cols = qkv_weight_ref.shape[2]
    values = x_ref[...].astype(F32)
    center = values - jnp.mean(values, axis=-1, keepdims=True)
    hat = center * lax.rsqrt(jnp.mean(center * center, axis=-1, keepdims=True) + EPSILON)
    hat_ref[...] = hat.astype(BF)
    attn_in = (hat * gain_a_ref[...]).astype(BF)
    feed_in = (hat * gain_m_ref[...]).astype(BF)
    cosine, sine = cos_ref[...], sin_ref[...]

    def one_third(i, carry):
        low = mm(attn_in, qkv_first_ref[i], 1, 0).astype(BF)
        low_ref[:, lanes(i, rank)] = low
        pre = mm(attn_in, qkv_weight_ref[i], 1, 0) + ADAPTER_SCALE * mm(
            low, qkv_second_ref[i], 1, 0
        )
        pre = pre.T
        turned = (i < 2).astype(F32)
        scale = jnp.where(i == 0, HEAD_DIM**-0.5, 1.0)
        cos_here = 1.0 + turned * (cosine - 1.0)
        sin_here = turned * sine
        for head in range(cols // HEAD_DIM):
            rows = turn(pre[head * HEAD_DIM : (head + 1) * HEAD_DIM], cos_here, sin_here)
            qkv_ref[i, head] = (rows * scale).astype(BF)
        return carry

    lax.fori_loop(0, 3, one_third, 0)
    low = mm(feed_in, up_first_ref[...], 1, 0).astype(BF)
    low_ref[:, 3 * rank :] = low
    mlp_ref[...] = feed_in

    def one_block(k, carry):
        part = lanes(k, BLOCK)
        pre = mm(mlp_ref[...], up_ref[:, part], 1, 0) + ADAPTER_SCALE * mm(
            low, up_second_ref[:, part], 1, 0
        )
        cdf = 0.5 * (1.0 + lax.erf(pre * (2.0**-0.5)))
        act_ref[:, part] = (pre * cdf).astype(BF)
        slope_ref[:, part] = (
            cdf + pre * (jnp.exp(-0.5 * pre * pre) * (1.0 / math.sqrt(2.0 * math.pi)))
        ).astype(BF)
        return carry

    lax.fori_loop(0, up_ref.shape[1] // BLOCK, one_block, 0)


def project(rows, gains, turns, weights):
    count, width = rows.shape
    cols, hidden, rank = weights[0].shape[2], weights[4].shape[1], weights[3].shape[1]
    return call(
        project_kernel,
        [rows, *gains, *turns, *weights],
        [
            ((3, cols // HEAD_DIM, HEAD_DIM, count), BF),
            ((count, 4 * rank), BF),
            ((count, width), BF),
            ((count, hidden), BF),
            ((count, hidden), BF),
        ],
        [pltpu.VMEM((count, width), BF)],
        flops=2 * count * width * (3 * cols + hidden + 4 * rank),
        exps=2 * count * hidden,
    )


def allowed_pairs(start, query_block, key_block):
    key_pos = key_block * BLOCK + lax.broadcasted_iota(jnp.int32, (BLOCK, BLOCK), 0)
    keep = key_pos >= start
    if key_block == query_block:
        query_pos = query_block * BLOCK + lax.broadcasted_iota(jnp.int32, (BLOCK, BLOCK), 1)
        keep = keep & (key_pos <= query_pos)
    return keep


def key_blocks(query_block):
    return range(max(0, query_block - MOST_DOC // BLOCK), query_block + 1)


def attend_forward(n, places_ref, start_ref, *rest):
    chunks, outs, log_ref = rest[:n], rest[n : 2 * n], rest[2 * n]
    qkv, mixed_all = rest[2 * n + 1 :]
    seq_len = start_ref.shape[1]
    count = seq_len // n
    heads = qkv.shape[1]
    for c in range(n):
        qkv[:, :, :, lanes(places_ref[c], count)] = chunks[c][...]

    def one_head(head, carry):
        queries, keys, values = qkv[0, head], qkv[1, head], qkv[2, head]
        keys_t = keys.T
        for i in range(seq_len // BLOCK):
            at = slice(i * BLOCK, (i + 1) * BLOCK)
            start = start_ref[:, at]
            scores = []
            for j in key_blocks(i):
                raw = mm(keys_t[j * BLOCK : (j + 1) * BLOCK], queries[:, at], 1, 0)
                scores.append(jnp.where(allowed_pairs(start, i, j), raw, MASKED))
            peak = jnp.max(scores[0], axis=0, keepdims=True)
            for block in scores[1:]:
                peak = jnp.maximum(peak, jnp.max(block, axis=0, keepdims=True))
            total, mixed = 0.0, 0.0
            for j, block in zip(key_blocks(i), scores):
                terms = jnp.exp(block - peak)
                total = total + jnp.sum(terms, axis=0, keepdims=True)
                mixed = mixed + mm(
                    values[:, j * BLOCK : (j + 1) * BLOCK], terms.astype(BF), 1, 0
                )
            mixed_all[head, :, at] = (mixed / total).astype(BF)
            log_ref[head, :, at] = peak + jnp.log(total)
        return carry

    lax.fori_loop(0, heads, one_head, 0)
    for c in range(n):
        outs[c][...] = mixed_all[:, :, lanes(places_ref[c], count)]


def attend_backward(n, first, places_ref, start_ref, cos_ref, sin_ref, log_ref, *rest):
    chunks, outs, grads, results = (rest[k * n : (k + 1) * n] for k in range(4))
    qkv, mixed_all, grad_all, result = rest[4 * n :]
    seq_len = start_ref.shape[1]
    count = seq_len // n
    heads = qkv.shape[1]
    mine = slice(first, first + heads)
    for c in range(n):
        at = lanes(places_ref[c], count)
        qkv[:, :, :, at] = chunks[c][:, mine]
        mixed_all[:, :, at] = outs[c][mine]
        grad_all[:, :, at] = grads[c][mine]
    cosine, sine = cos_ref[...], -sin_ref[...]
    blocks = seq_len // BLOCK

    def one_head(head, carry):
        queries, keys, values = qkv[0, head], qkv[1, head], qkv[2, head]
        grad = grad_all[head]
        inner = jnp.sum(
            grad.astype(F32) * mixed_all[head].astype(F32), axis=0, keepdims=True
        )
        keys_t, values_t = keys.T, values.T
        grad_keys, grad_values = [0.0] * blocks, [0.0] * blocks
        for i in range(blocks):
            at = slice(i * BLOCK, (i + 1) * BLOCK)
            start, log_total, inner_here = (
                start_ref[:, at],
                log_ref[first + head, :, at],
                inner[:, at],
            )
            query, grad_here = queries[:, at], grad[:, at]
            grad_query = 0.0
            for j in key_blocks(i):
                there = slice(j * BLOCK, (j + 1) * BLOCK)
                raw = mm(keys_t[there], query, 1, 0)
                terms = jnp.exp(jnp.where(allowed_pairs(start, i, j), raw, MASKED) - log_total)
                grad_terms = mm(values_t[there], grad_here, 1, 0)
                grad_scores = (terms * (grad_terms - inner_here)).astype(BF)
                grad_values[j] = grad_values[j] + mm(grad_here, terms.astype(BF), 1, 1)
                grad_keys[j] = grad_keys[j] + mm(query, grad_scores, 1, 1)
                grad_query = grad_query + mm(keys[:, there], grad_scores, 1, 0)
            grad_query = turn(grad_query * (HEAD_DIM**-0.5), cosine[:, at], sine[:, at])
            result[0, head, :, at] = grad_query.astype(BF)
        for j in range(blocks):
            there = slice(j * BLOCK, (j + 1) * BLOCK)
            result[1, head, :, there] = turn(
                grad_keys[j], cosine[:, there], sine[:, there]
            ).astype(BF)
            result[2, head, :, there] = grad_values[j].astype(BF)
        return carry

    lax.fori_loop(0, heads, one_head, 0)
    for c in range(n):
        results[c][...] = result[:, :, :, lanes(places_ref[c], count)]


def forward_attention(places, start, chunks):
    n = len(chunks)
    _, heads, _, count = chunks[0].shape
    seq_len = n * count
    pairs = heads * seq_len * seq_len // 2
    *outs, log_total = call(
        lambda *refs: attend_forward(n, *refs),
        [places, start, *chunks],
        [((heads, HEAD_DIM, count), BF)] * n + [((heads, 1, seq_len), F32)],
        [
            pltpu.VMEM((3, heads, HEAD_DIM, seq_len), BF),
            pltpu.VMEM((heads, HEAD_DIM, seq_len), BF),
        ],
        flops=pairs * 4 * HEAD_DIM * 4,
        exps=pairs,
        scalars=1,
    )
    return outs, log_total


def backward_attention(part, places, start, cosine, sine, log_total, chunks, outs, grads):
    n = len(chunks)
    _, heads, _, count = chunks[0].shape
    heads = heads // 2
    first = part * heads
    seq_len = n * count
    pairs = heads * seq_len * seq_len // 2
    return call(
        lambda *refs: attend_backward(n, first, *refs),
        [places, start, cosine, sine, log_total, *chunks, *outs, *grads],
        [((3, heads, HEAD_DIM, count), BF)] * n,
        [
            pltpu.VMEM((3, heads, HEAD_DIM, seq_len), BF),
            pltpu.VMEM((heads, HEAD_DIM, seq_len), BF),
            pltpu.VMEM((heads, HEAD_DIM, seq_len), BF),
            pltpu.VMEM((3, heads, HEAD_DIM, seq_len), BF),
        ],
        flops=pairs * 10 * HEAD_DIM * 4,
        exps=pairs,
        scalars=1,
    )


def out_kernel(
    mixed_ref, act_ref, out_full_ref, down_full_ref, out_first_ref, down_first_ref, *rest
):
    arrived_ref = rest[0] if len(rest) % 2 else None
    piece_ref, low_ref = rest[len(rest) % 2 :][:2]
    rank = out_first_ref.shape[1]
    cols, count = out_full_ref.shape[0], act_ref.shape[0]
    mixed = mixed_ref[...].reshape(cols, count)
    act = act_ref[...]
    total = mm(mixed, out_full_ref[...], 0, 0) + mm(act, down_full_ref[...], 1, 0)
    if arrived_ref is not None:
        total = total + arrived_ref[...].astype(F32)
    piece_ref[...] = total.astype(piece_ref.dtype)
    if len(rest) > 3:
        rest[-2][...] = total.astype(BF)
        rest[-1][...] = jnp.zeros(rest[-1].shape, BF)
    low_ref[:, :rank] = mm(mixed, out_first_ref[...], 0, 0).astype(BF)
    low_ref[:, rank:] = mm(act, down_first_ref[...], 1, 0).astype(BF)


def out_piece(
    mixed, act, out_full, down_full, out_first, down_first, dtype, arrived=None, both=False
):
    count, hidden = act.shape
    width, rank = out_full.shape[1], out_first.shape[1]
    operands = [mixed, act, out_full, down_full, out_first, down_first]
    return call(
        out_kernel,
        operands + ([] if arrived is None else [arrived]),
        [((count, width), dtype), ((count, 2 * rank), BF)]
        + ([((count, width), BF), ((8, 128), BF)] if both else []),
        flops=2 * count * (out_full.shape[0] + hidden) * width,
    )


def pull_kernel(
    g_ref,
    slope_ref,
    out_full_ref,
    down_ref,
    out_second_ref,
    down_second_ref,
    mixed_ref,
    low_ref,
    up_ref,
):
    grad = g_ref[...]
    mixed = mm(out_full_ref[...], grad, 1, 1)
    for head in range(mixed.shape[0] // HEAD_DIM):
        mixed_ref[head] = mixed[head * HEAD_DIM : (head + 1) * HEAD_DIM].astype(BF)
    rank = out_second_ref.shape[0]
    low_ref[:, :rank] = (ADAPTER_SCALE * mm(grad, out_second_ref[...], 1, 1)).astype(BF)
    low_ref[:, rank:] = (ADAPTER_SCALE * mm(grad, down_second_ref[...], 1, 1)).astype(BF)
    for begin in range(0, up_ref.shape[1], BLOCK):
        part = slice(begin, begin + BLOCK)
        up_ref[:, part] = (
            mm(grad, down_ref[part], 1, 1) * slope_ref[:, part].astype(F32)
        ).astype(BF)


def pull_back(grad, slope, out_full, down_full, out_second, down_second):
    count, width = grad.shape
    hidden, cols, twice = slope.shape[1], out_full.shape[0], 2 * out_second.shape[0]
    return call(
        pull_kernel,
        [grad, slope, out_full, down_full, out_second, down_second],
        [
            ((cols // HEAD_DIM, HEAD_DIM, count), BF),
            ((count, twice), BF),
            ((count, hidden), BF),
        ],
        flops=2 * count * width * (cols + hidden + twice),
    )


def slot_code(slot, bits):
    return sum(((slot >> b) & 1) << (bits - 1 - b) for b in range(bits))


def part_slots(members):
    halves = []
    while members > 4:
        members //= 2
        halves.append((members, members))
    return halves + [(slot, 1) for slot in range(members - 1, -1, -1)]


def move_slices(me, members, fields, parts, inward):
    bits = members.bit_length() - 1
    for (first, size), part in zip(part_slots(members), parts):
        for k in range(size):
            owner = me ^ slot_code(first + k, bits)
            low = 0
            for field in fields:
                rows = field.shape[0] // members
                at = pl.ds(pl.multiple_of(owner * rows, rows), rows)
                if inward:
                    part[k, low : low + rows] = field[at]
                else:
                    field[at] = part[k, low : low + rows]
                low += rows


def spread(me, members, fields, parts):
    move_slices(me, members, fields, parts, True)


def gather_spread(me, members, fields, parts):
    move_slices(me, members, fields, parts, False)


def early_kernel(chunks, packs, me_ref, up_second_ref, gain_ref, *rest):
    fields = 8
    more = rest[fields * chunks :]
    before, more = (more[:3], more[3:]) if packs != 1 else (None, more)
    if packs > 1:
        count = len(part_slots(packs))
        parts, more = more[:count], more[count:]
        out_ref, shared_ref, split_ref = more
    else:
        shared_ref, split_ref, out_ref = more
    rank = up_second_ref.shape[0]
    shared_up, shared_out, up_b, down_a, out_a = 0.0, 0.0, 0.0, 0.0, 0.0
    for c in range(chunks):
        grad, grad_up, hat, act, low, low_out, grad_low, mixed = (
            ref[...] for ref in rest[c * fields : (c + 1) * fields]
        )
        mixed = mixed.reshape(-1, mixed.shape[-1])
        low_up_grad = (ADAPTER_SCALE * mm(grad_up, up_second_ref[...], 1, 1)).astype(BF)
        shared_up = shared_up + mm(low_up_grad, hat, 0, 0)
        shared_out = shared_out + mm(low_out, grad, 0, 0)
        up_b = up_b + mm(low[:, 3 * rank :], grad_up, 0, 0)
        down_a = down_a + mm(grad_low[:, rank:], act, 0, 0)
        out_a = out_a + mm(grad_low[:, :rank], mixed, 0, 1)
    shared_up = shared_up * gain_ref[...]
    shared_out = ADAPTER_SCALE * shared_out
    up_b = ADAPTER_SCALE * up_b
    if before is not None:
        shared_up = shared_up + before[0][:rank]
        shared_out = shared_out + before[0][rank:]
        up_b = up_b + before[1][:rank]
        down_a = down_a + before[1][rank:]
        out_a = out_a + before[2][...]
    shared_ref[:rank] = shared_up.astype(shared_ref.dtype)
    shared_ref[rank:] = shared_out.astype(shared_ref.dtype)
    split_ref[:rank] = up_b.astype(split_ref.dtype)
    split_ref[rank:] = down_a.astype(split_ref.dtype)
    out_ref[...] = out_a.astype(out_ref.dtype)
    if packs > 1:
        spread(me_ref[0], packs, (shared_ref, split_ref), parts)


def part_shapes(members, rows, width):
    return [((size, rows, width), BF) for _, size in part_slots(members)]


def early_sums(me, items, up_second, gain, before=None, members=0):
    width, hidden, rank = items[0][0].shape[1], items[0][1].shape[1], up_second.shape[0]
    cols = items[0][7].shape[0] * HEAD_DIM
    sums = [((3 * rank, width), F32), ((2 * rank, hidden), F32), ((rank, cols), F32)]
    operands = [me, up_second, gain] + [array for item in items for array in item]
    scratch = []
    if before is None:
        packs, outputs = 1, sums
    elif not members:
        packs, outputs = 0, sums
    else:
        packs = members
        outputs = part_shapes(members, 5 * rank // members, width) + [((rank, cols), BF)]
        scratch = [pltpu.VMEM((3 * rank, width), BF), pltpu.VMEM((2 * rank, hidden), BF)]
    return call(
        lambda *refs: early_kernel(len(items), packs, *refs),
        operands + ([] if before is None else list(before)),
        outputs,
        scratch,
        flops=2 * len(items) * items[0][0].shape[0] * rank * 6 * width,
        scalars=1,
    )


def all_heads(first, second):
    return jnp.concatenate(
        [half.reshape(-1, half.shape[-1]) for half in (first, second)], axis=0
    )


def in_kernel(first_ref, second_ref, grad_up_ref, in_full_ref, up_full_ref, *rest):
    piece_ref = rest[-1]
    grad_pre = jnp.concatenate(
        [all_heads(first_ref[i], second_ref[i]) for i in range(3)], axis=0
    )
    total = mm(grad_pre, in_full_ref[...], 0, 1) + mm(grad_up_ref[...], up_full_ref[...], 1, 1)
    if len(rest) > 1:
        total = total + rest[0][...].astype(F32)
    piece_ref[...] = total.astype(piece_ref.dtype)


def in_piece(grad_pre, grad_up, in_full, up_full, dtype, arrived=None):
    count, hidden = grad_up.shape
    width = up_full.shape[0]
    operands = [*grad_pre, grad_up, in_full, up_full]
    (piece,) = call(
        in_kernel,
        operands + ([] if arrived is None else [arrived]),
        [((count, width), dtype)],
        flops=2 * count * (in_full.shape[1] + hidden) * width,
    )
    return piece


def late_kernel(chunks, packs, me_ref, second_ref, gain_ref, *rest):
    fields = 4
    more = rest[fields * chunks :]
    rank, cols = second_ref.shape[1], second_ref.shape[2]
    out_ref, more = more[0], more[1:]
    shared_ref, split_ref = more[-2:]

    def one_third(i, carry):
        shared, split = 0.0, 0.0
        for c in range(chunks):
            grad_first, grad_second, low, hat = rest[c * fields : (c + 1) * fields]
            part = all_heads(grad_first[i], grad_second[i])
            low_grad = (ADAPTER_SCALE * mm(part, second_ref[i], 0, 1)).astype(BF)
            shared = shared + mm(low_grad, hat[...], 0, 0)
            split = split + mm(low[:, lanes(i, rank)], part, 0, 1)
        shared_ref[pl.ds(pl.multiple_of(i * rank, rank), rank)] = (
            shared * gain_ref[...]
        ).astype(BF)
        split_ref[:, lanes(i, cols)] = (ADAPTER_SCALE * split).astype(BF)
        return carry

    lax.fori_loop(0, 3, one_third, 0, unroll=True)
    split_ref[:, 3 * cols :] = out_ref[...].astype(BF)
    if packs:
        spread(me_ref[0], packs, (shared_ref, split_ref), more[: len(part_slots(packs))])


def late_sums(me, items, second, gain, out_a, members=0):
    width, rank, cols = items[0][3].shape[1], second.shape[1], second.shape[2]
    sums = [((3 * rank, width), BF), ((rank, 4 * cols), BF)]
    packs = members
    return call(
        lambda *refs: late_kernel(len(items), packs, *refs),
        [me, second, gain] + [array for item in items for array in item] + [out_a],
        part_shapes(members, 4 * rank // members, width) if packs else sums,
        [pltpu.VMEM(*spec) for spec in sums] if packs else [],
        flops=2 * len(items) * items[0][2].shape[0] * rank * 3 * (width + 2 * cols),
        scalars=1,
    )


def early_unpack_kernel(packs, me_ref, *rest):
    count = len(part_slots(packs))
    parts = rest[:count]
    up_a_ref, out_b_ref, down_b_ref, up_b_ref, down_a_ref, shared_ref, split_ref = rest[count:]
    rank = out_b_ref.shape[0]
    gather_spread(me_ref[0], packs, (shared_ref, split_ref), parts)
    up_a_ref[...] = shared_ref[:rank].astype(F32).T
    out_b_ref[...] = shared_ref[rank : 2 * rank].astype(F32)
    down_b_ref[...] = shared_ref[2 * rank :].astype(F32)
    up_b_ref[...] = split_ref[:rank].astype(F32)
    down_a_ref[...] = split_ref[rank:].astype(F32).T


def late_unpack_kernel(packs, me_ref, *rest):
    count = len(part_slots(packs))
    parts = rest[:count]
    a_ref, b_ref, out_a_ref, shared_ref, split_ref = rest[count:]
    rank, cols = b_ref.shape[1], b_ref.shape[2]
    gather_spread(me_ref[0], packs, (shared_ref, split_ref), parts)
    for i in range(3):
        a_ref[i] = shared_ref[i * rank : (i + 1) * rank].astype(F32).T
        b_ref[i] = split_ref[:, i * cols : (i + 1) * cols].astype(F32)
    out_a_ref[...] = split_ref[:, 3 * cols :].astype(F32).T


def output_kernel(x_ref, own_ref, *rest):
    total = x_ref[...].astype(F32) + own_ref[...]
    for ref in rest[:-1]:
        total = total + ref[...].astype(F32)
    rest[-1][...] = total.astype(BF)


def input_grad_kernel(x_ref, g_ref, own_ref, *rest):
    total = own_ref[...]
    for ref in rest[:-1]:
        total = total + ref[...].astype(F32)
    hat, scale = normalize(x_ref[...])
    mean_grad = jnp.mean(total, axis=-1, keepdims=True)
    mean_cross = jnp.mean(total * hat, axis=-1, keepdims=True)
    rest[-1][...] = g_ref[...].astype(F32) + scale * (total - mean_grad - hat * mean_cross)


def add_kernel(left_ref, right_ref, sum_ref):
    sum_ref[...] = (left_ref[...].astype(F32) + right_ref[...].astype(F32)).astype(BF)


def added(left, right):
    return call(add_kernel, [left, right], [(left.shape, BF)])[0]


def fold_kernel(firsts, arrived_ref, *rest):
    parts, results = rest[: len(rest) // 2], rest[len(rest) // 2 :]
    for first, part, result in zip(firsts, parts, results):
        result[...] = (
            part[...].astype(F32) + arrived_ref[first : first + part.shape[0]].astype(F32)
        ).astype(BF)


def meet_kernel(count, *refs):
    total = refs[0][...].astype(F32)
    for ref in refs[1:count]:
        total = total + ref[...].astype(F32)
    shared_ref, split_ref = refs[count:]
    rows = shared_ref.shape[1]
    shared_ref[...] = total[:, :rows].astype(BF)
    split_ref[...] = total[:, rows:].astype(BF)


def close_kernel(shared_ref, arrived_ref, split_ref, both_ref):
    rows = shared_ref.shape[1]
    both_ref[:, :rows] = (
        shared_ref[...].astype(F32) + arrived_ref[...].astype(F32)
    ).astype(BF)
    both_ref[:, rows:] = split_ref[...]


def join_kernel(*refs):
    low = 0
    for ref in refs[:-1]:
        refs[-1][low : low + ref.shape[0]] = ref[...]
        low += ref.shape[0]


def swap_pairs(n):
    return [(i, i ^ 1) for i in range(n)]


def mirror_pairs(n):
    return [(i, n - 1 - i) for i in range(n)]


def together(*values):
    return lax.optimization_barrier(values)


def after(value, *earlier):
    return lax.optimization_barrier((value, earlier))[0]


def ring_scatter(piece, pieces):
    up = [(i, (i + 1) % pieces) for i in range(pieces)]
    running = piece(1, None)
    for k in range(2, pieces + 1):
        running = piece(k % pieces, lax.ppermute(running, "tensor", up))
    return running


class GroupSum:
    def __init__(self, parts, n_shared):
        self.parts, self.n_shared = list(parts), n_shared
        self.members, self.n = lax.axis_size("dp"), lax.axis_size("tensor")
        self.bits = self.members.bit_length() - 1
        self.slots = part_slots(self.members)
        halves = self.bits - 2
        self.steps = [("down", b) for b in range(halves)] + [("meet", 0)]
        jump = 1
        while jump < self.n:
            self.steps.append(("across", jump))
            jump *= 2
        self.steps += [("part", 0)] + [("back", b) for b in reversed(range(halves))]
        self.moving, self.at, self.results = None, 0, []

    def hop(self, value, code):
        pairs = [(k, k ^ code) for k in range(self.members)]
        return lax.ppermute(value, "dp", pairs)

    def start(self):
        kind, which = self.steps[self.at]
        codes = [slot_code(slot, self.bits) for slot in (1, 2, 3)]
        if kind == "across":
            pairs = [(k, k ^ which) for k in range(self.n)]
            self.moving = lax.ppermute(self.shared, "tensor", pairs)
        elif kind == "down":
            self.moving = self.hop(self.parts[which], 1 << which)
        elif kind == "meet":
            self.moving = [
                self.hop(self.parts[-1 - slot], code) for slot, code in zip((1, 2, 3), codes)
            ]
        elif kind == "part":
            self.moving = [self.hop(self.have, code) for code in codes]
        else:
            self.moving = self.hop(self.have, 1 << which)

    def finish(self, *earlier):
        kind, which = self.steps[self.at]
        arrived = after(self.moving, *earlier) if earlier else self.moving
        if kind == "down":
            later = self.parts[which + 1 :]
            firsts = [first for first, _ in self.slots[which + 1 :]]
            self.parts[which + 1 :] = call(
                lambda *refs: fold_kernel(firsts, *refs),
                [arrived, *later],
                [(part.shape, BF) for part in later],
            )
            value = self.parts[-1]
        elif kind == "meet":
            _, rows, width = self.parts[-1].shape
            self.shared, self.split = call(
                lambda *refs: meet_kernel(4, *refs),
                [self.parts[-1], *arrived],
                [((1, self.n_shared, width), BF), ((1, rows - self.n_shared, width), BF)],
            )
            value = self.shared
        elif kind == "across":
            if self.steps[self.at + 1][0] == "part":
                (self.have,) = call(
                    close_kernel,
                    [self.shared, arrived, self.split],
                    [(self.parts[-1].shape, BF)],
                )
                value = self.have
            else:
                self.shared = value = added(self.shared, arrived)
        else:
            pieces = list(arrived) if kind == "part" else [arrived]
            self.results = self.results or [self.have]
            self.results += pieces
            value = pieces[0]
            if self.at + 1 < len(self.steps):
                _, *rows = self.have.shape
                total = sum(piece.shape[0] for piece in [self.have, *pieces])
                (self.have,) = call(
                    join_kernel, [self.have, *pieces], [((total, *rows), BF)]
                )
                value = self.have
        self.at += 1
        return value

    def rest(self):
        while self.at < len(self.steps):
            self.start()
            self.finish()
        return self.results[::-1]


def slow_parts(me, shared, split, members):
    bits = members.bit_length() - 1
    width = shared.shape[1]
    both = jnp.concatenate(
        [
            shared.astype(BF).reshape(members, -1, width),
            split.astype(BF).reshape(members, -1, width),
        ],
        axis=1,
    )
    order = jnp.asarray([slot_code(slot, bits) for slot in range(members)], jnp.int32) ^ me
    both = both[order]
    return [both[first : first + size] for first, size in part_slots(members)]


def slow_whole(me, parts, n_shared, members):
    bits = members.bit_length() - 1
    both = jnp.concatenate(parts[::-1], axis=0)
    order = jnp.asarray([slot_code(slot, bits) for slot in range(members)], jnp.int32)
    both = both[order[jnp.arange(members, dtype=jnp.int32) ^ me]].astype(F32)
    width = both.shape[-1]
    return both[:, :n_shared].reshape(-1, width), both[:, n_shared:].reshape(-1, width)


def normalize(inputs):
    values = inputs.astype(F32)
    center = values - jnp.mean(values, axis=-1, keepdims=True)
    inv_scale = lax.rsqrt(jnp.mean(center * center, axis=-1, keepdims=True) + EPSILON)
    return center * inv_scale, inv_scale


def whole_step(
    layer_input,
    document_lengths,
    attention_norm_gain,
    feedfwd_norm_gain,
    query_key_value_weight,
    output_weight,
    up_weight,
    down_weight,
    adapter_query_key_value_first,
    adapter_query_key_value_second,
    adapter_output_first,
    adapter_output_second,
    adapter_up_first,
    adapter_up_second,
    adapter_down_first,
    adapter_down_second,
    cotangent,
):
    own_x, own_g = layer_input[0], cotangent[0]
    shard_len, width = own_x.shape
    n = lax.axis_size("tensor")
    me = lax.axis_index("tensor")
    seq_len = shard_len * n
    rank = adapter_up_first.shape[1]
    cols = query_key_value_weight.shape[2]
    hidden = up_weight.shape[1]
    swap, mirror = swap_pairs(n), mirror_pairs(n)
    short = n == 4

    def send(value, pairs):
        return lax.ppermute(value, "tensor", pairs)

    members = lax.axis_size("dp")
    tidy = short and hidden == width and 4 * cols == width and rank % (16 * members) == 0
    if short:
        owners = [me, me ^ 1, n - 1 - me, (n - 1 - me) ^ 1]
    else:
        owners = [lax.rem(me - k + n, n) for k in range(n)]
    places = jnp.stack(owners).astype(jnp.int32)
    me_dp = lax.axis_index("dp").astype(jnp.int32).reshape(1)
    places, me_dp, own_x = together(places, me_dp, own_x)
    turns = call(
        places_kernel,
        [places, document_lengths],
        [((1, seq_len), jnp.int32), ((HALF, seq_len), F32), ((HALF, seq_len), F32)]
        + [((HALF, shard_len), F32)] * (2 * n),
        scalars=2,
    )
    start, cosine, sine, turns = turns[0], turns[1], turns[2], turns[3:]
    gain_a, gain_m = attention_norm_gain[None], feedfwd_norm_gain[None]
    weights = (
        query_key_value_weight,
        adapter_query_key_value_first,
        adapter_query_key_value_second,
        adapter_up_first,
        up_weight,
        adapter_up_second,
    )

    def projected(k, rows):
        return project(rows, (gain_a, gain_m), (turns[k], turns[n + k]), weights)

    def merged():
        return merge_weights(
            query_key_value_weight,
            up_weight,
            output_weight,
            down_weight,
            (adapter_query_key_value_first, adapter_query_key_value_second),
            (adapter_up_first, adapter_up_second),
            (adapter_output_first, adapter_output_second),
            (adapter_down_first, adapter_down_second),
            gain_a,
            gain_m,
        )

    outward, inward, middle = [(0, 1), (3, 2)], [(1, 0), (2, 3)], [(1, 2), (2, 1)]
    if short:
        x_near, x_facing = send(own_x, swap), send(own_x, mirror)
        full = merged()
        first = projected(0, own_x)
        x_near, x_facing, first, full, own_g = together(x_near, x_facing, first, full, own_g)
        x_far = send(x_facing, swap)
        g_near, g_mid = send(own_g, swap), send(own_g, middle)
        state = [first, projected(1, x_near), projected(2, x_facing)]
        x_far, state = together(x_far, state)
        state = state + [projected(3, x_far)]
    else:
        full = merged()
        up_ring = [(i, (i + 1) % n) for i in range(n)]
        state, moving = [projected(0, own_x)], own_x
        for k in range(1, n):
            moving = send(moving, up_ring)
            state.append(projected(k, moving))
    in_full, up_full, out_full, down_full = full
    qkv, low, hat, act, slope = (list(field) for field in zip(*state))
    mixed, log_total = forward_attention(places, start, qkv)
    low_out = [None] * n

    def out_part(k, dtype, last=None, arrived=None, both=False):
        rows = mixed[k] if last is None else after(mixed[k], last)
        piece, low_out[k], *more = out_piece(
            rows,
            act[k],
            out_full,
            down_full,
            adapter_output_first,
            adapter_down_first,
            dtype,
            arrived,
            both,
        )
        return (piece, more[0]) if both else piece

    def pulled(k, grad):
        return pull_back(
            grad,
            slope[k],
            out_full,
            down_full,
            adapter_output_second,
            adapter_down_second,
        )

    def early_item(k, grad, back):
        return (grad, back[2], hat[k], act[k], low[k], low_out[k], back[1], mixed[k])

    if short:
        y_facing, y_facing_low = out_part(2, F32, both=True)
        y_far, y_far_low = out_part(3, F32, both=True)
        y_1, y_2 = send(y_facing_low, outward), send(y_far_low, outward)
        g_near, g_mid = after((g_near, g_mid), mixed)
        g_mid_far, g_end_far = send(g_near, middle), send(g_mid, inward)
        backs = [pulled(0, own_g)]
        g_mid_far, g_end_far = after((g_mid_far, g_end_far), y_far, backs)
        g_end = send(g_mid_far, inward)
        g_far = added(g_mid_far, g_end_far)
        backs.append(pulled(1, after(g_near, g_far)))
        y_near, y_own = out_part(1, F32, g_far), out_part(0, F32, g_far)
        pulled_far = pulled(3, g_far)
        y_3 = send(added(y_far, after(y_1, backs, y_near, y_own, pulled_far)), middle)
        backs = backs + [None, pulled_far]
        all_g = [own_g, g_near, None, g_far]
        before = early_sums(
            me_dp,
            [early_item(k, all_g[k], backs[k]) for k in (0, 1, 3)],
            adapter_up_second,
            gain_m,
        )
        y_5 = send(added(y_facing, after(y_2, before)), middle)
        g_end = after(g_end, before)
        g_facing = added(g_mid, g_end)
        backs[2] = pulled(2, g_facing)
        early = early_sums(
            me_dp,
            [early_item(2, g_facing, backs[2])],
            adapter_up_second,
            gain_m,
            before,
            members if tidy else 0,
        )
    else:
        y_own = ring_scatter(
            lambda k, arrived: out_part(k, BF if k else F32, arrived=arrived), n
        )
        backs, moving, all_g = [pulled(0, own_g)], own_g, [own_g]
        for k in range(1, n):
            moving = send(moving, up_ring)
            all_g.append(moving)
            backs.append(pulled(k, moving))
        early = early_sums(
            me_dp, [early_item(k, all_g[k], backs[k]) for k in range(n)], adapter_up_second, gain_m
        )

    *early, out_a = early
    if not tidy:
        early = slow_parts(me_dp[0], early[0], early[1].reshape(-1, width), members)
    early = GroupSum(early, 3 * rank // members)
    early.start()
    grads_mixed = [back[0] for back in backs]
    if short:
        last = early.finish()
        early.start()
        grads_mixed = after(grads_mixed, last)
    halves = []
    for part in range(2):
        halves.append(
            backward_attention(
                part, places, start, cosine, sine, log_total, qkv, mixed, grads_mixed
            )
        )
        if short and not part:
            y_near = added(y_near, after(y_3, halves[0]))
            y_4 = send(y_near, swap)
            grads_mixed = after(grads_mixed, y_near)
    grad_pre = list(zip(*halves))

    def in_part(k, dtype, arrived=None, last=None):
        pre = grad_pre[k] if last is None else after(grad_pre[k], last)
        return in_piece(pre, backs[k][2], in_full, up_full, dtype, arrived)

    def early_whole(parts):
        if not tidy:
            early_a, early_b = slow_whole(me_dp[0], parts, 3 * rank // members, members)
            early_b = early_b.reshape(2 * rank, hidden)
            return (
                early_a[:rank].T,
                early_a[rank : 2 * rank],
                early_a[2 * rank :],
                early_b[:rank],
                early_b[rank:].T,
            )
        return call(
            lambda *refs: early_unpack_kernel(members, *refs),
            [me_dp, *parts],
            [
                ((width, rank), F32),
                ((rank, width), F32),
                ((rank, width), F32),
                ((rank, hidden), F32),
                ((hidden, rank), F32),
            ],
            [pltpu.VMEM((3 * rank, width), BF), pltpu.VMEM((2 * rank, width), BF)],
            scalars=1,
        )

    def late_parts():
        late = late_sums(
            me_dp,
            [(*grad_pre[k], low[k], hat[k]) for k in range(n)],
            adapter_query_key_value_second,
            gain_a,
            out_a,
            members if tidy else 0,
        )
        if not tidy:
            late = slow_parts(me_dp[0], late[0], late[1].reshape(-1, width), members)
        return GroupSum(late, 3 * rank // members)

    if short:
        last = early.finish(grad_pre)
        early.start()
        late = late_parts()
        late.start()
        dx_far = in_part(3, BF)
        last = early.finish(dx_far)
        early.start()
        dx_swap = send(dx_far, swap)
        last = late.finish(last)
        late.start()
        dx_near = in_part(1, BF, last=last)
        last = early.finish(dx_near)
        early.start()
        last = late.finish(last)
        late.start()
        dx_own = in_part(0, F32, last=last)
        dx_facing = in_part(2, BF, after(dx_swap, dx_own))
        last = late.finish(dx_facing)
        late.start()
        dx_a = send(dx_near, swap)
        dx_b = send(dx_facing, mirror)
        last = early.finish(last)
        early.start()
        (layer_output,) = call(
            output_kernel,
            [own_x, y_own, *after((y_4, y_5), last)],
            [((shard_len, width), BF)],
        )
        last = late.finish(last, layer_output)
        late.start()
        early.finish(last)
        early_done = early_whole(early.rest())
        last = late.finish(early_done)
        late.start()
        dx_parts = [dx_own, dx_a, dx_b]
    else:
        (layer_output,) = call(output_kernel, [own_x, y_own], [((shard_len, width), BF)])
        dx_parts = [
            ring_scatter(lambda k, arrived: in_part(k, BF if k else F32, arrived), n)
        ]
        early.finish()
        late = late_parts()
        early_done = early_whole(early.rest())
    up_a, out_b, down_b, up_b, down_a = early_done
    late = late.rest()
    if tidy:
        a_qkv, b_qkv, out_a = call(
            lambda *refs: late_unpack_kernel(members, *refs),
            [me_dp, *late],
            [((3, width, rank), F32), ((3, rank, cols), F32), ((cols, rank), F32)],
            [pltpu.VMEM((3 * rank, width), BF), pltpu.VMEM((rank, width), BF)],
            scalars=1,
        )
    else:
        late_a, late_b = slow_whole(me_dp[0], late, 3 * rank // members, members)
        late_b = late_b.reshape(rank, 4 * cols)
        a_qkv = jnp.swapaxes(late_a.reshape(3, rank, width), 1, 2)
        b_qkv = jnp.stack([late_b[:, i * cols : (i + 1) * cols] for i in range(3)])
        out_a = late_b[:, 3 * cols :].T
    dx_parts = [dx_parts[0], *after(dx_parts[1:], a_qkv)]
    (grad_in,) = call(
        input_grad_kernel, [own_x, own_g, *dx_parts], [((shard_len, width), F32)]
    )
    return (
        layer_output[None],
        grad_in[None],
        a_qkv,
        b_qkv,
        out_a,
        out_b,
        up_a,
        up_b,
        down_a,
        down_b,
    )


def solution(mesh):
    in_specs = (
        P("dp", "tensor", None),
        P("dp", None),
        P(),
        P(),
        P(None, None, "tensor"),
        P("tensor", None),
        P(None, "tensor"),
        P("tensor", None),
        P(),
        P(None, None, "tensor"),
        P("tensor", None),
        P(),
        P(),
        P(None, "tensor"),
        P("tensor", None),
        P(),
        P("dp", "tensor", None),
    )
    out_specs = (
        P("dp", "tensor", None),
        P("dp", "tensor", None),
        P(),
        P(None, None, "tensor"),
        P("tensor", None),
        P(),
        P(),
        P(None, "tensor"),
        P("tensor", None),
        P(),
    )
    return jax.shard_map(
        whole_step, mesh=mesh, in_specs=in_specs, out_specs=out_specs, check_vma=False
    )
```

```python
import math

import jax
import jax.numpy as jnp
from jax import lax
from jax.experimental import pallas as pl
from jax.experimental.pallas import tpu as pltpu
from jax.sharding import PartitionSpec as P

HEAD_DIM = 64
ROT = 16
HALF = ROT // 2
BLOCK = 256
MOST_DOC = 512

EPSILON = 1e-05
ADAPTER_SCALE = 0.25
MASKED = -1e30
VMEM_GRANT = 12 << 20
BF = jnp.bfloat16
F32 = jnp.float32


def mm(left, right, left_dim, right_dim):
    return lax.dot_general(
        left, right, (((left_dim,), (right_dim,)), ((), ())), preferred_element_type=F32
    )


def call(kernel, operands, outputs, scratch=(), flops=0, exps=0, scalars=0):
    spaces = [pltpu.SMEM] * scalars + [pltpu.VMEM] * (len(operands) - scalars)
    moved = sum(math.prod(s) * jnp.dtype(d).itemsize for s, d in outputs)
    return pl.pallas_call(
        kernel,
        in_specs=[pl.BlockSpec(memory_space=space) for space in spaces],
        out_specs=[pl.BlockSpec(memory_space=pltpu.VMEM) for _ in outputs],
        out_shape=[jax.ShapeDtypeStruct(s, d) for s, d in outputs],
        scratch_shapes=list(scratch),
        compiler_params=pltpu.CompilerParams(vmem_limit_bytes=VMEM_GRANT),
        cost_estimate=pl.CostEstimate(
            flops=flops, bytes_accessed=2 * moved, transcendentals=exps
        ),
    )(*operands)


def places_kernel(places_ref, lengths_ref, start_ref, cos_ref, sin_ref, *shards):
    count, seq_len = lengths_ref.shape[1], start_ref.shape[1]
    pos = lax.broadcasted_iota(jnp.int32, (HALF, seq_len), 1)
    start, end = jnp.zeros((HALF, seq_len), jnp.int32), jnp.int32(0)
    for j in range(count):
        end = end + lengths_ref[0, j]
        start = jnp.where(pos >= end, end, start)
    start_ref[...] = start[:1]
    row = lax.broadcasted_iota(jnp.int32, (HALF, seq_len), 0).astype(F32)
    inverse = jnp.exp(row * (-2.0 * math.log(10000.0) / ROT))
    angles = (pos - start).astype(F32) * inverse
    cos_ref[...] = jnp.cos(angles)
    sin_ref[...] = jnp.sin(angles)
    n = len(shards) // 2
    for k in range(n):
        at = lanes(places_ref[k], seq_len // n)
        shards[k][...] = cos_ref[:, at]
        shards[n + k][...] = sin_ref[:, at]


def turn(value, cosine, sine):
    lead, tail = value[:HALF], value[HALF:ROT]
    return jnp.concatenate(
        [lead * cosine - tail * sine, tail * cosine + lead * sine, value[ROT:]], axis=0
    )


def lanes(place, count):
    return pl.ds(pl.multiple_of(place * count, 128), count)


def merge_kernel(
    qkv_ref,
    qkv_first_ref,
    qkv_second_ref,
    up_ref,
    up_first_ref,
    up_second_ref,
    out_ref,
    out_first_ref,
    out_second_ref,
    down_ref,
    down_first_ref,
    down_second_ref,
    gain_a_ref,
    gain_m_ref,
    in_full_ref,
    up_full_ref,
    out_full_ref,
    down_full_ref,
):
    cols = qkv_ref.shape[2]

    def joined(weight, first, second):
        return weight.astype(F32) + ADAPTER_SCALE * mm(first, second, 1, 0)

    def column(row):
        return jnp.broadcast_to(row, (128, row.shape[1])).T

    def times(value, tall):
        return jnp.concatenate(
            [value[:, k : k + 128] * tall for k in range(0, value.shape[1], 128)], axis=1
        )

    gain_a, gain_m = column(gain_a_ref[...]), column(gain_m_ref[...])

    for i in range(3):
        in_full_ref[:, i * cols : (i + 1) * cols] = times(
            joined(qkv_ref[i], qkv_first_ref[i], qkv_second_ref[i]), gain_a
        ).astype(BF)
    up_full_ref[...] = times(
        joined(up_ref[...], up_first_ref[...], up_second_ref[...]), gain_m
    ).astype(BF)
    out_full_ref[...] = joined(out_ref[...], out_first_ref[...], out_second_ref[...]).astype(BF)
    down_full_ref[...] = joined(down_ref[...], down_first_ref[...], down_second_ref[...]).astype(
        BF
    )


def merge_weights(qkv, up, out, down, qkv_ab, up_ab, out_ab, down_ab, gain_a, gain_m):
    steps = 4
    width, cols = qkv.shape[1], qkv.shape[2]
    hidden, rank = up.shape[1], up_ab[0].shape[1]
    rows, out_rows, down_rows = width // steps, cols // steps, hidden // steps

    def fixed(shape):
        return pl.BlockSpec(shape, lambda s: (0,) * len(shape))

    def moving(shape):
        return pl.BlockSpec(shape, lambda s: (s,) + (0,) * (len(shape) - 1))

    def middle(shape):
        return pl.BlockSpec(shape, lambda s: (0, s, 0))

    return pl.pallas_call(
        merge_kernel,
        grid=(steps,),
        in_specs=[
            middle((3, rows, cols)),
            middle((3, rows, rank)),
            fixed((3, rank, cols)),
            moving((rows, hidden)),
            moving((rows, rank)),
            fixed((rank, hidden)),
            moving((out_rows, width)),
            moving((out_rows, rank)),
            fixed((rank, width)),
            moving((down_rows, width)),
            moving((down_rows, rank)),
            fixed((rank, width)),
            pl.BlockSpec((1, rows), lambda s: (0, s)),
            pl.BlockSpec((1, rows), lambda s: (0, s)),
        ],
        out_specs=[
            moving((rows, 3 * cols)),
            moving((rows, hidden)),
            moving((out_rows, width)),
            moving((down_rows, width)),
        ],
        out_shape=[
            jax.ShapeDtypeStruct((width, 3 * cols), BF),
            jax.ShapeDtypeStruct((width, hidden), BF),
            jax.ShapeDtypeStruct((cols, width), BF),
            jax.ShapeDtypeStruct((hidden, width), BF),
        ],
        compiler_params=pltpu.CompilerParams(vmem_limit_bytes=VMEM_GRANT),
        cost_estimate=pl.CostEstimate(
            flops=2 * rank * width * (4 * cols + 2 * hidden),
            bytes_accessed=4 * width * (4 * cols + 2 * hidden),
            transcendentals=0,
        ),
    )(
        qkv,
        qkv_ab[0],
        qkv_ab[1],
        up,
        up_ab[0],
        up_ab[1],
        out,
        out_ab[0],
        out_ab[1],
        down,
        down_ab[0],
        down_ab[1],
        gain_a,
        gain_m,
    )


def project_kernel(
    x_ref,
    gain_a_ref,
    gain_m_ref,
    cos_ref,
    sin_ref,
    qkv_weight_ref,
    qkv_first_ref,
    qkv_second_ref,
    up_first_ref,
    up_ref,
    up_second_ref,
    qkv_ref,
    low_ref,
    hat_ref,
    act_ref,
    slope_ref,
    mlp_ref,
):
    rank = up_first_ref.shape[1]
    cols = qkv_weight_ref.shape[2]
    values = x_ref[...].astype(F32)
    center = values - jnp.mean(values, axis=-1, keepdims=True)
    hat = center * lax.rsqrt(jnp.mean(center * center, axis=-1, keepdims=True) + EPSILON)
    hat_ref[...] = hat.astype(BF)
    attn_in = (hat * gain_a_ref[...]).astype(BF)
    feed_in = (hat * gain_m_ref[...]).astype(BF)
    cosine, sine = cos_ref[...], sin_ref[...]

    def one_third(i, carry):
        low = mm(attn_in, qkv_first_ref[i], 1, 0).astype(BF)
        low_ref[:, lanes(i, rank)] = low
        pre = mm(attn_in, qkv_weight_ref[i], 1, 0) + ADAPTER_SCALE * mm(
            low, qkv_second_ref[i], 1, 0
        )
        pre = pre.T
        turned = (i < 2).astype(F32)
        scale = jnp.where(i == 0, HEAD_DIM**-0.5, 1.0)
        cos_here = 1.0 + turned * (cosine - 1.0)
        sin_here = turned * sine
        for head in range(cols // HEAD_DIM):
            rows = turn(pre[head * HEAD_DIM : (head + 1) * HEAD_DIM], cos_here, sin_here)
            qkv_ref[i, head] = (rows * scale).astype(BF)
        return carry

    lax.fori_loop(0, 3, one_third, 0)
    low = mm(feed_in, up_first_ref[...], 1, 0).astype(BF)
    low_ref[:, 3 * rank :] = low
    mlp_ref[...] = feed_in

    def one_block(k, carry):
        part = lanes(k, BLOCK)
        pre = mm(mlp_ref[...], up_ref[:, part], 1, 0) + ADAPTER_SCALE * mm(
            low, up_second_ref[:, part], 1, 0
        )
        cdf = 0.5 * (1.0 + lax.erf(pre * (2.0**-0.5)))
        act_ref[:, part] = (pre * cdf).astype(BF)
        slope_ref[:, part] = (
            cdf + pre * (jnp.exp(-0.5 * pre * pre) * (1.0 / math.sqrt(2.0 * math.pi)))
        ).astype(BF)
        return carry

    lax.fori_loop(0, up_ref.shape[1] // BLOCK, one_block, 0)


def project(rows, gains, turns, weights):
    count, width = rows.shape
    cols, hidden, rank = weights[0].shape[2], weights[4].shape[1], weights[3].shape[1]
    return call(
        project_kernel,
        [rows, *gains, *turns, *weights],
        [
            ((3, cols // HEAD_DIM, HEAD_DIM, count), BF),
            ((count, 4 * rank), BF),
            ((count, width), BF),
            ((count, hidden), BF),
            ((count, hidden), BF),
        ],
        [pltpu.VMEM((count, width), BF)],
        flops=2 * count * width * (3 * cols + hidden + 4 * rank),
        exps=2 * count * hidden,
    )


def allowed_pairs(start, query_block, key_block):
    key_pos = key_block * BLOCK + lax.broadcasted_iota(jnp.int32, (BLOCK, BLOCK), 0)
    keep = key_pos >= start
    if key_block == query_block:
        query_pos = query_block * BLOCK + lax.broadcasted_iota(jnp.int32, (BLOCK, BLOCK), 1)
        keep = keep & (key_pos <= query_pos)
    return keep


def key_blocks(query_block):
    return range(max(0, query_block - MOST_DOC // BLOCK), query_block + 1)


def attend_forward(n, places_ref, start_ref, *rest):
    chunks, outs, log_ref = rest[:n], rest[n : 2 * n], rest[2 * n]
    qkv, mixed_all = rest[2 * n + 1 :]
    seq_len = start_ref.shape[1]
    count = seq_len // n
    heads = qkv.shape[1]
    for c in range(n):
        qkv[:, :, :, lanes(places_ref[c], count)] = chunks[c][...]

    def one_head(head, carry):
        queries, keys, values = qkv[0, head], qkv[1, head], qkv[2, head]
        keys_t = keys.T
        for i in range(seq_len // BLOCK):
            at = slice(i * BLOCK, (i + 1) * BLOCK)
            start = start_ref[:, at]
            scores = []
            for j in key_blocks(i):
                raw = mm(keys_t[j * BLOCK : (j + 1) * BLOCK], queries[:, at], 1, 0)
                scores.append(jnp.where(allowed_pairs(start, i, j), raw, MASKED))
            peak = jnp.max(scores[0], axis=0, keepdims=True)
            for block in scores[1:]:
                peak = jnp.maximum(peak, jnp.max(block, axis=0, keepdims=True))
            total, mixed = 0.0, 0.0
            for j, block in zip(key_blocks(i), scores):
                terms = jnp.exp(block - peak)
                total = total + jnp.sum(terms, axis=0, keepdims=True)
                mixed = mixed + mm(
                    values[:, j * BLOCK : (j + 1) * BLOCK], terms.astype(BF), 1, 0
                )
            mixed_all[head, :, at] = (mixed / total).astype(BF)
            log_ref[head, :, at] = peak + jnp.log(total)
        return carry

    lax.fori_loop(0, heads, one_head, 0)
    for c in range(n):
        outs[c][...] = mixed_all[:, :, lanes(places_ref[c], count)]


def attend_backward(n, first, places_ref, start_ref, cos_ref, sin_ref, log_ref, *rest):
    chunks, outs, grads, results = (rest[k * n : (k + 1) * n] for k in range(4))
    qkv, mixed_all, grad_all, result = rest[4 * n :]
    seq_len = start_ref.shape[1]
    count = seq_len // n
    heads = qkv.shape[1]
    mine = slice(first, first + heads)
    for c in range(n):
        at = lanes(places_ref[c], count)
        qkv[:, :, :, at] = chunks[c][:, mine]
        mixed_all[:, :, at] = outs[c][mine]
        grad_all[:, :, at] = grads[c][mine]
    cosine, sine = cos_ref[...], -sin_ref[...]
    blocks = seq_len // BLOCK

    def one_head(head, carry):
        queries, keys, values = qkv[0, head], qkv[1, head], qkv[2, head]
        grad = grad_all[head]
        inner = jnp.sum(
            grad.astype(F32) * mixed_all[head].astype(F32), axis=0, keepdims=True
        )
        keys_t, values_t = keys.T, values.T
        grad_keys, grad_values = [0.0] * blocks, [0.0] * blocks
        for i in range(blocks):
            at = slice(i * BLOCK, (i + 1) * BLOCK)
            start, log_total, inner_here = (
                start_ref[:, at],
                log_ref[first + head, :, at],
                inner[:, at],
            )
            query, grad_here = queries[:, at], grad[:, at]
            grad_query = 0.0
            for j in key_blocks(i):
                there = slice(j * BLOCK, (j + 1) * BLOCK)
                raw = mm(keys_t[there], query, 1, 0)
                terms = jnp.exp(jnp.where(allowed_pairs(start, i, j), raw, MASKED) - log_total)
                grad_terms = mm(values_t[there], grad_here, 1, 0)
                grad_scores = (terms * (grad_terms - inner_here)).astype(BF)
                grad_values[j] = grad_values[j] + mm(grad_here, terms.astype(BF), 1, 1)
                grad_keys[j] = grad_keys[j] + mm(query, grad_scores, 1, 1)
                grad_query = grad_query + mm(keys[:, there], grad_scores, 1, 0)
            grad_query = turn(grad_query * (HEAD_DIM**-0.5), cosine[:, at], sine[:, at])
            result[0, head, :, at] = grad_query.astype(BF)
        for j in range(blocks):
            there = slice(j * BLOCK, (j + 1) * BLOCK)
            result[1, head, :, there] = turn(
                grad_keys[j], cosine[:, there], sine[:, there]
            ).astype(BF)
            result[2, head, :, there] = grad_values[j].astype(BF)
        return carry

    lax.fori_loop(0, heads, one_head, 0)
    for c in range(n):
        results[c][...] = result[:, :, :, lanes(places_ref[c], count)]


def forward_attention(places, start, chunks):
    n = len(chunks)
    _, heads, _, count = chunks[0].shape
    seq_len = n * count
    pairs = heads * seq_len * seq_len // 2
    *outs, log_total = call(
        lambda *refs: attend_forward(n, *refs),
        [places, start, *chunks],
        [((heads, HEAD_DIM, count), BF)] * n + [((heads, 1, seq_len), F32)],
        [
            pltpu.VMEM((3, heads, HEAD_DIM, seq_len), BF),
            pltpu.VMEM((heads, HEAD_DIM, seq_len), BF),
        ],
        flops=pairs * 4 * HEAD_DIM * 4,
        exps=pairs,
        scalars=1,
    )
    return outs, log_total


def backward_attention(part, places, start, cosine, sine, log_total, chunks, outs, grads):
    n = len(chunks)
    _, heads, _, count = chunks[0].shape
    heads = heads // 2
    first = part * heads
    seq_len = n * count
    pairs = heads * seq_len * seq_len // 2
    return call(
        lambda *refs: attend_backward(n, first, *refs),
        [places, start, cosine, sine, log_total, *chunks, *outs, *grads],
        [((3, heads, HEAD_DIM, count), BF)] * n,
        [
            pltpu.VMEM((3, heads, HEAD_DIM, seq_len), BF),
            pltpu.VMEM((heads, HEAD_DIM, seq_len), BF),
            pltpu.VMEM((heads, HEAD_DIM, seq_len), BF),
            pltpu.VMEM((3, heads, HEAD_DIM, seq_len), BF),
        ],
        flops=pairs * 10 * HEAD_DIM * 4,
        exps=pairs,
        scalars=1,
    )


def out_kernel(
    mixed_ref, act_ref, out_full_ref, down_full_ref, out_first_ref, down_first_ref, *rest
):
    arrived_ref = rest[0] if len(rest) % 2 else None
    piece_ref, low_ref = rest[len(rest) % 2 :][:2]
    rank = out_first_ref.shape[1]
    cols, count = out_full_ref.shape[0], act_ref.shape[0]
    mixed = mixed_ref[...].reshape(cols, count)
    act = act_ref[...]
    total = mm(mixed, out_full_ref[...], 0, 0) + mm(act, down_full_ref[...], 1, 0)
    if arrived_ref is not None:
        total = total + arrived_ref[...].astype(F32)
    piece_ref[...] = total.astype(piece_ref.dtype)
    if len(rest) > 3:
        rest[-2][...] = total.astype(BF)
        rest[-1][...] = jnp.zeros(rest[-1].shape, BF)
    low_ref[:, :rank] = mm(mixed, out_first_ref[...], 0, 0).astype(BF)
    low_ref[:, rank:] = mm(act, down_first_ref[...], 1, 0).astype(BF)


def out_piece(
    mixed, act, out_full, down_full, out_first, down_first, dtype, arrived=None, both=False
):
    count, hidden = act.shape
    width, rank = out_full.shape[1], out_first.shape[1]
    operands = [mixed, act, out_full, down_full, out_first, down_first]
    return call(
        out_kernel,
        operands + ([] if arrived is None else [arrived]),
        [((count, width), dtype), ((count, 2 * rank), BF)]
        + ([((count, width), BF), ((8, 128), BF)] if both else []),
        flops=2 * count * (out_full.shape[0] + hidden) * width,
    )


def pull_kernel(
    g_ref,
    slope_ref,
    out_full_ref,
    down_ref,
    out_second_ref,
    down_second_ref,
    mixed_ref,
    low_ref,
    up_ref,
):
    grad = g_ref[...]
    mixed = mm(out_full_ref[...], grad, 1, 1)
    for head in range(mixed.shape[0] // HEAD_DIM):
        mixed_ref[head] = mixed[head * HEAD_DIM : (head + 1) * HEAD_DIM].astype(BF)
    rank = out_second_ref.shape[0]
    low_ref[:, :rank] = (ADAPTER_SCALE * mm(grad, out_second_ref[...], 1, 1)).astype(BF)
    low_ref[:, rank:] = (ADAPTER_SCALE * mm(grad, down_second_ref[...], 1, 1)).astype(BF)
    for begin in range(0, up_ref.shape[1], BLOCK):
        part = slice(begin, begin + BLOCK)
        up_ref[:, part] = (
            mm(grad, down_ref[part], 1, 1) * slope_ref[:, part].astype(F32)
        ).astype(BF)


def pull_back(grad, slope, out_full, down_full, out_second, down_second):
    count, width = grad.shape
    hidden, cols, twice = slope.shape[1], out_full.shape[0], 2 * out_second.shape[0]
    return call(
        pull_kernel,
        [grad, slope, out_full, down_full, out_second, down_second],
        [
            ((cols // HEAD_DIM, HEAD_DIM, count), BF),
            ((count, twice), BF),
            ((count, hidden), BF),
        ],
        flops=2 * count * width * (cols + hidden + twice),
    )


def slot_code(slot, bits):
    return sum(((slot >> b) & 1) << (bits - 1 - b) for b in range(bits))


def part_slots(members):
    halves = []
    while members > 4:
        members //= 2
        halves.append((members, members))
    return halves + [(slot, 1) for slot in range(members - 1, -1, -1)]


def move_slices(me, members, fields, parts, inward):
    bits = members.bit_length() - 1
    for (first, size), part in zip(part_slots(members), parts):
        for k in range(size):
            owner = me ^ slot_code(first + k, bits)
            low = 0
            for field in fields:
                rows = field.shape[0] // members
                at = pl.ds(pl.multiple_of(owner * rows, rows), rows)
                if inward:
                    part[k, low : low + rows] = field[at]
                else:
                    field[at] = part[k, low : low + rows]
                low += rows


def spread(me, members, fields, parts):
    move_slices(me, members, fields, parts, True)


def gather_spread(me, members, fields, parts):
    move_slices(me, members, fields, parts, False)


def early_kernel(chunks, packs, me_ref, up_second_ref, gain_ref, *rest):
    fields = 8
    more = rest[fields * chunks :]
    before, more = (more[:3], more[3:]) if packs != 1 else (None, more)
    if packs > 1:
        count = len(part_slots(packs))
        parts, more = more[:count], more[count:]
        out_ref, shared_ref, split_ref = more
    else:
        shared_ref, split_ref, out_ref = more
    rank = up_second_ref.shape[0]
    shared_up, shared_out, up_b, down_a, out_a = 0.0, 0.0, 0.0, 0.0, 0.0
    for c in range(chunks):
        grad, grad_up, hat, act, low, low_out, grad_low, mixed = (
            ref[...] for ref in rest[c * fields : (c + 1) * fields]
        )
        mixed = mixed.reshape(-1, mixed.shape[-1])
        low_up_grad = (ADAPTER_SCALE * mm(grad_up, up_second_ref[...], 1, 1)).astype(BF)
        shared_up = shared_up + mm(low_up_grad, hat, 0, 0)
        shared_out = shared_out + mm(low_out, grad, 0, 0)
        up_b = up_b + mm(low[:, 3 * rank :], grad_up, 0, 0)
        down_a = down_a + mm(grad_low[:, rank:], act, 0, 0)
        out_a = out_a + mm(grad_low[:, :rank], mixed, 0, 1)
    shared_up = shared_up * gain_ref[...]
    shared_out = ADAPTER_SCALE * shared_out
    up_b = ADAPTER_SCALE * up_b
    if before is not None:
        shared_up = shared_up + before[0][:rank]
        shared_out = shared_out + before[0][rank:]
        up_b = up_b + before[1][:rank]
        down_a = down_a + before[1][rank:]
        out_a = out_a + before[2][...]
    shared_ref[:rank] = shared_up.astype(shared_ref.dtype)
    shared_ref[rank:] = shared_out.astype(shared_ref.dtype)
    split_ref[:rank] = up_b.astype(split_ref.dtype)
    split_ref[rank:] = down_a.astype(split_ref.dtype)
    out_ref[...] = out_a.astype(out_ref.dtype)
    if packs > 1:
        spread(me_ref[0], packs, (shared_ref, split_ref), parts)


def part_shapes(members, rows, width):
    return [((size, rows, width), BF) for _, size in part_slots(members)]


def early_sums(me, items, up_second, gain, before=None, members=0):
    width, hidden, rank = items[0][0].shape[1], items[0][1].shape[1], up_second.shape[0]
    cols = items[0][7].shape[0] * HEAD_DIM
    sums = [((3 * rank, width), F32), ((2 * rank, hidden), F32), ((rank, cols), F32)]
    operands = [me, up_second, gain] + [array for item in items for array in item]
    scratch = []
    if before is None:
        packs, outputs = 1, sums
    elif not members:
        packs, outputs = 0, sums
    else:
        packs = members
        outputs = part_shapes(members, 5 * rank // members, width) + [((rank, cols), BF)]
        scratch = [pltpu.VMEM((3 * rank, width), BF), pltpu.VMEM((2 * rank, hidden), BF)]
    return call(
        lambda *refs: early_kernel(len(items), packs, *refs),
        operands + ([] if before is None else list(before)),
        outputs,
        scratch,
        flops=2 * len(items) * items[0][0].shape[0] * rank * 6 * width,
        scalars=1,
    )


def all_heads(first, second):
    return jnp.concatenate(
        [half.reshape(-1, half.shape[-1]) for half in (first, second)], axis=0
    )


def in_kernel(first_ref, second_ref, grad_up_ref, in_full_ref, up_full_ref, *rest):
    piece_ref = rest[-1]
    grad_pre = jnp.concatenate(
        [all_heads(first_ref[i], second_ref[i]) for i in range(3)], axis=0
    )
    total = mm(grad_pre, in_full_ref[...], 0, 1) + mm(grad_up_ref[...], up_full_ref[...], 1, 1)
    if len(rest) > 1:
        total = total + rest[0][...].astype(F32)
    piece_ref[...] = total.astype(piece_ref.dtype)


def in_piece(grad_pre, grad_up, in_full, up_full, dtype, arrived=None):
    count, hidden = grad_up.shape
    width = up_full.shape[0]
    operands = [*grad_pre, grad_up, in_full, up_full]
    (piece,) = call(
        in_kernel,
        operands + ([] if arrived is None else [arrived]),
        [((count, width), dtype)],
        flops=2 * count * (in_full.shape[1] + hidden) * width,
    )
    return piece


def late_kernel(chunks, packs, me_ref, second_ref, gain_ref, *rest):
    fields = 4
    more = rest[fields * chunks :]
    rank, cols = second_ref.shape[1], second_ref.shape[2]
    out_ref, more = more[0], more[1:]
    shared_ref, split_ref = more[-2:]

    def one_third(i, carry):
        shared, split = 0.0, 0.0
        for c in range(chunks):
            grad_first, grad_second, low, hat = rest[c * fields : (c + 1) * fields]
            part = all_heads(grad_first[i], grad_second[i])
            low_grad = (ADAPTER_SCALE * mm(part, second_ref[i], 0, 1)).astype(BF)
            shared = shared + mm(low_grad, hat[...], 0, 0)
            split = split + mm(low[:, lanes(i, rank)], part, 0, 1)
        shared_ref[pl.ds(pl.multiple_of(i * rank, rank), rank)] = (
            shared * gain_ref[...]
        ).astype(BF)
        split_ref[:, lanes(i, cols)] = (ADAPTER_SCALE * split).astype(BF)
        return carry

    lax.fori_loop(0, 3, one_third, 0, unroll=True)
    split_ref[:, 3 * cols :] = out_ref[...].astype(BF)
    if packs:
        spread(me_ref[0], packs, (shared_ref, split_ref), more[: len(part_slots(packs))])


def late_sums(me, items, second, gain, out_a, members=0):
    width, rank, cols = items[0][3].shape[1], second.shape[1], second.shape[2]
    sums = [((3 * rank, width), BF), ((rank, 4 * cols), BF)]
    packs = members
    return call(
        lambda *refs: late_kernel(len(items), packs, *refs),
        [me, second, gain] + [array for item in items for array in item] + [out_a],
        part_shapes(members, 4 * rank // members, width) if packs else sums,
        [pltpu.VMEM(*spec) for spec in sums] if packs else [],
        flops=2 * len(items) * items[0][2].shape[0] * rank * 3 * (width + 2 * cols),
        scalars=1,
    )


def early_unpack_kernel(packs, me_ref, *rest):
    count = len(part_slots(packs))
    parts = rest[:count]
    up_a_ref, out_b_ref, down_b_ref, up_b_ref, down_a_ref, shared_ref, split_ref = rest[count:]
    rank = out_b_ref.shape[0]
    gather_spread(me_ref[0], packs, (shared_ref, split_ref), parts)
    up_a_ref[...] = shared_ref[:rank].astype(F32).T
    out_b_ref[...] = shared_ref[rank : 2 * rank].astype(F32)
    down_b_ref[...] = shared_ref[2 * rank :].astype(F32)
    up_b_ref[...] = split_ref[:rank].astype(F32)
    down_a_ref[...] = split_ref[rank:].astype(F32).T


def late_unpack_kernel(packs, me_ref, *rest):
    count = len(part_slots(packs))
    parts = rest[:count]
    a_ref, b_ref, out_a_ref, shared_ref, split_ref = rest[count:]
    rank, cols = b_ref.shape[1], b_ref.shape[2]
    gather_spread(me_ref[0], packs, (shared_ref, split_ref), parts)
    for i in range(3):
        a_ref[i] = shared_ref[i * rank : (i + 1) * rank].astype(F32).T
        b_ref[i] = split_ref[:, i * cols : (i + 1) * cols].astype(F32)
    out_a_ref[...] = split_ref[:, 3 * cols :].astype(F32).T


def output_kernel(x_ref, own_ref, *rest):
    total = x_ref[...].astype(F32) + own_ref[...]
    for ref in rest[:-1]:
        total = total + ref[...].astype(F32)
    rest[-1][...] = total.astype(BF)


def input_grad_kernel(x_ref, g_ref, own_ref, *rest):
    total = own_ref[...]
    for ref in rest[:-1]:
        total = total + ref[...].astype(F32)
    hat, scale = normalize(x_ref[...])
    mean_grad = jnp.mean(total, axis=-1, keepdims=True)
    mean_cross = jnp.mean(total * hat, axis=-1, keepdims=True)
    rest[-1][...] = g_ref[...].astype(F32) + scale * (total - mean_grad - hat * mean_cross)


def add_kernel(left_ref, right_ref, sum_ref):
    sum_ref[...] = (left_ref[...].astype(F32) + right_ref[...].astype(F32)).astype(BF)


def added(left, right):
    return call(add_kernel, [left, right], [(left.shape, BF)])[0]


def fold_kernel(firsts, arrived_ref, *rest):
    parts, results = rest[: len(rest) // 2], rest[len(rest) // 2 :]
    for first, part, result in zip(firsts, parts, results):
        result[...] = (
            part[...].astype(F32) + arrived_ref[first : first + part.shape[0]].astype(F32)
        ).astype(BF)


def meet_kernel(count, *refs):
    total = refs[0][...].astype(F32)
    for ref in refs[1:count]:
        total = total + ref[...].astype(F32)
    shared_ref, split_ref = refs[count:]
    rows = shared_ref.shape[1]
    shared_ref[...] = total[:, :rows].astype(BF)
    split_ref[...] = total[:, rows:].astype(BF)


def close_kernel(shared_ref, arrived_ref, split_ref, both_ref):
    rows = shared_ref.shape[1]
    both_ref[:, :rows] = (
        shared_ref[...].astype(F32) + arrived_ref[...].astype(F32)
    ).astype(BF)
    both_ref[:, rows:] = split_ref[...]


def join_kernel(*refs):
    low = 0
    for ref in refs[:-1]:
        refs[-1][low : low + ref.shape[0]] = ref[...]
        low += ref.shape[0]


def swap_pairs(n):
    return [(i, i ^ 1) for i in range(n)]


def mirror_pairs(n):
    return [(i, n - 1 - i) for i in range(n)]


def together(*values):
    return lax.optimization_barrier(values)


def after(value, *earlier):
    return lax.optimization_barrier((value, earlier))[0]


def ring_scatter(piece, pieces):
    up = [(i, (i + 1) % pieces) for i in range(pieces)]
    running = piece(1, None)
    for k in range(2, pieces + 1):
        running = piece(k % pieces, lax.ppermute(running, "tensor", up))
    return running


class GroupSum:
    def __init__(self, parts, n_shared):
        self.parts, self.n_shared = list(parts), n_shared
        self.members, self.n = lax.axis_size("dp"), lax.axis_size("tensor")
        self.bits = self.members.bit_length() - 1
        self.slots = part_slots(self.members)
        halves = self.bits - 2
        self.steps = [("down", b) for b in range(halves)] + [("meet", 0)]
        jump = 1
        while jump < self.n:
            self.steps.append(("across", jump))
            jump *= 2
        self.steps += [("part", 0)] + [("back", b) for b in reversed(range(halves))]
        self.moving, self.at, self.results = None, 0, []

    def hop(self, value, code):
        pairs = [(k, k ^ code) for k in range(self.members)]
        return lax.ppermute(value, "dp", pairs)

    def start(self):
        kind, which = self.steps[self.at]
        codes = [slot_code(slot, self.bits) for slot in (1, 2, 3)]
        if kind == "across":
            pairs = [(k, k ^ which) for k in range(self.n)]
            self.moving = lax.ppermute(self.shared, "tensor", pairs)
        elif kind == "down":
            self.moving = self.hop(self.parts[which], 1 << which)
        elif kind == "meet":
            self.moving = [
                self.hop(self.parts[-1 - slot], code) for slot, code in zip((1, 2, 3), codes)
            ]
        elif kind == "part":
            self.moving = [self.hop(self.have, code) for code in codes]
        else:
            self.moving = self.hop(self.have, 1 << which)

    def finish(self, *earlier):
        kind, which = self.steps[self.at]
        arrived = after(self.moving, *earlier) if earlier else self.moving
        if kind == "down":
            later = self.parts[which + 1 :]
            firsts = [first for first, _ in self.slots[which + 1 :]]
            self.parts[which + 1 :] = call(
                lambda *refs: fold_kernel(firsts, *refs),
                [arrived, *later],
                [(part.shape, BF) for part in later],
            )
            value = self.parts[-1]
        elif kind == "meet":
            _, rows, width = self.parts[-1].shape
            self.shared, self.split = call(
                lambda *refs: meet_kernel(4, *refs),
                [self.parts[-1], *arrived],
                [((1, self.n_shared, width), BF), ((1, rows - self.n_shared, width), BF)],
            )
            value = self.shared
        elif kind == "across":
            if self.steps[self.at + 1][0] == "part":
                (self.have,) = call(
                    close_kernel,
                    [self.shared, arrived, self.split],
                    [(self.parts[-1].shape, BF)],
                )
                value = self.have
            else:
                self.shared = value = added(self.shared, arrived)
        else:
            pieces = list(arrived) if kind == "part" else [arrived]
            self.results = self.results or [self.have]
            self.results += pieces
            value = pieces[0]
            if self.at + 1 < len(self.steps):
                _, *rows = self.have.shape
                total = sum(piece.shape[0] for piece in [self.have, *pieces])
                (self.have,) = call(
                    join_kernel, [self.have, *pieces], [((total, *rows), BF)]
                )
                value = self.have
        self.at += 1
        return value

    def rest(self):
        while self.at < len(self.steps):
            self.start()
            self.finish()
        return self.results[::-1]


def slow_parts(me, shared, split, members):
    bits = members.bit_length() - 1
    width = shared.shape[1]
    both = jnp.concatenate(
        [
            shared.astype(BF).reshape(members, -1, width),
            split.astype(BF).reshape(members, -1, width),
        ],
        axis=1,
    )
    order = jnp.asarray([slot_code(slot, bits) for slot in range(members)], jnp.int32) ^ me
    both = both[order]
    return [both[first : first + size] for first, size in part_slots(members)]


def slow_whole(me, parts, n_shared, members):
    bits = members.bit_length() - 1
    both = jnp.concatenate(parts[::-1], axis=0)
    order = jnp.asarray([slot_code(slot, bits) for slot in range(members)], jnp.int32)
    both = both[order[jnp.arange(members, dtype=jnp.int32) ^ me]].astype(F32)
    width = both.shape[-1]
    return both[:, :n_shared].reshape(-1, width), both[:, n_shared:].reshape(-1, width)


def normalize(inputs):
    values = inputs.astype(F32)
    center = values - jnp.mean(values, axis=-1, keepdims=True)
    inv_scale = lax.rsqrt(jnp.mean(center * center, axis=-1, keepdims=True) + EPSILON)
    return center * inv_scale, inv_scale


def whole_step(
    layer_input,
    document_lengths,
    attention_norm_gain,
    feedfwd_norm_gain,
    query_key_value_weight,
    output_weight,
    up_weight,
    down_weight,
    adapter_query_key_value_first,
    adapter_query_key_value_second,
    adapter_output_first,
    adapter_output_second,
    adapter_up_first,
    adapter_up_second,
    adapter_down_first,
    adapter_down_second,
    cotangent,
):
    own_x, own_g = layer_input[0], cotangent[0]
    shard_len, width = own_x.shape
    n = lax.axis_size("tensor")
    me = lax.axis_index("tensor")
    seq_len = shard_len * n
    rank = adapter_up_first.shape[1]
    cols = query_key_value_weight.shape[2]
    hidden = up_weight.shape[1]
    swap, mirror = swap_pairs(n), mirror_pairs(n)
    short = n == 4

    def send(value, pairs):
        return lax.ppermute(value, "tensor", pairs)

    members = lax.axis_size("dp")
    tidy = short and hidden == width and 4 * cols == width and rank % (16 * members) == 0
    if short:
        owners = [me, me ^ 1, n - 1 - me, (n - 1 - me) ^ 1]
    else:
        owners = [lax.rem(me - k + n, n) for k in range(n)]
    places = jnp.stack(owners).astype(jnp.int32)
    me_dp = lax.axis_index("dp").astype(jnp.int32).reshape(1)
    places, me_dp, own_x = together(places, me_dp, own_x)
    turns = call(
        places_kernel,
        [places, document_lengths],
        [((1, seq_len), jnp.int32), ((HALF, seq_len), F32), ((HALF, seq_len), F32)]
        + [((HALF, shard_len), F32)] * (2 * n),
        scalars=2,
    )
    start, cosine, sine, turns = turns[0], turns[1], turns[2], turns[3:]
    gain_a, gain_m = attention_norm_gain[None], feedfwd_norm_gain[None]
    weights = (
        query_key_value_weight,
        adapter_query_key_value_first,
        adapter_query_key_value_second,
        adapter_up_first,
        up_weight,
        adapter_up_second,
    )

    def projected(k, rows):
        return project(rows, (gain_a, gain_m), (turns[k], turns[n + k]), weights)

    def merged():
        return merge_weights(
            query_key_value_weight,
            up_weight,
            output_weight,
            down_weight,
            (adapter_query_key_value_first, adapter_query_key_value_second),
            (adapter_up_first, adapter_up_second),
            (adapter_output_first, adapter_output_second),
            (adapter_down_first, adapter_down_second),
            gain_a,
            gain_m,
        )

    outward, inward, middle = [(0, 1), (3, 2)], [(1, 0), (2, 3)], [(1, 2), (2, 1)]
    if short:
        x_near, x_facing = send(own_x, swap), send(own_x, mirror)
        full = merged()
        first = projected(0, own_x)
        x_near, x_facing, first, full, own_g = together(x_near, x_facing, first, full, own_g)
        x_far = send(x_facing, swap)
        g_near, g_mid = send(own_g, swap), send(own_g, middle)
        state = [first, projected(1, x_near), projected(2, x_facing)]
        x_far, state = together(x_far, state)
        state = state + [projected(3, x_far)]
    else:
        full = merged()
        up_ring = [(i, (i + 1) % n) for i in range(n)]
        state, moving = [projected(0, own_x)], own_x
        for k in range(1, n):
            moving = send(moving, up_ring)
            state.append(projected(k, moving))
    in_full, up_full, out_full, down_full = full
    qkv, low, hat, act, slope = (list(field) for field in zip(*state))
    mixed, log_total = forward_attention(places, start, qkv)
    low_out = [None] * n

    def out_part(k, dtype, last=None, arrived=None, both=False):
        rows = mixed[k] if last is None else after(mixed[k], last)
        piece, low_out[k], *more = out_piece(
            rows,
            act[k],
            out_full,
            down_full,
            adapter_output_first,
            adapter_down_first,
            dtype,
            arrived,
            both,
        )
        return (piece, more[0]) if both else piece

    def pulled(k, grad):
        return pull_back(
            grad,
            slope[k],
            out_full,
            down_full,
            adapter_output_second,
            adapter_down_second,
        )

    def early_item(k, grad, back):
        return (grad, back[2], hat[k], act[k], low[k], low_out[k], back[1], mixed[k])

    if short:
        y_facing, y_facing_low = out_part(2, F32, both=True)
        y_far, y_far_low = out_part(3, F32, both=True)
        y_1, y_2 = send(y_facing_low, outward), send(y_far_low, outward)
        g_near, g_mid = after((g_near, g_mid), mixed)
        g_mid_far, g_end_far = send(g_near, middle), send(g_mid, inward)
        backs = [pulled(0, own_g)]
        g_mid_far, g_end_far = after((g_mid_far, g_end_far), y_far, backs)
        g_end = send(g_mid_far, inward)
        g_far = added(g_mid_far, g_end_far)
        backs.append(pulled(1, after(g_near, g_far)))
        y_near, y_own = out_part(1, F32, g_far), out_part(0, F32, g_far)
        pulled_far = pulled(3, g_far)
        y_3 = send(added(y_far, after(y_1, backs, y_near, y_own, pulled_far)), middle)
        backs = backs + [None, pulled_far]
        all_g = [own_g, g_near, None, g_far]
        before = early_sums(
            me_dp,
            [early_item(k, all_g[k], backs[k]) for k in (0, 1, 3)],
            adapter_up_second,
            gain_m,
        )
        g_end = after(g_end, before)
        g_facing = added(g_mid, g_end)
        backs[2] = pulled(2, g_facing)
        early = early_sums(
            me_dp,
            [early_item(2, g_facing, backs[2])],
            adapter_up_second,
            gain_m,
            before,
            members if tidy else 0,
        )
    else:
        y_own = ring_scatter(
            lambda k, arrived: out_part(k, BF if k else F32, arrived=arrived), n
        )
        backs, moving, all_g = [pulled(0, own_g)], own_g, [own_g]
        for k in range(1, n):
            moving = send(moving, up_ring)
            all_g.append(moving)
            backs.append(pulled(k, moving))
        early = early_sums(
            me_dp, [early_item(k, all_g[k], backs[k]) for k in range(n)], adapter_up_second, gain_m
        )

    *early, out_a = early
    if not tidy:
        early = slow_parts(me_dp[0], early[0], early[1].reshape(-1, width), members)
    early = GroupSum(early, 3 * rank // members)
    early.start()
    grads_mixed = [back[0] for back in backs]
    halves = []
    for part in range(2):
        halves.append(
            backward_attention(
                part, places, start, cosine, sine, log_total, qkv, mixed, grads_mixed
            )
        )
        if short and not part:
            last = early.finish(halves[0])
            early.start()
            y_5 = send(added(y_facing, after(y_2, last)), middle)
            y_near = added(y_near, after(y_3, last))
            y_4 = send(y_near, swap)
            grads_mixed = after(grads_mixed, y_near)
    grad_pre = list(zip(*halves))

    def in_part(k, dtype, arrived=None, last=None):
        pre = grad_pre[k] if last is None else after(grad_pre[k], last)
        return in_piece(pre, backs[k][2], in_full, up_full, dtype, arrived)

    def early_whole(parts):
        if not tidy:
            early_a, early_b = slow_whole(me_dp[0], parts, 3 * rank // members, members)
            early_b = early_b.reshape(2 * rank, hidden)
            return (
                early_a[:rank].T,
                early_a[rank : 2 * rank],
                early_a[2 * rank :],
                early_b[:rank],
                early_b[rank:].T,
            )
        return call(
            lambda *refs: early_unpack_kernel(members, *refs),
            [me_dp, *parts],
            [
                ((width, rank), F32),
                ((rank, width), F32),
                ((rank, width), F32),
                ((rank, hidden), F32),
                ((hidden, rank), F32),
            ],
            [pltpu.VMEM((3 * rank, width), BF), pltpu.VMEM((2 * rank, width), BF)],
            scalars=1,
        )

    def late_parts():
        late = late_sums(
            me_dp,
            [(*grad_pre[k], low[k], hat[k]) for k in range(n)],
            adapter_query_key_value_second,
            gain_a,
            out_a,
            members if tidy else 0,
        )
        if not tidy:
            late = slow_parts(me_dp[0], late[0], late[1].reshape(-1, width), members)
        return GroupSum(late, 3 * rank // members)

    if short:
        last = early.finish(grad_pre)
        early.start()
        late = late_parts()
        late.start()
        dx_far = in_part(3, BF)
        last = early.finish(dx_far)
        early.start()
        dx_swap = send(dx_far, swap)
        last = late.finish(last)
        late.start()
        dx_near = in_part(1, BF, last=last)
        last = early.finish(dx_near)
        early.start()
        last = late.finish(last)
        late.start()
        dx_own = in_part(0, F32, last=last)
        dx_facing = in_part(2, BF, after(dx_swap, dx_own))
        last = late.finish(dx_facing)
        late.start()
        dx_a = send(dx_near, swap)
        dx_b = send(dx_facing, mirror)
        last = early.finish(last)
        early.start()
        (layer_output,) = call(
            output_kernel,
            [own_x, y_own, *after((y_4, y_5), last)],
            [((shard_len, width), BF)],
        )
        last = late.finish(last, layer_output)
        late.start()
        early.finish(last)
        early_done = early_whole(early.rest())
        last = late.finish(early_done)
        late.start()
        dx_parts = [dx_own, dx_a, dx_b]
    else:
        (layer_output,) = call(output_kernel, [own_x, y_own], [((shard_len, width), BF)])
        dx_parts = [
            ring_scatter(lambda k, arrived: in_part(k, BF if k else F32, arrived), n)
        ]
        early.finish()
        late = late_parts()
        early_done = early_whole(early.rest())
    up_a, out_b, down_b, up_b, down_a = early_done
    late = late.rest()
    if tidy:
        a_qkv, b_qkv, out_a = call(
            lambda *refs: late_unpack_kernel(members, *refs),
            [me_dp, *late],
            [((3, width, rank), F32), ((3, rank, cols), F32), ((cols, rank), F32)],
            [pltpu.VMEM((3 * rank, width), BF), pltpu.VMEM((rank, width), BF)],
            scalars=1,
        )
    else:
        late_a, late_b = slow_whole(me_dp[0], late, 3 * rank // members, members)
        late_b = late_b.reshape(rank, 4 * cols)
        a_qkv = jnp.swapaxes(late_a.reshape(3, rank, width), 1, 2)
        b_qkv = jnp.stack([late_b[:, i * cols : (i + 1) * cols] for i in range(3)])
        out_a = late_b[:, 3 * cols :].T
    dx_parts = [dx_parts[0], *after(dx_parts[1:], a_qkv)]
    (grad_in,) = call(
        input_grad_kernel, [own_x, own_g, *dx_parts], [((shard_len, width), F32)]
    )
    return (
        layer_output[None],
        grad_in[None],
        a_qkv,
        b_qkv,
        out_a,
        out_b,
        up_a,
        up_b,
        down_a,
        down_b,
    )


def solution(mesh):
    in_specs = (
        P("dp", "tensor", None),
        P("dp", None),
        P(),
        P(),
        P(None, None, "tensor"),
        P("tensor", None),
        P(None, "tensor"),
        P("tensor", None),
        P(),
        P(None, None, "tensor"),
        P("tensor", None),
        P(),
        P(),
        P(None, "tensor"),
        P("tensor", None),
        P(),
        P("dp", "tensor", None),
    )
    out_specs = (
        P("dp", "tensor", None),
        P("dp", "tensor", None),
        P(),
        P(None, None, "tensor"),
        P("tensor", None),
        P(),
        P(),
        P(None, "tensor"),
        P("tensor", None),
        P(),
    )
    return jax.shard_map(
        whole_step, mesh=mesh, in_specs=in_specs, out_specs=out_specs, check_vma=False
    )
```

```python
import math

import jax
import jax.numpy as jnp
from jax import lax
from jax.experimental import pallas as pl
from jax.experimental.pallas import tpu as pltpu
from jax.sharding import PartitionSpec as P

HEAD_DIM = 64
ROT = 16
HALF = ROT // 2
BLOCK = 256
MOST_DOC = 512

EPSILON = 1e-05
ADAPTER_SCALE = 0.25
MASKED = -1e30
VMEM_GRANT = 12 << 20
BF = jnp.bfloat16
F32 = jnp.float32


def mm(left, right, left_dim, right_dim):
    return lax.dot_general(
        left, right, (((left_dim,), (right_dim,)), ((), ())), preferred_element_type=F32
    )


def call(kernel, operands, outputs, scratch=(), flops=0, exps=0, scalars=0):
    spaces = [pltpu.SMEM] * scalars + [pltpu.VMEM] * (len(operands) - scalars)
    moved = sum(math.prod(s) * jnp.dtype(d).itemsize for s, d in outputs)
    return pl.pallas_call(
        kernel,
        in_specs=[pl.BlockSpec(memory_space=space) for space in spaces],
        out_specs=[pl.BlockSpec(memory_space=pltpu.VMEM) for _ in outputs],
        out_shape=[jax.ShapeDtypeStruct(s, d) for s, d in outputs],
        scratch_shapes=list(scratch),
        compiler_params=pltpu.CompilerParams(vmem_limit_bytes=VMEM_GRANT),
        cost_estimate=pl.CostEstimate(
            flops=flops, bytes_accessed=2 * moved, transcendentals=exps
        ),
    )(*operands)


def places_kernel(places_ref, lengths_ref, start_ref, cos_ref, sin_ref, *shards):
    count, seq_len = lengths_ref.shape[1], start_ref.shape[1]
    pos = lax.broadcasted_iota(jnp.int32, (HALF, seq_len), 1)
    start, end = jnp.zeros((HALF, seq_len), jnp.int32), jnp.int32(0)
    for j in range(count):
        end = end + lengths_ref[0, j]
        start = jnp.where(pos >= end, end, start)
    start_ref[...] = start[:1]
    row = lax.broadcasted_iota(jnp.int32, (HALF, seq_len), 0).astype(F32)
    inverse = jnp.exp(row * (-2.0 * math.log(10000.0) / ROT))
    angles = (pos - start).astype(F32) * inverse
    cos_ref[...] = jnp.cos(angles)
    sin_ref[...] = jnp.sin(angles)
    n = len(shards) // 2
    for k in range(n):
        at = lanes(places_ref[k], seq_len // n)
        shards[k][...] = cos_ref[:, at]
        shards[n + k][...] = sin_ref[:, at]


def turn(value, cosine, sine):
    lead, tail = value[:HALF], value[HALF:ROT]
    return jnp.concatenate(
        [lead * cosine - tail * sine, tail * cosine + lead * sine, value[ROT:]], axis=0
    )


def lanes(place, count):
    return pl.ds(pl.multiple_of(place * count, 128), count)


def merge_kernel(
    qkv_ref,
    qkv_first_ref,
    qkv_second_ref,
    up_ref,
    up_first_ref,
    up_second_ref,
    out_ref,
    out_first_ref,
    out_second_ref,
    down_ref,
    down_first_ref,
    down_second_ref,
    gain_a_ref,
    gain_m_ref,
    in_full_ref,
    up_full_ref,
    out_full_ref,
    down_full_ref,
):
    cols = qkv_ref.shape[2]

    def joined(weight, first, second):
        return weight.astype(F32) + ADAPTER_SCALE * mm(first, second, 1, 0)

    def column(row):
        return jnp.broadcast_to(row, (128, row.shape[1])).T

    def times(value, tall):
        return jnp.concatenate(
            [value[:, k : k + 128] * tall for k in range(0, value.shape[1], 128)], axis=1
        )

    gain_a, gain_m = column(gain_a_ref[...]), column(gain_m_ref[...])

    for i in range(3):
        in_full_ref[:, i * cols : (i + 1) * cols] = times(
            joined(qkv_ref[i], qkv_first_ref[i], qkv_second_ref[i]), gain_a
        ).astype(BF)
    up_full_ref[...] = times(
        joined(up_ref[...], up_first_ref[...], up_second_ref[...]), gain_m
    ).astype(BF)
    out_full_ref[...] = joined(out_ref[...], out_first_ref[...], out_second_ref[...]).astype(BF)
    down_full_ref[...] = joined(down_ref[...], down_first_ref[...], down_second_ref[...]).astype(
        BF
    )


def merge_weights(qkv, up, out, down, qkv_ab, up_ab, out_ab, down_ab, gain_a, gain_m):
    steps = 4
    width, cols = qkv.shape[1], qkv.shape[2]
    hidden, rank = up.shape[1], up_ab[0].shape[1]
    rows, out_rows, down_rows = width // steps, cols // steps, hidden // steps

    def fixed(shape):
        return pl.BlockSpec(shape, lambda s: (0,) * len(shape))

    def moving(shape):
        return pl.BlockSpec(shape, lambda s: (s,) + (0,) * (len(shape) - 1))

    def middle(shape):
        return pl.BlockSpec(shape, lambda s: (0, s, 0))

    return pl.pallas_call(
        merge_kernel,
        grid=(steps,),
        in_specs=[
            middle((3, rows, cols)),
            middle((3, rows, rank)),
            fixed((3, rank, cols)),
            moving((rows, hidden)),
            moving((rows, rank)),
            fixed((rank, hidden)),
            moving((out_rows, width)),
            moving((out_rows, rank)),
            fixed((rank, width)),
            moving((down_rows, width)),
            moving((down_rows, rank)),
            fixed((rank, width)),
            pl.BlockSpec((1, rows), lambda s: (0, s)),
            pl.BlockSpec((1, rows), lambda s: (0, s)),
        ],
        out_specs=[
            moving((rows, 3 * cols)),
            moving((rows, hidden)),
            moving((out_rows, width)),
            moving((down_rows, width)),
        ],
        out_shape=[
            jax.ShapeDtypeStruct((width, 3 * cols), BF),
            jax.ShapeDtypeStruct((width, hidden), BF),
            jax.ShapeDtypeStruct((cols, width), BF),
            jax.ShapeDtypeStruct((hidden, width), BF),
        ],
        compiler_params=pltpu.CompilerParams(vmem_limit_bytes=VMEM_GRANT),
        cost_estimate=pl.CostEstimate(
            flops=2 * rank * width * (4 * cols + 2 * hidden),
            bytes_accessed=4 * width * (4 * cols + 2 * hidden),
            transcendentals=0,
        ),
    )(
        qkv,
        qkv_ab[0],
        qkv_ab[1],
        up,
        up_ab[0],
        up_ab[1],
        out,
        out_ab[0],
        out_ab[1],
        down,
        down_ab[0],
        down_ab[1],
        gain_a,
        gain_m,
    )


def project_kernel(
    x_ref,
    gain_a_ref,
    gain_m_ref,
    cos_ref,
    sin_ref,
    qkv_weight_ref,
    qkv_first_ref,
    qkv_second_ref,
    up_first_ref,
    up_ref,
    up_second_ref,
    qkv_ref,
    low_ref,
    hat_ref,
    act_ref,
    slope_ref,
    mlp_ref,
):
    rank = up_first_ref.shape[1]
    cols = qkv_weight_ref.shape[2]
    values = x_ref[...].astype(F32)
    center = values - jnp.mean(values, axis=-1, keepdims=True)
    hat = center * lax.rsqrt(jnp.mean(center * center, axis=-1, keepdims=True) + EPSILON)
    hat_ref[...] = hat.astype(BF)
    attn_in = (hat * gain_a_ref[...]).astype(BF)
    feed_in = (hat * gain_m_ref[...]).astype(BF)
    cosine, sine = cos_ref[...], sin_ref[...]

    def one_third(i, carry):
        low = mm(attn_in, qkv_first_ref[i], 1, 0).astype(BF)
        low_ref[:, lanes(i, rank)] = low
        pre = mm(attn_in, qkv_weight_ref[i], 1, 0) + ADAPTER_SCALE * mm(
            low, qkv_second_ref[i], 1, 0
        )
        pre = pre.T
        turned = (i < 2).astype(F32)
        scale = jnp.where(i == 0, HEAD_DIM**-0.5, 1.0)
        cos_here = 1.0 + turned * (cosine - 1.0)
        sin_here = turned * sine
        for head in range(cols // HEAD_DIM):
            rows = turn(pre[head * HEAD_DIM : (head + 1) * HEAD_DIM], cos_here, sin_here)
            qkv_ref[i, head] = (rows * scale).astype(BF)
        return carry

    lax.fori_loop(0, 3, one_third, 0)
    low = mm(feed_in, up_first_ref[...], 1, 0).astype(BF)
    low_ref[:, 3 * rank :] = low
    mlp_ref[...] = feed_in

    def one_block(k, carry):
        part = lanes(k, BLOCK)
        pre = mm(mlp_ref[...], up_ref[:, part], 1, 0) + ADAPTER_SCALE * mm(
            low, up_second_ref[:, part], 1, 0
        )
        cdf = 0.5 * (1.0 + lax.erf(pre * (2.0**-0.5)))
        act_ref[:, part] = (pre * cdf).astype(BF)
        slope_ref[:, part] = (
            cdf + pre * (jnp.exp(-0.5 * pre * pre) * (1.0 / math.sqrt(2.0 * math.pi)))
        ).astype(BF)
        return carry

    lax.fori_loop(0, up_ref.shape[1] // BLOCK, one_block, 0)


def project(rows, gains, turns, weights):
    count, width = rows.shape
    cols, hidden, rank = weights[0].shape[2], weights[4].shape[1], weights[3].shape[1]
    return call(
        project_kernel,
        [rows, *gains, *turns, *weights],
        [
            ((3, cols // HEAD_DIM, HEAD_DIM, count), BF),
            ((count, 4 * rank), BF),
            ((count, width), BF),
            ((count, hidden), BF),
            ((count, hidden), BF),
        ],
        [pltpu.VMEM((count, width), BF)],
        flops=2 * count * width * (3 * cols + hidden + 4 * rank),
        exps=2 * count * hidden,
    )


def allowed_pairs(start, query_block, key_block):
    key_pos = key_block * BLOCK + lax.broadcasted_iota(jnp.int32, (BLOCK, BLOCK), 0)
    keep = key_pos >= start
    if key_block == query_block:
        query_pos = query_block * BLOCK + lax.broadcasted_iota(jnp.int32, (BLOCK, BLOCK), 1)
        keep = keep & (key_pos <= query_pos)
    return keep


def key_blocks(query_block):
    return range(max(0, query_block - MOST_DOC // BLOCK), query_block + 1)


def attend_forward(n, places_ref, start_ref, *rest):
    chunks, outs, log_ref = rest[:n], rest[n : 2 * n], rest[2 * n]
    qkv, mixed_all = rest[2 * n + 1 :]
    seq_len = start_ref.shape[1]
    count = seq_len // n
    heads = qkv.shape[1]
    for c in range(n):
        qkv[:, :, :, lanes(places_ref[c], count)] = chunks[c][...]

    def one_head(head, carry):
        queries, keys, values = qkv[0, head], qkv[1, head], qkv[2, head]
        keys_t = keys.T
        for i in range(seq_len // BLOCK):
            at = slice(i * BLOCK, (i + 1) * BLOCK)
            start = start_ref[:, at]
            scores = []
            for j in key_blocks(i):
                raw = mm(keys_t[j * BLOCK : (j + 1) * BLOCK], queries[:, at], 1, 0)
                scores.append(jnp.where(allowed_pairs(start, i, j), raw, MASKED))
            peak = jnp.max(scores[0], axis=0, keepdims=True)
            for block in scores[1:]:
                peak = jnp.maximum(peak, jnp.max(block, axis=0, keepdims=True))
            total, mixed = 0.0, 0.0
            for j, block in zip(key_blocks(i), scores):
                terms = jnp.exp(block - peak)
                total = total + jnp.sum(terms, axis=0, keepdims=True)
                mixed = mixed + mm(
                    values[:, j * BLOCK : (j + 1) * BLOCK], terms.astype(BF), 1, 0
                )
            mixed_all[head, :, at] = (mixed / total).astype(BF)
            log_ref[head, :, at] = peak + jnp.log(total)
        return carry

    lax.fori_loop(0, heads, one_head, 0)
    for c in range(n):
        outs[c][...] = mixed_all[:, :, lanes(places_ref[c], count)]


def attend_backward(n, first, places_ref, start_ref, cos_ref, sin_ref, log_ref, *rest):
    chunks, outs, grads, results = (rest[k * n : (k + 1) * n] for k in range(4))
    qkv, mixed_all, grad_all, result = rest[4 * n :]
    seq_len = start_ref.shape[1]
    count = seq_len // n
    heads = qkv.shape[1]
    mine = slice(first, first + heads)
    for c in range(n):
        at = lanes(places_ref[c], count)
        qkv[:, :, :, at] = chunks[c][:, mine]
        mixed_all[:, :, at] = outs[c][mine]
        grad_all[:, :, at] = grads[c][mine]
    cosine, sine = cos_ref[...], -sin_ref[...]
    blocks = seq_len // BLOCK

    def one_head(head, carry):
        queries, keys, values = qkv[0, head], qkv[1, head], qkv[2, head]
        grad = grad_all[head]
        inner = jnp.sum(
            grad.astype(F32) * mixed_all[head].astype(F32), axis=0, keepdims=True
        )
        keys_t, values_t = keys.T, values.T
        grad_keys, grad_values = [0.0] * blocks, [0.0] * blocks
        for i in range(blocks):
            at = slice(i * BLOCK, (i + 1) * BLOCK)
            start, log_total, inner_here = (
                start_ref[:, at],
                log_ref[first + head, :, at],
                inner[:, at],
            )
            query, grad_here = queries[:, at], grad[:, at]
            grad_query = 0.0
            for j in key_blocks(i):
                there = slice(j * BLOCK, (j + 1) * BLOCK)
                raw = mm(keys_t[there], query, 1, 0)
                terms = jnp.exp(jnp.where(allowed_pairs(start, i, j), raw, MASKED) - log_total)
                grad_terms = mm(values_t[there], grad_here, 1, 0)
                grad_scores = (terms * (grad_terms - inner_here)).astype(BF)
                grad_values[j] = grad_values[j] + mm(grad_here, terms.astype(BF), 1, 1)
                grad_keys[j] = grad_keys[j] + mm(query, grad_scores, 1, 1)
                grad_query = grad_query + mm(keys[:, there], grad_scores, 1, 0)
            grad_query = turn(grad_query * (HEAD_DIM**-0.5), cosine[:, at], sine[:, at])
            result[0, head, :, at] = grad_query.astype(BF)
        for j in range(blocks):
            there = slice(j * BLOCK, (j + 1) * BLOCK)
            result[1, head, :, there] = turn(
                grad_keys[j], cosine[:, there], sine[:, there]
            ).astype(BF)
            result[2, head, :, there] = grad_values[j].astype(BF)
        return carry

    lax.fori_loop(0, heads, one_head, 0)
    for c in range(n):
        results[c][...] = result[:, :, :, lanes(places_ref[c], count)]


def forward_attention(places, start, chunks):
    n = len(chunks)
    _, heads, _, count = chunks[0].shape
    seq_len = n * count
    pairs = heads * seq_len * seq_len // 2
    *outs, log_total = call(
        lambda *refs: attend_forward(n, *refs),
        [places, start, *chunks],
        [((heads, HEAD_DIM, count), BF)] * n + [((heads, 1, seq_len), F32)],
        [
            pltpu.VMEM((3, heads, HEAD_DIM, seq_len), BF),
            pltpu.VMEM((heads, HEAD_DIM, seq_len), BF),
        ],
        flops=pairs * 4 * HEAD_DIM * 4,
        exps=pairs,
        scalars=1,
    )
    return outs, log_total


def backward_attention(part, places, start, cosine, sine, log_total, chunks, outs, grads):
    n = len(chunks)
    _, heads, _, count = chunks[0].shape
    heads = heads // 2
    first = part * heads
    seq_len = n * count
    pairs = heads * seq_len * seq_len // 2
    return call(
        lambda *refs: attend_backward(n, first, *refs),
        [places, start, cosine, sine, log_total, *chunks, *outs, *grads],
        [((3, heads, HEAD_DIM, count), BF)] * n,
        [
            pltpu.VMEM((3, heads, HEAD_DIM, seq_len), BF),
            pltpu.VMEM((heads, HEAD_DIM, seq_len), BF),
            pltpu.VMEM((heads, HEAD_DIM, seq_len), BF),
            pltpu.VMEM((3, heads, HEAD_DIM, seq_len), BF),
        ],
        flops=pairs * 10 * HEAD_DIM * 4,
        exps=pairs,
        scalars=1,
    )


def out_kernel(
    mixed_ref, act_ref, out_full_ref, down_full_ref, out_first_ref, down_first_ref, *rest
):
    arrived_ref = rest[0] if len(rest) % 2 else None
    piece_ref, low_ref = rest[len(rest) % 2 :][:2]
    rank = out_first_ref.shape[1]
    cols, count = out_full_ref.shape[0], act_ref.shape[0]
    mixed = mixed_ref[...].reshape(cols, count)
    act = act_ref[...]
    total = mm(mixed, out_full_ref[...], 0, 0) + mm(act, down_full_ref[...], 1, 0)
    if arrived_ref is not None:
        total = total + arrived_ref[...].astype(F32)
    piece_ref[...] = total.astype(piece_ref.dtype)
    if len(rest) > 3:
        rest[-2][...] = total.astype(BF)
        rest[-1][...] = jnp.zeros(rest[-1].shape, BF)
    low_ref[:, :rank] = mm(mixed, out_first_ref[...], 0, 0).astype(BF)
    low_ref[:, rank:] = mm(act, down_first_ref[...], 1, 0).astype(BF)


def out_piece(
    mixed, act, out_full, down_full, out_first, down_first, dtype, arrived=None, both=False
):
    count, hidden = act.shape
    width, rank = out_full.shape[1], out_first.shape[1]
    operands = [mixed, act, out_full, down_full, out_first, down_first]
    return call(
        out_kernel,
        operands + ([] if arrived is None else [arrived]),
        [((count, width), dtype), ((count, 2 * rank), BF)]
        + ([((count, width), BF), ((8, 128), BF)] if both else []),
        flops=2 * count * (out_full.shape[0] + hidden) * width,
    )


def pull_kernel(
    g_ref,
    slope_ref,
    out_full_ref,
    down_ref,
    out_second_ref,
    down_second_ref,
    mixed_ref,
    low_ref,
    up_ref,
):
    grad = g_ref[...]
    mixed = mm(out_full_ref[...], grad, 1, 1)
    for head in range(mixed.shape[0] // HEAD_DIM):
        mixed_ref[head] = mixed[head * HEAD_DIM : (head + 1) * HEAD_DIM].astype(BF)
    rank = out_second_ref.shape[0]
    low_ref[:, :rank] = (ADAPTER_SCALE * mm(grad, out_second_ref[...], 1, 1)).astype(BF)
    low_ref[:, rank:] = (ADAPTER_SCALE * mm(grad, down_second_ref[...], 1, 1)).astype(BF)
    for begin in range(0, up_ref.shape[1], BLOCK):
        part = slice(begin, begin + BLOCK)
        up_ref[:, part] = (
            mm(grad, down_ref[part], 1, 1) * slope_ref[:, part].astype(F32)
        ).astype(BF)


def pull_back(grad, slope, out_full, down_full, out_second, down_second):
    count, width = grad.shape
    hidden, cols, twice = slope.shape[1], out_full.shape[0], 2 * out_second.shape[0]
    return call(
        pull_kernel,
        [grad, slope, out_full, down_full, out_second, down_second],
        [
            ((cols // HEAD_DIM, HEAD_DIM, count), BF),
            ((count, twice), BF),
            ((count, hidden), BF),
        ],
        flops=2 * count * width * (cols + hidden + twice),
    )


def slot_code(slot, bits):
    return sum(((slot >> b) & 1) << (bits - 1 - b) for b in range(bits))


def part_slots(members):
    halves = []
    while members > 4:
        members //= 2
        halves.append((members, members))
    return halves + [(slot, 1) for slot in range(members - 1, -1, -1)]


def move_slices(me, members, fields, parts, inward):
    bits = members.bit_length() - 1
    for (first, size), part in zip(part_slots(members), parts):
        for k in range(size):
            owner = me ^ slot_code(first + k, bits)
            low = 0
            for field in fields:
                rows = field.shape[0] // members
                at = pl.ds(pl.multiple_of(owner * rows, rows), rows)
                if inward:
                    part[k, low : low + rows] = field[at]
                else:
                    field[at] = part[k, low : low + rows]
                low += rows


def spread(me, members, fields, parts):
    move_slices(me, members, fields, parts, True)


def gather_spread(me, members, fields, parts):
    move_slices(me, members, fields, parts, False)


def early_kernel(chunks, packs, me_ref, up_second_ref, gain_ref, *rest):
    fields = 8
    more = rest[fields * chunks :]
    before, more = (more[:3], more[3:]) if packs != 1 else (None, more)
    if packs > 1:
        count = len(part_slots(packs))
        parts, more = more[:count], more[count:]
        out_ref, shared_ref, split_ref = more
    else:
        shared_ref, split_ref, out_ref = more
    rank = up_second_ref.shape[0]
    shared_up, shared_out, up_b, down_a, out_a = 0.0, 0.0, 0.0, 0.0, 0.0
    for c in range(chunks):
        grad, grad_up, hat, act, low, low_out, grad_low, mixed = (
            ref[...] for ref in rest[c * fields : (c + 1) * fields]
        )
        mixed = mixed.reshape(-1, mixed.shape[-1])
        low_up_grad = (ADAPTER_SCALE * mm(grad_up, up_second_ref[...], 1, 1)).astype(BF)
        shared_up = shared_up + mm(low_up_grad, hat, 0, 0)
        shared_out = shared_out + mm(low_out, grad, 0, 0)
        up_b = up_b + mm(low[:, 3 * rank :], grad_up, 0, 0)
        down_a = down_a + mm(grad_low[:, rank:], act, 0, 0)
        out_a = out_a + mm(grad_low[:, :rank], mixed, 0, 1)
    shared_up = shared_up * gain_ref[...]
    shared_out = ADAPTER_SCALE * shared_out
    up_b = ADAPTER_SCALE * up_b
    if before is not None:
        shared_up = shared_up + before[0][:rank]
        shared_out = shared_out + before[0][rank:]
        up_b = up_b + before[1][:rank]
        down_a = down_a + before[1][rank:]
        out_a = out_a + before[2][...]
    shared_ref[:rank] = shared_up.astype(shared_ref.dtype)
    shared_ref[rank:] = shared_out.astype(shared_ref.dtype)
    split_ref[:rank] = up_b.astype(split_ref.dtype)
    split_ref[rank:] = down_a.astype(split_ref.dtype)
    out_ref[...] = out_a.astype(out_ref.dtype)
    if packs > 1:
        spread(me_ref[0], packs, (shared_ref, split_ref), parts)


def part_shapes(members, rows, width):
    return [((size, rows, width), BF) for _, size in part_slots(members)]


def early_sums(me, items, up_second, gain, before=None, members=0):
    width, hidden, rank = items[0][0].shape[1], items[0][1].shape[1], up_second.shape[0]
    cols = items[0][7].shape[0] * HEAD_DIM
    sums = [((3 * rank, width), F32), ((2 * rank, hidden), F32), ((rank, cols), F32)]
    operands = [me, up_second, gain] + [array for item in items for array in item]
    scratch = []
    if before is None:
        packs, outputs = 1, sums
    elif not members:
        packs, outputs = 0, sums
    else:
        packs = members
        outputs = part_shapes(members, 5 * rank // members, width) + [((rank, cols), BF)]
        scratch = [pltpu.VMEM((3 * rank, width), BF), pltpu.VMEM((2 * rank, hidden), BF)]
    return call(
        lambda *refs: early_kernel(len(items), packs, *refs),
        operands + ([] if before is None else list(before)),
        outputs,
        scratch,
        flops=2 * len(items) * items[0][0].shape[0] * rank * 6 * width,
        scalars=1,
    )


def all_heads(first, second):
    return jnp.concatenate(
        [half.reshape(-1, half.shape[-1]) for half in (first, second)], axis=0
    )


def in_kernel(first_ref, second_ref, grad_up_ref, in_full_ref, up_full_ref, *rest):
    piece_ref = rest[-1]
    grad_pre = jnp.concatenate(
        [all_heads(first_ref[i], second_ref[i]) for i in range(3)], axis=0
    )
    total = mm(grad_pre, in_full_ref[...], 0, 1) + mm(grad_up_ref[...], up_full_ref[...], 1, 1)
    if len(rest) > 1:
        total = total + rest[0][...].astype(F32)
    piece_ref[...] = total.astype(piece_ref.dtype)


def in_piece(grad_pre, grad_up, in_full, up_full, dtype, arrived=None):
    count, hidden = grad_up.shape
    width = up_full.shape[0]
    operands = [*grad_pre, grad_up, in_full, up_full]
    (piece,) = call(
        in_kernel,
        operands + ([] if arrived is None else [arrived]),
        [((count, width), dtype)],
        flops=2 * count * (in_full.shape[1] + hidden) * width,
    )
    return piece


def late_kernel(chunks, packs, me_ref, second_ref, gain_ref, *rest):
    fields = 4
    more = rest[fields * chunks :]
    rank, cols = second_ref.shape[1], second_ref.shape[2]
    out_ref, more = more[0], more[1:]
    shared_ref, split_ref = more[-2:]

    def one_third(i, carry):
        shared, split = 0.0, 0.0
        for c in range(chunks):
            grad_first, grad_second, low, hat = rest[c * fields : (c + 1) * fields]
            part = all_heads(grad_first[i], grad_second[i])
            low_grad = (ADAPTER_SCALE * mm(part, second_ref[i], 0, 1)).astype(BF)
            shared = shared + mm(low_grad, hat[...], 0, 0)
            split = split + mm(low[:, lanes(i, rank)], part, 0, 1)
        shared_ref[pl.ds(pl.multiple_of(i * rank, rank), rank)] = (
            shared * gain_ref[...]
        ).astype(BF)
        split_ref[:, lanes(i, cols)] = (ADAPTER_SCALE * split).astype(BF)
        return carry

    lax.fori_loop(0, 3, one_third, 0, unroll=True)
    split_ref[:, 3 * cols :] = out_ref[...].astype(BF)
    if packs:
        spread(me_ref[0], packs, (shared_ref, split_ref), more[: len(part_slots(packs))])


def late_sums(me, items, second, gain, out_a, members=0):
    width, rank, cols = items[0][3].shape[1], second.shape[1], second.shape[2]
    sums = [((3 * rank, width), BF), ((rank, 4 * cols), BF)]
    packs = members
    return call(
        lambda *refs: late_kernel(len(items), packs, *refs),
        [me, second, gain] + [array for item in items for array in item] + [out_a],
        part_shapes(members, 4 * rank // members, width) if packs else sums,
        [pltpu.VMEM(*spec) for spec in sums] if packs else [],
        flops=2 * len(items) * items[0][2].shape[0] * rank * 3 * (width + 2 * cols),
        scalars=1,
    )


def early_unpack_kernel(packs, me_ref, *rest):
    count = len(part_slots(packs))
    parts = rest[:count]
    up_a_ref, out_b_ref, down_b_ref, up_b_ref, down_a_ref, shared_ref, split_ref = rest[count:]
    rank = out_b_ref.shape[0]
    gather_spread(me_ref[0], packs, (shared_ref, split_ref), parts)
    up_a_ref[...] = shared_ref[:rank].astype(F32).T
    out_b_ref[...] = shared_ref[rank : 2 * rank].astype(F32)
    down_b_ref[...] = shared_ref[2 * rank :].astype(F32)
    up_b_ref[...] = split_ref[:rank].astype(F32)
    down_a_ref[...] = split_ref[rank:].astype(F32).T


def late_unpack_kernel(packs, me_ref, *rest):
    count = len(part_slots(packs))
    parts = rest[:count]
    a_ref, b_ref, out_a_ref, shared_ref, split_ref = rest[count:]
    rank, cols = b_ref.shape[1], b_ref.shape[2]
    gather_spread(me_ref[0], packs, (shared_ref, split_ref), parts)
    for i in range(3):
        a_ref[i] = shared_ref[i * rank : (i + 1) * rank].astype(F32).T
        b_ref[i] = split_ref[:, i * cols : (i + 1) * cols].astype(F32)
    out_a_ref[...] = split_ref[:, 3 * cols :].astype(F32).T


def output_kernel(x_ref, own_ref, *rest):
    total = x_ref[...].astype(F32) + own_ref[...]
    for ref in rest[:-1]:
        total = total + ref[...].astype(F32)
    rest[-1][...] = total.astype(BF)


def input_grad_kernel(x_ref, g_ref, own_ref, *rest):
    total = own_ref[...]
    for ref in rest[:-1]:
        total = total + ref[...].astype(F32)
    hat, scale = normalize(x_ref[...])
    mean_grad = jnp.mean(total, axis=-1, keepdims=True)
    mean_cross = jnp.mean(total * hat, axis=-1, keepdims=True)
    rest[-1][...] = g_ref[...].astype(F32) + scale * (total - mean_grad - hat * mean_cross)


def add_kernel(left_ref, right_ref, sum_ref):
    sum_ref[...] = (left_ref[...].astype(F32) + right_ref[...].astype(F32)).astype(BF)


def added(left, right):
    return call(add_kernel, [left, right], [(left.shape, BF)])[0]


def fold_kernel(firsts, arrived_ref, *rest):
    parts, results = rest[: len(rest) // 2], rest[len(rest) // 2 :]
    for first, part, result in zip(firsts, parts, results):
        result[...] = (
            part[...].astype(F32) + arrived_ref[first : first + part.shape[0]].astype(F32)
        ).astype(BF)


def meet_kernel(count, *refs):
    total = refs[0][...].astype(F32)
    for ref in refs[1:count]:
        total = total + ref[...].astype(F32)
    shared_ref, split_ref = refs[count:]
    rows = shared_ref.shape[1]
    shared_ref[...] = total[:, :rows].astype(BF)
    split_ref[...] = total[:, rows:].astype(BF)


def close_kernel(shared_ref, arrived_ref, split_ref, both_ref):
    rows = shared_ref.shape[1]
    both_ref[:, :rows] = (
        shared_ref[...].astype(F32) + arrived_ref[...].astype(F32)
    ).astype(BF)
    both_ref[:, rows:] = split_ref[...]


def close_all_kernel(own_ref, near_ref, second_ref, third_ref, split_ref, both_ref):
    rows = own_ref.shape[1]
    own, near, second, third = (
        ref[...].astype(F32) for ref in (own_ref, near_ref, second_ref, third_ref)
    )
    both_ref[:, :rows] = ((own + near) + (second + third)).astype(BF)
    both_ref[:, rows:] = split_ref[...]


def join_kernel(*refs):
    low = 0
    for ref in refs[:-1]:
        refs[-1][low : low + ref.shape[0]] = ref[...]
        low += ref.shape[0]


def swap_pairs(n):
    return [(i, i ^ 1) for i in range(n)]


def mirror_pairs(n):
    return [(i, n - 1 - i) for i in range(n)]


def together(*values):
    return lax.optimization_barrier(values)


def after(value, *earlier):
    return lax.optimization_barrier((value, earlier))[0]


def ring_scatter(piece, pieces):
    up = [(i, (i + 1) % pieces) for i in range(pieces)]
    running = piece(1, None)
    for k in range(2, pieces + 1):
        running = piece(k % pieces, lax.ppermute(running, "tensor", up))
    return running


class GroupSum:
    def __init__(self, parts, n_shared):
        self.parts, self.n_shared = list(parts), n_shared
        self.members, self.n = lax.axis_size("dp"), lax.axis_size("tensor")
        self.bits = self.members.bit_length() - 1
        self.slots = part_slots(self.members)
        halves = self.bits - 2
        self.steps = [("down", b) for b in range(halves)] + [("meet", 0)]
        jump = 1
        while jump < self.n and self.n != 4:
            self.steps.append(("across", jump))
            jump *= 2
        if self.n == 4:
            self.steps.append(("all", 0))
        self.steps += [("part", 0)] + [("back", b) for b in reversed(range(halves))]
        self.moving, self.at, self.results = None, 0, []

    def hop(self, value, code):
        pairs = [(k, k ^ code) for k in range(self.members)]
        return lax.ppermute(value, "dp", pairs)

    def start(self):
        kind, which = self.steps[self.at]
        codes = [slot_code(slot, self.bits) for slot in (1, 2, 3)]
        if kind == "across":
            pairs = [(k, k ^ which) for k in range(self.n)]
            self.moving = lax.ppermute(self.shared, "tensor", pairs)
        elif kind == "all":
            self.moving = [
                lax.ppermute(self.shared, "tensor", [(k, k ^ jump) for k in range(4)])
                for jump in (1, 2, 3)
            ]
        elif kind == "down":
            self.moving = self.hop(self.parts[which], 1 << which)
        elif kind == "meet":
            self.moving = [
                self.hop(self.parts[-1 - slot], code) for slot, code in zip((1, 2, 3), codes)
            ]
        elif kind == "part":
            self.moving = [self.hop(self.have, code) for code in codes]
        else:
            self.moving = self.hop(self.have, 1 << which)

    def finish(self, *earlier):
        kind, which = self.steps[self.at]
        arrived = after(self.moving, *earlier) if earlier else self.moving
        if kind == "down":
            later = self.parts[which + 1 :]
            firsts = [first for first, _ in self.slots[which + 1 :]]
            self.parts[which + 1 :] = call(
                lambda *refs: fold_kernel(firsts, *refs),
                [arrived, *later],
                [(part.shape, BF) for part in later],
            )
            value = self.parts[-1]
        elif kind == "meet":
            _, rows, width = self.parts[-1].shape
            self.shared, self.split = call(
                lambda *refs: meet_kernel(4, *refs),
                [self.parts[-1], *arrived],
                [((1, self.n_shared, width), BF), ((1, rows - self.n_shared, width), BF)],
            )
            value = self.shared
        elif kind == "all":
            (self.have,) = call(
                close_all_kernel,
                [self.shared, *arrived, self.split],
                [(self.parts[-1].shape, BF)],
            )
            value = self.have
        elif kind == "across":
            if self.steps[self.at + 1][0] == "part":
                (self.have,) = call(
                    close_kernel,
                    [self.shared, arrived, self.split],
                    [(self.parts[-1].shape, BF)],
                )
                value = self.have
            else:
                self.shared = value = added(self.shared, arrived)
        else:
            pieces = list(arrived) if kind == "part" else [arrived]
            self.results = self.results or [self.have]
            self.results += pieces
            value = pieces[0]
            if self.at + 1 < len(self.steps):
                _, *rows = self.have.shape
                total = sum(piece.shape[0] for piece in [self.have, *pieces])
                (self.have,) = call(
                    join_kernel, [self.have, *pieces], [((total, *rows), BF)]
                )
                value = self.have
        self.at += 1
        return value

    def rest(self):
        while self.at < len(self.steps):
            self.start()
            self.finish()
        return self.results[::-1]


def slow_parts(me, shared, split, members):
    bits = members.bit_length() - 1
    width = shared.shape[1]
    both = jnp.concatenate(
        [
            shared.astype(BF).reshape(members, -1, width),
            split.astype(BF).reshape(members, -1, width),
        ],
        axis=1,
    )
    order = jnp.asarray([slot_code(slot, bits) for slot in range(members)], jnp.int32) ^ me
    both = both[order]
    return [both[first : first + size] for first, size in part_slots(members)]


def slow_whole(me, parts, n_shared, members):
    bits = members.bit_length() - 1
    both = jnp.concatenate(parts[::-1], axis=0)
    order = jnp.asarray([slot_code(slot, bits) for slot in range(members)], jnp.int32)
    both = both[order[jnp.arange(members, dtype=jnp.int32) ^ me]].astype(F32)
    width = both.shape[-1]
    return both[:, :n_shared].reshape(-1, width), both[:, n_shared:].reshape(-1, width)


def normalize(inputs):
    values = inputs.astype(F32)
    center = values - jnp.mean(values, axis=-1, keepdims=True)
    inv_scale = lax.rsqrt(jnp.mean(center * center, axis=-1, keepdims=True) + EPSILON)
    return center * inv_scale, inv_scale


def whole_step(
    layer_input,
    document_lengths,
    attention_norm_gain,
    feedfwd_norm_gain,
    query_key_value_weight,
    output_weight,
    up_weight,
    down_weight,
    adapter_query_key_value_first,
    adapter_query_key_value_second,
    adapter_output_first,
    adapter_output_second,
    adapter_up_first,
    adapter_up_second,
    adapter_down_first,
    adapter_down_second,
    cotangent,
):
    own_x, own_g = layer_input[0], cotangent[0]
    shard_len, width = own_x.shape
    n = lax.axis_size("tensor")
    me = lax.axis_index("tensor")
    seq_len = shard_len * n
    rank = adapter_up_first.shape[1]
    cols = query_key_value_weight.shape[2]
    hidden = up_weight.shape[1]
    swap, mirror = swap_pairs(n), mirror_pairs(n)
    short = n == 4

    def send(value, pairs):
        return lax.ppermute(value, "tensor", pairs)

    members = lax.axis_size("dp")
    tidy = short and hidden == width and 4 * cols == width and rank % (16 * members) == 0
    if short:
        owners = [me, me ^ 1, n - 1 - me, (n - 1 - me) ^ 1]
    else:
        owners = [lax.rem(me - k + n, n) for k in range(n)]
    places = jnp.stack(owners).astype(jnp.int32)
    me_dp = lax.axis_index("dp").astype(jnp.int32).reshape(1)
    places, me_dp, own_x = together(places, me_dp, own_x)
    turns = call(
        places_kernel,
        [places, document_lengths],
        [((1, seq_len), jnp.int32), ((HALF, seq_len), F32), ((HALF, seq_len), F32)]
        + [((HALF, shard_len), F32)] * (2 * n),
        scalars=2,
    )
    start, cosine, sine, turns = turns[0], turns[1], turns[2], turns[3:]
    gain_a, gain_m = attention_norm_gain[None], feedfwd_norm_gain[None]
    weights = (
        query_key_value_weight,
        adapter_query_key_value_first,
        adapter_query_key_value_second,
        adapter_up_first,
        up_weight,
        adapter_up_second,
    )

    def projected(k, rows):
        return project(rows, (gain_a, gain_m), (turns[k], turns[n + k]), weights)

    def merged():
        return merge_weights(
            query_key_value_weight,
            up_weight,
            output_weight,
            down_weight,
            (adapter_query_key_value_first, adapter_query_key_value_second),
            (adapter_up_first, adapter_up_second),
            (adapter_output_first, adapter_output_second),
            (adapter_down_first, adapter_down_second),
            gain_a,
            gain_m,
        )

    outward, inward, middle = [(0, 1), (3, 2)], [(1, 0), (2, 3)], [(1, 2), (2, 1)]
    if short:
        x_near, x_facing = send(own_x, swap), send(own_x, mirror)
        full = merged()
        first = projected(0, own_x)
        x_near, x_facing, first, full, own_g = together(x_near, x_facing, first, full, own_g)
        x_far = send(x_facing, swap)
        g_near, g_mid = send(own_g, swap), send(own_g, middle)
        state = [first, projected(1, x_near), projected(2, x_facing)]
        x_far, state = together(x_far, state)
        state = state + [projected(3, x_far)]
    else:
        full = merged()
        up_ring = [(i, (i + 1) % n) for i in range(n)]
        state, moving = [projected(0, own_x)], own_x
        for k in range(1, n):
            moving = send(moving, up_ring)
            state.append(projected(k, moving))
    in_full, up_full, out_full, down_full = full
    qkv, low, hat, act, slope = (list(field) for field in zip(*state))
    mixed, log_total = forward_attention(places, start, qkv)
    low_out = [None] * n

    def out_part(k, dtype, last=None, arrived=None, both=False):
        rows = mixed[k] if last is None else after(mixed[k], last)
        piece, low_out[k], *more = out_piece(
            rows,
            act[k],
            out_full,
            down_full,
            adapter_output_first,
            adapter_down_first,
            dtype,
            arrived,
            both,
        )
        return (piece, more[0]) if both else piece

    def pulled(k, grad):
        return pull_back(
            grad,
            slope[k],
            out_full,
            down_full,
            adapter_output_second,
            adapter_down_second,
        )

    def early_item(k, grad, back):
        return (grad, back[2], hat[k], act[k], low[k], low_out[k], back[1], mixed[k])

    if short:
        y_facing, y_facing_low = out_part(2, F32, both=True)
        y_far, y_far_low = out_part(3, F32, both=True)
        y_1, y_2 = send(y_facing_low, outward), send(y_far_low, outward)
        g_near, g_mid = after((g_near, g_mid), mixed)
        g_mid_far, g_end_far = send(g_near, middle), send(g_mid, inward)
        backs = [pulled(0, own_g)]
        g_mid_far, g_end_far = after((g_mid_far, g_end_far), y_far, backs)
        g_end = send(g_mid_far, inward)
        g_far = added(g_mid_far, g_end_far)
        backs.append(pulled(1, after(g_near, g_far)))
        y_near, y_own = out_part(1, F32, g_far), out_part(0, F32, g_far)
        pulled_far = pulled(3, g_far)
        y_3 = send(added(y_far, after(y_1, backs, y_near, y_own, pulled_far)), middle)
        backs = backs + [None, pulled_far]
        all_g = [own_g, g_near, None, g_far]
        before = early_sums(
            me_dp,
            [early_item(k, all_g[k], backs[k]) for k in (0, 1, 3)],
            adapter_up_second,
            gain_m,
        )
        g_end = after(g_end, before)
        g_facing = added(g_mid, g_end)
        backs[2] = pulled(2, g_facing)
        early = early_sums(
            me_dp,
            [early_item(2, g_facing, backs[2])],
            adapter_up_second,
            gain_m,
            before,
            members if tidy else 0,
        )
    else:
        y_own = ring_scatter(
            lambda k, arrived: out_part(k, BF if k else F32, arrived=arrived), n
        )
        backs, moving, all_g = [pulled(0, own_g)], own_g, [own_g]
        for k in range(1, n):
            moving = send(moving, up_ring)
            all_g.append(moving)
            backs.append(pulled(k, moving))
        early = early_sums(
            me_dp, [early_item(k, all_g[k], backs[k]) for k in range(n)], adapter_up_second, gain_m
        )

    *early, out_a = early
    if not tidy:
        early = slow_parts(me_dp[0], early[0], early[1].reshape(-1, width), members)
    early = GroupSum(early, 3 * rank // members)
    early.start()
    grads_mixed = [back[0] for back in backs]
    halves = []
    for part in range(2):
        halves.append(
            backward_attention(
                part, places, start, cosine, sine, log_total, qkv, mixed, grads_mixed
            )
        )
        if short and not part:
            last = early.finish(halves[0])
            early.start()
            y_5 = send(added(y_facing, after(y_2, last)), middle)
            y_near = added(y_near, after(y_3, last))
            y_4 = send(y_near, swap)
            grads_mixed = after(grads_mixed, y_near)
    grad_pre = list(zip(*halves))

    def in_part(k, dtype, arrived=None, last=None):
        pre = grad_pre[k] if last is None else after(grad_pre[k], last)
        return in_piece(pre, backs[k][2], in_full, up_full, dtype, arrived)

    def early_whole(parts):
        if not tidy:
            early_a, early_b = slow_whole(me_dp[0], parts, 3 * rank // members, members)
            early_b = early_b.reshape(2 * rank, hidden)
            return (
                early_a[:rank].T,
                early_a[rank : 2 * rank],
                early_a[2 * rank :],
                early_b[:rank],
                early_b[rank:].T,
            )
        return call(
            lambda *refs: early_unpack_kernel(members, *refs),
            [me_dp, *parts],
            [
                ((width, rank), F32),
                ((rank, width), F32),
                ((rank, width), F32),
                ((rank, hidden), F32),
                ((hidden, rank), F32),
            ],
            [pltpu.VMEM((3 * rank, width), BF), pltpu.VMEM((2 * rank, width), BF)],
            scalars=1,
        )

    def late_parts():
        late = late_sums(
            me_dp,
            [(*grad_pre[k], low[k], hat[k]) for k in range(n)],
            adapter_query_key_value_second,
            gain_a,
            out_a,
            members if tidy else 0,
        )
        if not tidy:
            late = slow_parts(me_dp[0], late[0], late[1].reshape(-1, width), members)
        return GroupSum(late, 3 * rank // members)

    if short:
        last = early.finish(grad_pre)
        early.start()
        late = late_parts()
        late.start()
        dx_far = in_part(3, BF)
        dx_swap = send(dx_far, swap)
        last = late.finish(dx_far)
        late.start()
        dx_near = in_part(1, BF, last=last)
        last = early.finish(dx_near)
        early.start()
        last = late.finish(last)
        late.start()
        dx_facing = in_part(2, BF, after(dx_swap, last))
        dx_own = in_part(0, F32, last=dx_facing)
        dx_a = send(dx_near, swap)
        dx_b = send(dx_facing, mirror)
        last = early.finish(dx_own)
        early.start()
        (layer_output,) = call(
            output_kernel,
            [own_x, y_own, *after((y_4, y_5), last)],
            [((shard_len, width), BF)],
        )
        last = late.finish(last, layer_output)
        late.start()
        early.finish(last)
        early_done = early_whole(early.rest())
        last = late.finish(early_done)
        late.start()
        dx_parts = [dx_own, dx_a, dx_b]
    else:
        (layer_output,) = call(output_kernel, [own_x, y_own], [((shard_len, width), BF)])
        dx_parts = [
            ring_scatter(lambda k, arrived: in_part(k, BF if k else F32, arrived), n)
        ]
        early.finish()
        late = late_parts()
        early_done = early_whole(early.rest())
    up_a, out_b, down_b, up_b, down_a = early_done
    late = late.rest()
    if tidy:
        a_qkv, b_qkv, out_a = call(
            lambda *refs: late_unpack_kernel(members, *refs),
            [me_dp, *late],
            [((3, width, rank), F32), ((3, rank, cols), F32), ((cols, rank), F32)],
            [pltpu.VMEM((3 * rank, width), BF), pltpu.VMEM((rank, width), BF)],
            scalars=1,
        )
    else:
        late_a, late_b = slow_whole(me_dp[0], late, 3 * rank // members, members)
        late_b = late_b.reshape(rank, 4 * cols)
        a_qkv = jnp.swapaxes(late_a.reshape(3, rank, width), 1, 2)
        b_qkv = jnp.stack([late_b[:, i * cols : (i + 1) * cols] for i in range(3)])
        out_a = late_b[:, 3 * cols :].T
    dx_parts = [dx_parts[0], *after(dx_parts[1:], a_qkv)]
    (grad_in,) = call(
        input_grad_kernel, [own_x, own_g, *dx_parts], [((shard_len, width), F32)]
    )
    return (
        layer_output[None],
        grad_in[None],
        a_qkv,
        b_qkv,
        out_a,
        out_b,
        up_a,
        up_b,
        down_a,
        down_b,
    )


def solution(mesh):
    in_specs = (
        P("dp", "tensor", None),
        P("dp", None),
        P(),
        P(),
        P(None, None, "tensor"),
        P("tensor", None),
        P(None, "tensor"),
        P("tensor", None),
        P(),
        P(None, None, "tensor"),
        P("tensor", None),
        P(),
        P(),
        P(None, "tensor"),
        P("tensor", None),
        P(),
        P("dp", "tensor", None),
    )
    out_specs = (
        P("dp", "tensor", None),
        P("dp", "tensor", None),
        P(),
        P(None, None, "tensor"),
        P("tensor", None),
        P(),
        P(),
        P(None, "tensor"),
        P("tensor", None),
        P(),
    )
    return jax.shard_map(
        whole_step, mesh=mesh, in_specs=in_specs, out_specs=out_specs, check_vma=False
    )
```
